256 devices in a mesh: section: 2 (over z_hi), gy: 32 (over z_lo, x, core), gz: 4 (over y).
Axes of the slice: x: 4, y: 4, z: 8 (z_hi: 2, z_lo: 4; z = z_hi * 4 + z_lo), core: 2. Of those that a mesh axis runs over, the one named last changes fastest.
Arguments:
- inflow: float32 [2, 64, 2, 64, 512], P(None, None, None, 'gy', 'gz'), may hold values from -6 to 6
- weights: float32 [4, 27, 64, 64], P('section'), may hold values from -0.15625 to 0.15625
- biases: float32 [4, 64], P('section'), may hold values from -3 to 3
- cotangent: float32 [2, 64, 2, 64, 512], P(None, None, None, 'gy', 'gz'), may hold values from -6 to 6
Outputs:
- section_out: float32 [2, 2, 64, 2, 64, 512], P('section', None, None, None, 'gy', 'gz')
- section_grad: float32 [2, 2, 64, 2, 64, 512], P('section', None, None, None, 'gy', 'gz')
- weight_grad: float32 [4, 27, 64, 64], P('section')
- bias_grad: float32 [4, 64], P('section')
The draws below stay inside these ranges and needn't reach their ends.
All inputs are finite; a program needn't handle non-finite values.
Results may differ from the reference program's by a relative error of at most 0.0001.
Values sent between devices are 32-bit elements; how exact they have to be, the bound alone decides.
A program may use at most 128 MiB of HBM per device.

```python
import math
import jax
import jax.numpy as jnp
from jax import lax

C = 64
LAYERS_DEV = 2
MB = 2
LAYERS = 4
NX = 2
NY = 64
NZ = 512


def block_levels(stream_key, shape, cuts, smallest, largest):
    factor_of, own = 1.0, jax.random.fold_in(stream_key, 6)
    for axis_at, parts in cuts:
        heights = jnp.exp(jax.random.uniform(jax.random.fold_in(own, axis_at), (parts,), jnp.float32, smallest / len(cuts), largest / len(cuts)))
        factor_of = factor_of * jnp.repeat(heights, shape[axis_at] // parts).reshape([-1 if axis == axis_at else 1 for axis in range(len(shape))])
    return factor_of


def bell_draw(key, shape, deviation, most, split=(), kind=jnp.bfloat16):
    level = block_levels(key, shape, split, -0.22, 0.18) if split else 1.0
    drawn = jax.random.normal(key, shape, jnp.float32) * deviation * level
    return jnp.minimum(jnp.maximum(drawn, -most), most).astype(kind)


def setup_inputs(seed: int = 0) -> dict:
    seeds = jax.random.split(jax.random.key(seed), 5)
    inflow = bell_draw(seeds[0], (MB, C, NX, NY, NZ), 1.0, 6.0, ((3, 32), (4, 4)), jnp.float32)
    weights = bell_draw(seeds[1], (LAYERS, 27, C, C), (27 * C) ** -0.5, 0.15625, ((0, 2),), jnp.float32)
    biases = bell_draw(seeds[2], (LAYERS, C), 0.5, 3.0, ((0, 2),), jnp.float32)
    cotangent = bell_draw(seeds[3], (MB, C, NX, NY, NZ), 1.0, 6.0, ((3, 32), (4, 4)), jnp.float32)
    return dict(inflow=inflow, weights=weights, biases=biases, cotangent=cotangent)


def stacked_taps(padded, out_sizes, flipped):
    size_x, size_y, size_z = out_sizes
    pieces = []
    for offset in range(27):
        start_x, start_y, start_z = (offset // 9, offset // 3 % 3, offset % 3)
        if flipped:
            start_x, start_y, start_z = (2 - start_x, 2 - start_y, 2 - start_z)
        pieces.append(padded[:, start_x:start_x + size_x, start_y:start_y + size_y, start_z:start_z + size_z])
    return jnp.stack(pieces)

def zero_rim(values):
    return jnp.pad(values, ((0, 0), (1, 1), (1, 1), (1, 1)))

def reference(inflow, weights, biases, cotangent):
    highest = lax.Precision.HIGHEST
    grad_scale = 1.0 / math.sqrt(MB * NX * NY * NZ)
    extents = inflow.shape[2:]
    weight_grads = jnp.zeros(weights.shape, jnp.float32)
    bias_grads = jnp.zeros(biases.shape, jnp.float32)
    middles, finals, inflow_grads, middle_grads = ([], [], [], [])
    for micro in range(MB):
        current = inflow[micro]
        stored = []
        for layer_index in range(LAYERS):
            padded = zero_rim(current)
            pre_act = jnp.einsum('toc,tcxyz->oxyz', weights[layer_index], stacked_taps(padded, extents, False), precision=highest)
            pre_act = pre_act + biases[layer_index][:, None, None, None]
            current = jax.nn.silu(pre_act)
            stored.append((padded, pre_act))
            if layer_index == LAYERS_DEV - 1:
                middles.append(current)
        finals.append(current)
        gradient = cotangent[micro]
        for layer_index in reversed(range(LAYERS)):
            padded, pre_act = stored[layer_index]
            sigmoid_value = jax.nn.sigmoid(pre_act)
            slope_grad = gradient * sigmoid_value * (1.0 + pre_act * (1.0 - sigmoid_value))
            weight_grads = weight_grads.at[layer_index].add(jnp.einsum('oxyz,tcxyz->toc', slope_grad, stacked_taps(padded, extents, False), precision=highest))
            bias_grads = bias_grads.at[layer_index].add(lax.optimization_barrier(jnp.sum(slope_grad, axis=(1, 2, 3))))
            gradient = jnp.einsum('toc,toxyz->cxyz', weights[layer_index], stacked_taps(zero_rim(slope_grad), extents, True), precision=highest)
            if layer_index == LAYERS_DEV:
                middle_grads.append(gradient)
        inflow_grads.append(gradient)
    section_out = jnp.stack([jnp.stack(middles), jnp.stack(finals)])
    section_grad = jnp.stack([jnp.stack(inflow_grads), jnp.stack(middle_grads)])
    return (section_out, section_grad, weight_grads * grad_scale, bias_grads * grad_scale)
```

```python
import math

import jax
import jax.numpy as jnp
from jax import lax
from jax.experimental import pallas as pl
from jax.experimental.pallas import tpu as pltpu
from jax.sharding import PartitionSpec as P

MESH = pl.DeviceIdType.MESH
F32 = jnp.float32
BF16 = jnp.bfloat16
LAYERS = 4
TAPS = 9
DIRS = [(dy, dz) for dy in (-1, 0, 1) for dz in (-1, 0, 1) if (dy, dz) != (0, 0)]
TAP_ROWS = 96
PACK = 880
CHUNKS = 5
CHUNK = PACK // 2 // CHUNKS
GRAD = 1024


def split_parts(value):
    high = value.astype(BF16)
    return high, (value - high.astype(F32)).astype(BF16)


def source_window(dy, dz):
    rows = {1: pl.ds(2, 1), -1: pl.ds(1, 1), 0: pl.ds(1, 2)}[dy]
    cells = {1: pl.ds(128, 8), -1: pl.ds(8, 8), 0: pl.ds(8, 128)}[dz]
    return rows, cells


def target_window(dy, dz):
    rows = {1: pl.ds(0, 1), -1: pl.ds(3, 1), 0: pl.ds(1, 2)}[dy]
    cells = {1: pl.ds(0, 8), -1: pl.ds(136, 8), 0: pl.ds(8, 128)}[dz]
    return rows, cells


def landed(ref, sem):
    pltpu.make_async_copy(ref, ref, sem).wait()


def kernel(
    scale,
    inflow,
    weights,
    biases,
    cotangent,
    out_act,
    out_grad,
    out_weight,
    out_bias,
    ext,
    patch,
    slope_patch,
    wide_f,
    wide_b,
    packed,
    pre,
    flow,
    stage,
    part,
    final,
    half_in,
    half_sum,
    one_in,
    one_sum,
    two_in,
    two_sum,
    three_in,
    halo_send,
    halo_recv,
    source_send,
    relay_send,
    relay_recv,
    mate_send,
    mate_recv,
    out_send,
    out_recv,
    pair_send,
    pair_recv,
    group_send,
    group_recv,
    deep_send,
    deep_recv,
):
    sec = lax.axis_index("section")
    gy = lax.axis_index("gy")
    gz = lax.axis_index("gz")
    core = gy % 2
    px = (gy // 2) % 4
    zlo = gy // 8
    depth = sec * 4 + zlo
    other = 1 - sec

    def at_depth(level, parity):
        return (level // 4, (level % 4) * 8 + px * 2 + parity, gz)

    def in_plane(first, index):
        on_x = (1 - core) if first else core
        new_gy = gy + on_x * 2 * (index - px)
        new_gz = gz + (1 - on_x) * (index - gz)
        return (sec, new_gy, new_gz)

    mate = (sec, gy + 1 - 2 * core, gz)
    step_sign = 1 - 2 * core
    following = at_depth((depth + step_sign + 8) % 8, core)
    at_end = zlo == 3 * (1 - core)

    def exists(dy, dz):
        ok = None
        for index, delta, count in ((gy, dy, 32), (gz, dz, 4)):
            if delta == 0:
                continue
            good = index > 0 if delta < 0 else index < count - 1
            ok = good if ok is None else jnp.logical_and(ok, good)
        return ok

    lane = lax.broadcasted_iota(jnp.int32, (1, 128), 1)
    left = lane < 64

    def turned(value):
        return pltpu.roll(value, 64, 1)

    for i in range(2):
        for b in range(3):
            for c in range(3):
                tap = b * 3 + c
                base = tap * TAP_ROWS
                middle = weights[i, 9 + tap]
                far = weights[i, 18 + tap]
                near = weights[i, tap]
                packed[2 * sec + i, base : base + 64, :] = jnp.concatenate([middle, far], axis=1)
                packed[2 * sec + i, base + 64 : base + 96, :] = jnp.concatenate(
                    [near[0:32], near[32:64]], axis=1
                )
        row = biases[i : i + 1, :]
        packed[2 * sec + i, 864:880, :] = jnp.broadcast_to(
            jnp.concatenate([row, row], axis=1), (16, 128)
        )

    def clear(rows, cells):
        shape = (8, rows.size, cells.size, 128)
        ext[:, rows, cells, :] = jnp.zeros(shape, F32)

    @pl.when(gy == 0)
    def _():
        clear(pl.ds(0, 1), pl.ds(0, 144))

    @pl.when(gy == 31)
    def _():
        clear(pl.ds(3, 1), pl.ds(0, 144))

    @pl.when(gz == 0)
    def _():
        clear(pl.ds(0, 4), pl.ds(0, 8))

    @pl.when(gz == 3)
    def _():
        clear(pl.ds(0, 4), pl.ds(136, 8))

    def turned_in(ref, y):
        rows = [ref[sec, pl.ds(2 * x + y, 64, stride=4), :] for x in range(2)]
        return jnp.concatenate(rows, axis=0).T

    for y in range(2):
        ext[0, 1 + y, 8:136, :] = turned_in(inflow, y)
        flow[y * 128 : (y + 1) * 128, :] = turned_in(cotangent, y)
    for layer in range(LAYERS):
        part[layer, 864:GRAD, :] = jnp.zeros((GRAD - 864, 128), F32)

    barrier = pltpu.get_barrier_semaphore()

    def greet(device):
        pl.semaphore_signal(barrier, inc=1, device_id=device, device_id_type=MESH)

    for d in range(1, 8):
        greet(at_depth((depth + d) % 8, core))
    for d in range(1, 4):
        greet((sec, gy + 2 * ((px + d) % 4 - px), gz))
        greet((sec, gy, (gz + d) % 4))
    for dy, dz in DIRS:
        if dy != 0:

            @pl.when(exists(dy, dz))
            def _():
                greet((sec, gy + dy, gz + dz))

    sides_y = 2 - jnp.where(gy == 0, 1, 0) - jnp.where(gy == 31, 1, 0)
    sides_z = 2 - jnp.where(gz == 0, 1, 0) - jnp.where(gz == 3, 1, 0)
    pl.semaphore_wait(barrier, 13 + sides_y * (1 + sides_z))

    def send_rims(slot):
        for d, (dy, dz) in enumerate(DIRS):
            rows, cells = source_window(dy, dz)
            rows_to, cells_to = target_window(dy, dz)

            @pl.when(exists(dy, dz))
            def _():
                pltpu.make_async_remote_copy(
                    src_ref=ext.at[slot, rows, cells, :],
                    dst_ref=ext.at[slot, rows_to, cells_to, :],
                    send_sem=halo_send.at[slot, d],
                    recv_sem=halo_recv.at[slot, d],
                    device_id=(sec, gy + dy, gz + dz),
                    device_id_type=MESH,
                ).start()

    def await_rims(slot):
        for d, (dy, dz) in enumerate(DIRS):
            rows_to, cells_to = target_window(dy, dz)

            @pl.when(exists(-dy, -dz))
            def _():
                landed(ext.at[slot, rows_to, cells_to, :], halo_recv.at[slot, d])

    send_rims(0)

    def chunk_of(layer, parity, chunk):
        start = parity * (PACK // 2) + chunk * CHUNK
        return packed.at[layer, pl.ds(pl.multiple_of(start, 8), CHUNK), :]

    @pl.when(at_end)
    def _():
        for i in range(2):
            for chunk in range(CHUNKS):
                piece = chunk_of(2 * sec + i, core, chunk)
                pltpu.make_async_remote_copy(
                    src_ref=piece,
                    dst_ref=piece,
                    send_sem=source_send.at[i, chunk],
                    recv_sem=relay_recv.at[i, chunk],
                    device_id=following,
                    device_id_type=MESH,
                ).start()

    def widen(layer):
        for tap in range(TAPS):
            base = tap * TAP_ROWS
            top = packed[layer, base : base + 64, :]
            near = packed[layer, base + 64 : base + 96, :]
            bottom = jnp.where(
                left, jnp.concatenate([near, turned(near)], axis=0), turned(top)
            )
            high, low = split_parts(jnp.concatenate([top, bottom], axis=0))
            cols = slice(tap * 128, tap * 128 + 128)
            wide_f[layer, 0:128, cols] = high
            wide_f[layer, 128:256, cols] = low
            rows = slice((8 - tap) * 128, (8 - tap) * 128 + 128)
            wide_b[layer, rows, 0:128] = high
            wide_b[layer, rows, 128:256] = low

    def widen_own(i, carry):
        widen(2 * sec + i)
        return carry

    lax.fori_loop(0, 2, widen_own, 0)

    for i in range(2):
        for chunk in range(CHUNKS):
            piece = chunk_of(2 * other + i, core, chunk)
            landed(piece, relay_recv.at[i, chunk])

            @pl.when(jnp.logical_not(at_end))
            def _():
                pltpu.make_async_remote_copy(
                    src_ref=piece,
                    dst_ref=piece,
                    send_sem=relay_send.at[i, chunk],
                    recv_sem=relay_recv.at[i, chunk],
                    device_id=following,
                    device_id_type=MESH,
                ).start()

            pltpu.make_async_remote_copy(
                src_ref=piece,
                dst_ref=piece,
                send_sem=mate_send.at[i, chunk],
                recv_sem=mate_recv.at[i, chunk],
                device_id=mate,
                device_id_type=MESH,
            ).start()
    for i in range(2):
        for chunk in range(CHUNKS):
            landed(chunk_of(2 * other + i, 1 - core, chunk), mate_recv.at[i, chunk])

    def widen_other(i, carry):
        widen(2 * other + i)
        return carry

    lax.fori_loop(0, 2, widen_other, 0)

    def fill(slot, store):
        for c in range(3):
            for row in range(4):
                high, low = split_parts(ext[slot, row, 7 + c : 135 + c, :])
                for y in range(2):
                    b = row - y
                    if 0 <= b <= 2:
                        tap = b * 3 + c
                        store(y, tap, high, low)

    def hand_out(value, keeper, kind, result):
        def put(ref, lead):
            for y in range(2):
                block = value[y * 128 : (y + 1) * 128, :].T
                for x in range(2):
                    where = pl.ds(2 * x + y, 64, stride=4)
                    ref[lead, where, :] = block[x * 64 : (x + 1) * 64, :]

        @pl.when(sec == keeper)
        def _():
            put(result, sec)

        @pl.when(sec != keeper)
        def _():
            put(stage, kind)
            pltpu.make_async_remote_copy(
                src_ref=stage.at[kind],
                dst_ref=result.at[sec],
                send_sem=out_send.at[kind],
                recv_sem=out_recv.at[kind],
                device_id=(other, gy, gz),
                device_id_type=MESH,
            ).start()

    def joined(product):
        return (
            product[0:256, 0:128]
            + product[0:256, 128:256]
            + product[256:512, 0:128]
            + product[256:512, 128:256]
        )

    def forward(layer, carry):
        await_rims(layer)

        def store(y, tap, high, low):
            cols = slice(tap * 128, tap * 128 + 128)
            patch[layer, y * 128 : y * 128 + 128, cols] = high
            patch[layer, 256 + y * 128 : 384 + y * 128, cols] = low

        fill(layer, store)
        product = lax.dot_general(
            patch[layer],
            wide_f[layer],
            (((1,), (1,)), ((), ())),
            preferred_element_type=F32,
        )
        value = joined(product) + packed[layer, 864:865, :]
        pre[layer] = value
        active = value * (1.0 / (1.0 + jnp.exp(-value)))

        @pl.when(layer < LAYERS - 1)
        def _():
            for y in range(2):
                ext[layer + 1, 1 + y, 8:136, :] = active[y * 128 : (y + 1) * 128, :]
            send_rims(layer + 1)

        @pl.when(layer == 1)
        def _():
            hand_out(active, 0, 0, out_act)

        @pl.when(layer == 3)
        def _():
            hand_out(active, 1, 0, out_act)

        return carry

    lax.fori_loop(0, LAYERS, forward, 0)

    index_one = px + core * (gz - px)
    index_two = gz + core * (px - gz)
    offset_half = core * 512
    offset_one = offset_half + index_one * 128
    offset_two = offset_one + index_two * 32
    offset_three = offset_two + zlo * 8

    def rows_at(ref, layer, start, size):
        return ref.at[layer, pl.ds(pl.multiple_of(start, 8), size), :]

    def push(source, target, send, recv, device):
        pltpu.make_async_remote_copy(
            src_ref=source,
            dst_ref=target,
            send_sem=send,
            recv_sem=recv,
            device_id=device,
            device_id_type=MESH,
        ).start()

    def reduce_start(layer):
        push(
            rows_at(part, layer, (1 - core) * 512, 512),
            half_in.at[layer],
            pair_send.at[0, layer],
            pair_recv.at[0, layer],
            mate,
        )

    def reduce_half(layer):
        landed(half_in.at[layer], pair_recv.at[0, layer])
        half_sum[layer] = (
            part[layer, pl.ds(pl.multiple_of(offset_half, 8), 512), :] + half_in[layer]
        )
        for d in range(1, 4):
            peer = (index_one + d) % 4
            push(
                rows_at(half_sum, layer, peer * 128, 128),
                one_in.at[layer, 3 - d],
                group_send.at[0, layer, 3 - d],
                group_recv.at[0, layer, 3 - d],
                in_plane(True, peer),
            )

    def reduce_one(layer):
        for s in range(3):
            landed(one_in.at[layer, s], group_recv.at[0, layer, s])
        own = half_sum[layer, pl.ds(pl.multiple_of(index_one * 128, 8), 128), :]
        one_sum[layer] = (own + one_in[layer, 0]) + (one_in[layer, 1] + one_in[layer, 2])
        for d in range(1, 4):
            peer = (index_two + d) % 4
            push(
                rows_at(one_sum, layer, peer * 32, 32),
                two_in.at[layer, 3 - d],
                group_send.at[1, layer, 3 - d],
                group_recv.at[1, layer, 3 - d],
                in_plane(False, peer),
            )

    def reduce_two(layer):
        for s in range(3):
            landed(two_in.at[layer, s], group_recv.at[1, layer, s])
        own = one_sum[layer, pl.ds(pl.multiple_of(index_two * 32, 8), 32), :]
        two_sum[layer] = (own + two_in[layer, 0]) + (two_in[layer, 1] + two_in[layer, 2])
        for d in range(1, 8):
            peer = (depth + d) % 8

            @pl.when(peer // 4 == layer // 2)
            def _():
                push(
                    rows_at(two_sum, layer, (peer % 4) * 8, 8),
                    three_in.at[layer, 7 - d],
                    deep_send.at[layer, 7 - d],
                    deep_recv.at[layer, 7 - d],
                    at_depth(peer, core),
                )

    def gather_three(layer):
        for s in range(7):
            landed(three_in.at[layer, s], deep_recv.at[layer, s])
        total = two_sum[layer, pl.ds(pl.multiple_of(zlo * 8, 8), 8), :]
        for s in range(7):
            total = total + three_in[layer, s]
        start = pl.multiple_of(offset_three, 8)
        final[layer, pl.ds(start, 8), :] = total * scale
        for d in range(1, 4):
            piece = rows_at(final, layer, offset_three, 8)
            push(
                piece,
                piece,
                group_send.at[2, layer, 3 - d],
                group_recv.at[2, layer, 3 - d],
                at_depth(sec * 4 + (zlo + d) % 4, core),
            )

    def gathered(layer, stage_at, base, index, size):
        for s in range(3):
            sender = (index + 1 + s) % 4
            piece = rows_at(final, layer, base + sender * size, size)
            landed(piece, group_recv.at[stage_at, layer, s])

    def gather_two(layer):
        gathered(layer, 2, offset_two, zlo, 8)
        for d in range(1, 4):
            piece = rows_at(final, layer, offset_two, 32)
            push(
                piece,
                piece,
                group_send.at[3, layer, 3 - d],
                group_recv.at[3, layer, 3 - d],
                in_plane(False, (index_two + d) % 4),
            )

    def gather_one(layer):
        gathered(layer, 3, offset_one, index_two, 32)
        for d in range(1, 4):
            piece = rows_at(final, layer, offset_one, 128)
            push(
                piece,
                piece,
                group_send.at[4, layer, 3 - d],
                group_recv.at[4, layer, 3 - d],
                in_plane(True, (index_one + d) % 4),
            )

    def gather_half(layer):
        gathered(layer, 4, offset_half, index_one, 128)
        piece = rows_at(final, layer, offset_half, 512)
        push(piece, piece, pair_send.at[1, layer], pair_recv.at[1, layer], mate)

    def unpack(layer):
        i = layer % 2
        landed(rows_at(final, layer, (1 - core) * 512, 512), pair_recv.at[1, layer])
        for tap in range(TAPS):
            base = tap * TAP_ROWS
            top = final[layer, base : base + 64, :]
            near = final[layer, base + 64 : base + 96, :]
            out_weight[i, 9 + tap] = top[:, 0:64]
            out_weight[i, 18 + tap] = turned(top)[:, 0:64]
            out_weight[i, tap, 0:32, :] = near[:, 0:64]
            out_weight[i, tap, 32:64, :] = turned(near)[:, 0:64]
        out_bias[i : i + 1, :] = final[layer, 864:865, 0:64]

    everywhere = [reduce_half, reduce_one, reduce_two]
    at_home = [gather_three, gather_two, gather_one, gather_half, unpack]

    def backward(step, carry):
        layer = LAYERS - 1 - step
        slot = LAYERS + layer
        value = pre[layer]
        sigma = 1.0 / (1.0 + jnp.exp(-value))
        slope = flow[...] * sigma * (1.0 + value * (1.0 - sigma))
        for y in range(2):
            ext[slot, 1 + y, 8:136, :] = slope[y * 128 : (y + 1) * 128, :]
        send_rims(slot)

        across = jnp.concatenate([slope[0:128, :].T, slope[128:256, :].T], axis=1)
        high, low = split_parts(across)
        sides = jnp.concatenate(
            [
                jnp.concatenate([high, high], axis=1),
                jnp.concatenate([low, low], axis=1),
            ],
            axis=0,
        )
        product = jnp.dot(sides, patch[layer], preferred_element_type=F32)
        for tap in range(TAPS):
            cols = slice(tap * 128, tap * 128 + 128)
            block = product[0:128, cols] + product[128:256, cols]
            base = tap * TAP_ROWS
            flipped = turned(block[64:128, :])
            part[layer, base : base + 64, :] = block[0:64, :] + jnp.where(left, flipped, 0.0)
            part[layer, base + 64 : base + 96, :] = jnp.where(
                left, block[64:96, :], flipped[32:64, :]
            )
        sums = jnp.sum(slope, axis=0, keepdims=True)
        part[layer, 864:865, :] = sums + turned(sums)
        reduce_start(layer)
        for k, tick in enumerate(everywhere):

            @pl.when(layer + k + 1 < LAYERS)
            def _():
                tick(layer + k + 1)

        await_rims(slot)

        def store(y, tap, high, low):
            cols = slice(tap * 128, tap * 128 + 128)
            slope_patch[y * 128 : y * 128 + 128, cols] = high
            slope_patch[256 + y * 128 : 384 + y * 128, cols] = low

        fill(slot, store)
        gradient = joined(
            jnp.dot(slope_patch[...], wide_b[layer], preferred_element_type=F32)
        )
        flow[...] = gradient

        @pl.when(layer == 2)
        def _():
            hand_out(gradient, 1, 1, out_grad)

        @pl.when(layer == 0)
        def _():
            hand_out(gradient, 0, 1, out_grad)

        return carry

    lax.fori_loop(0, LAYERS, backward, 0)

    for round_at in range(8):
        for layer in reversed(range(LAYERS)):
            tick = layer + round_at
            if tick < 3:
                everywhere[tick](layer)
            elif tick < 8:

                @pl.when(sec == layer // 2)
                def _():
                    at_home[tick - 3](layer)

    landed(out_act.at[1 - sec], out_recv.at[0])
    landed(out_grad.at[1 - sec], out_recv.at[1])

    def drain_rims(slot, carry):
        for d, (dy, dz) in enumerate(DIRS):
            rows, cells = source_window(dy, dz)

            @pl.when(exists(dy, dz))
            def _():
                landed(ext.at[slot, rows, cells, :], halo_send.at[slot, d])

        return carry

    lax.fori_loop(0, 8, drain_rims, 0)
    for i in range(2):
        for chunk in range(CHUNKS):

            @pl.when(at_end)
            def _():
                landed(chunk_of(2 * sec + i, core, chunk), source_send.at[i, chunk])

            @pl.when(jnp.logical_not(at_end))
            def _():
                landed(chunk_of(2 * other + i, core, chunk), relay_send.at[i, chunk])

            landed(chunk_of(2 * other + i, core, chunk), mate_send.at[i, chunk])
    for kind in range(2):
        landed(stage.at[kind], out_send.at[kind])

    def drain_sums(layer, carry):
        home = sec == layer // 2
        landed(half_in.at[layer], pair_send.at[0, layer])
        for s in range(3):
            landed(one_in.at[layer, s], group_send.at[0, layer, s])
            landed(two_in.at[layer, s], group_send.at[1, layer, s])
        for d in range(1, 8):

            @pl.when(((depth + d) % 8) // 4 == layer // 2)
            def _():
                landed(three_in.at[layer, 7 - d], deep_send.at[layer, 7 - d])

        @pl.when(home)
        def _():
            for s in range(3):
                landed(three_in.at[layer, s], group_send.at[2, layer, s])
                landed(two_in.at[layer, s], group_send.at[3, layer, s])
                landed(one_in.at[layer, s], group_send.at[4, layer, s])
            landed(half_in.at[layer], pair_send.at[1, layer])

        return carry

    lax.fori_loop(0, LAYERS, drain_sums, 0)


def per_device(inflow, weights, biases, cotangent):
    micro, channels, nx, ny, nz = inflow.shape
    cells = micro * nx * ny * lax.axis_size("gy") * nz * lax.axis_size("gz")
    scale = 1.0 / math.sqrt(cells)
    rows = channels * nx * ny
    vmem = pltpu.VMEM
    dma = pltpu.SemaphoreType.DMA
    scratch = [
        vmem((8, 4, 144, 128), F32),
        vmem((LAYERS, 512, TAPS * 128), BF16),
        vmem((512, TAPS * 128), BF16),
        vmem((LAYERS, 256, TAPS * 128), BF16),
        vmem((LAYERS, TAPS * 128, 256), BF16),
        vmem((LAYERS, PACK, 128), F32),
        vmem((LAYERS, 256, 128), F32),
        vmem((256, 128), F32),
        vmem((2, 256, 128), F32),
        vmem((LAYERS, GRAD, 128), F32),
        vmem((LAYERS, GRAD, 128), F32),
        vmem((LAYERS, 512, 128), F32),
        vmem((LAYERS, 512, 128), F32),
        vmem((LAYERS, 3, 128, 128), F32),
        vmem((LAYERS, 128, 128), F32),
        vmem((LAYERS, 3, 32, 128), F32),
        vmem((LAYERS, 32, 128), F32),
        vmem((LAYERS, 7, 8, 128), F32),
        dma((8, 8)),
        dma((8, 8)),
        dma((2, CHUNKS)),
        dma((2, CHUNKS)),
        dma((2, CHUNKS)),
        dma((2, CHUNKS)),
        dma((2, CHUNKS)),
        dma((2,)),
        dma((2,)),
        dma((2, LAYERS)),
        dma((2, LAYERS)),
        dma((5, LAYERS, 3)),
        dma((5, LAYERS, 3)),
        dma((LAYERS, 7)),
        dma((LAYERS, 7)),
    ]
    spec = pl.BlockSpec(memory_space=pltpu.VMEM)

    def body(*refs):
        kernel(scale, *refs)

    act, grad, weight, bias = pl.pallas_call(
        body,
        name="encoder_sections",
        out_shape=(
            jax.ShapeDtypeStruct((micro, rows, nz), F32),
            jax.ShapeDtypeStruct((micro, rows, nz), F32),
            jax.ShapeDtypeStruct(weights.shape, F32),
            jax.ShapeDtypeStruct(biases.shape, F32),
        ),
        in_specs=[spec] * 4,
        out_specs=(spec,) * 4,
        scratch_shapes=scratch,
        compiler_params=pltpu.CompilerParams(
            collective_id=0, has_side_effects=True, vmem_limit_bytes=60 << 20
        ),
    )(
        inflow.reshape(micro, rows, nz),
        weights,
        biases,
        cotangent.reshape(micro, rows, nz),
    )
    shape = (1, micro, channels, nx, ny, nz)
    return act.reshape(shape), grad.reshape(shape), weight, bias


def solution(mesh):
    return jax.shard_map(
        per_device,
        mesh=mesh,
        in_specs=(
            P(None, None, None, "gy", "gz"),
            P("section", None, None, None),
            P("section", None),
            P(None, None, None, "gy", "gz"),
        ),
        out_specs=(
            P("section", None, None, None, "gy", "gz"),
            P("section", None, None, None, "gy", "gz"),
            P("section", None, None, None),
            P("section", None),
        ),
        check_vma=False,
    )
```

```python
import math

import jax
import jax.numpy as jnp
from jax import lax
from jax.experimental import pallas as pl
from jax.experimental.pallas import tpu as pltpu
from jax.sharding import PartitionSpec as P

MESH = pl.DeviceIdType.MESH
F32 = jnp.float32
BF16 = jnp.bfloat16
LAYERS = 4
TAPS = 9
DIRS = [(dy, dz) for dy in (-1, 0, 1) for dz in (-1, 0, 1) if (dy, dz) != (0, 0)]
TAP_ROWS = 96
PACK = 880
CHUNKS = 5
CHUNK = PACK // 2 // CHUNKS
EARLY = 3
GRAD = 1024


def split_parts(value):
    high = value.astype(BF16)
    return high, (value - high.astype(F32)).astype(BF16)


def source_window(dy, dz):
    rows = {1: pl.ds(2, 1), -1: pl.ds(1, 1), 0: pl.ds(1, 2)}[dy]
    cells = {1: pl.ds(128, 8), -1: pl.ds(8, 8), 0: pl.ds(8, 128)}[dz]
    return rows, cells


def target_window(dy, dz):
    rows = {1: pl.ds(0, 1), -1: pl.ds(3, 1), 0: pl.ds(1, 2)}[dy]
    cells = {1: pl.ds(0, 8), -1: pl.ds(136, 8), 0: pl.ds(8, 128)}[dz]
    return rows, cells


def landed(ref, sem):
    pltpu.make_async_copy(ref, ref, sem).wait()


def kernel(
    scale,
    inflow_hbm,
    weights_hbm,
    biases,
    cotangent_hbm,
    out_act,
    out_grad,
    final,
    inflow,
    weights,
    cotangent,
    ext,
    patch,
    slope_patch,
    wide_f,
    wide_b,
    packed,
    pre,
    flow,
    stage,
    part,
    half_in,
    half_sum,
    one_in,
    one_sum,
    two_in,
    two_sum,
    three_in,
    load_sem,
    halo_send,
    halo_recv,
    source_send,
    relay_send,
    relay_recv,
    mate_send,
    mate_recv,
    out_send,
    out_recv,
    pair_send,
    pair_recv,
    group_send,
    group_recv,
    deep_send,
    deep_recv,
):
    sec = lax.axis_index("section")
    gy = lax.axis_index("gy")
    gz = lax.axis_index("gz")
    core = gy % 2
    px = (gy // 2) % 4
    zlo = gy // 8
    depth = sec * 4 + zlo
    other = 1 - sec

    def at_depth(level, parity):
        return (level // 4, (level % 4) * 8 + px * 2 + parity, gz)

    def in_plane(first, index):
        on_x = (1 - core) if first else core
        new_gy = gy + on_x * 2 * (index - px)
        new_gz = gz + (1 - on_x) * (index - gz)
        return (sec, new_gy, new_gz)

    mate = (sec, gy + 1 - 2 * core, gz)
    first_plane = zlo == 0
    last_plane = zlo == 3
    at_end = jnp.logical_or(first_plane, last_plane)
    outward = at_depth((depth + jnp.where(last_plane, 1, 7)) % 8, core)
    inward = at_depth((depth + jnp.where(last_plane, 7, 1)) % 8, core)

    def exists(dy, dz):
        ok = None
        for index, delta, count in ((gy, dy, 32), (gz, dz, 4)):
            if delta == 0:
                continue
            good = index > 0 if delta < 0 else index < count - 1
            ok = good if ok is None else jnp.logical_and(ok, good)
        return ok

    lane = lax.broadcasted_iota(jnp.int32, (1, 128), 1)
    left = lane < 64

    def turned(value):
        return pltpu.roll(value, 64, 1)

    loads = [
        pltpu.make_async_copy(weights_hbm, weights, load_sem.at[0]),
        pltpu.make_async_copy(inflow_hbm.at[sec], inflow, load_sem.at[1]),
        pltpu.make_async_copy(cotangent_hbm.at[sec], cotangent, load_sem.at[2]),
    ]
    for load in loads:
        load.start()

    barrier = pltpu.get_barrier_semaphore()

    def greet(device):
        pl.semaphore_signal(barrier, inc=1, device_id=device, device_id_type=MESH)

    for d in range(1, 8):
        greet(at_depth((depth + d) % 8, core))
    for d in range(1, 4):
        greet((sec, gy + 2 * ((px + d) % 4 - px), gz))
        greet((sec, gy, (gz + d) % 4))
    for dy, dz in DIRS:
        if dy != 0:

            @pl.when(exists(dy, dz))
            def _():
                greet((sec, gy + dy, gz + dz))

    sides_y = 2 - jnp.where(gy == 0, 1, 0) - jnp.where(gy == 31, 1, 0)
    sides_z = 2 - jnp.where(gz == 0, 1, 0) - jnp.where(gz == 3, 1, 0)
    def clear(rows, cells):
        shape = (8, rows.size, cells.size, 128)
        ext[:, rows, cells, :] = jnp.zeros(shape, F32)

    @pl.when(gy == 0)
    def _():
        clear(pl.ds(0, 1), pl.ds(0, 144))

    @pl.when(gy == 31)
    def _():
        clear(pl.ds(3, 1), pl.ds(0, 144))

    @pl.when(gz == 0)
    def _():
        clear(pl.ds(0, 4), pl.ds(0, 8))

    @pl.when(gz == 3)
    def _():
        clear(pl.ds(0, 4), pl.ds(136, 8))

    def turned_in(ref, y):
        rows = [ref[pl.ds(2 * x + y, 64, stride=4), :] for x in range(2)]
        return jnp.concatenate(rows, axis=0).T

    loads[1].wait()
    for y in range(2):
        ext[0, 1 + y, 8:136, :] = turned_in(inflow, y)
    loads[0].wait()
    for i in range(2):
        for b in range(3):
            for c in range(3):
                tap = b * 3 + c
                base = tap * TAP_ROWS
                middle = weights[i, 9 + tap]
                far = weights[i, 18 + tap]
                near = weights[i, tap]
                packed[2 * sec + i, base : base + 64, :] = jnp.concatenate([middle, far], axis=1)
                packed[2 * sec + i, base + 64 : base + 96, :] = jnp.concatenate(
                    [near[0:32], near[32:64]], axis=1
                )
        row = biases[i : i + 1, :]
        packed[2 * sec + i, 864:880, :] = jnp.broadcast_to(
            jnp.concatenate([row, row], axis=1), (16, 128)
        )

    pl.semaphore_wait(barrier, 13 + sides_y * (1 + sides_z))

    def send_rims(slot):
        for d, (dy, dz) in enumerate(DIRS):
            rows, cells = source_window(dy, dz)
            rows_to, cells_to = target_window(dy, dz)

            @pl.when(exists(dy, dz))
            def _():
                pltpu.make_async_remote_copy(
                    src_ref=ext.at[slot, rows, cells, :],
                    dst_ref=ext.at[slot, rows_to, cells_to, :],
                    send_sem=halo_send.at[slot, d],
                    recv_sem=halo_recv.at[slot, d],
                    device_id=(sec, gy + dy, gz + dz),
                    device_id_type=MESH,
                ).start()

    def await_rims(slot):
        for d, (dy, dz) in enumerate(DIRS):
            rows_to, cells_to = target_window(dy, dz)

            @pl.when(exists(-dy, -dz))
            def _():
                landed(ext.at[slot, rows_to, cells_to, :], halo_recv.at[slot, d])

    send_rims(0)

    def chunk_of(layer, parity, chunk):
        start = parity * (PACK // 2) + chunk * CHUNK
        return packed.at[layer, pl.ds(pl.multiple_of(start, 8), CHUNK), :]

    def pass_on(layer, i, chunk, send, recv, device):
        piece = chunk_of(layer, core, chunk)
        pltpu.make_async_remote_copy(
            src_ref=piece,
            dst_ref=piece,
            send_sem=send.at[i, chunk],
            recv_sem=recv.at[i, chunk],
            device_id=device,
            device_id_type=MESH,
        ).start()

    @pl.when(at_end)
    def _():
        for i in range(2):
            for chunk in range(CHUNKS):
                pass_on(2 * sec + i, i, chunk, source_send, relay_recv, outward)

    def widen(layer):
        for tap in range(TAPS):
            base = tap * TAP_ROWS
            top = packed[layer, base : base + 64, :]
            near = packed[layer, base + 64 : base + 96, :]
            bottom = jnp.where(
                left, jnp.concatenate([near, turned(near)], axis=0), turned(top)
            )
            high, low = split_parts(jnp.concatenate([top, bottom], axis=0))
            cols = slice(tap * 128, tap * 128 + 128)
            wide_f[layer, 0:128, cols] = high
            wide_f[layer, 128:256, cols] = low
            rows = slice((8 - tap) * 128, (8 - tap) * 128 + 128)
            wide_b[layer, rows, 0:128] = high
            wide_b[layer, rows, 128:256] = low

    def widen_own(i, carry):
        widen(2 * sec + i)
        return carry

    lax.fori_loop(0, 2, widen_own, 0)

    loads[2].wait()
    for y in range(2):
        flow[y * 128 : (y + 1) * 128, :] = turned_in(cotangent, y)
    for layer in range(LAYERS):
        part[layer, 864:GRAD, :] = jnp.zeros((GRAD - 864, 128), F32)

    def relay(i, chunks):
        for chunk in chunks:
            landed(chunk_of(2 * other + i, core, chunk), relay_recv.at[i, chunk])

            @pl.when(at_end)
            def _():
                pass_on(2 * other + i, i, chunk, relay_send, relay_recv, inward)

            pass_on(2 * other + i, i, chunk, mate_send, mate_recv, mate)

    def receive(i):
        for chunk in range(CHUNKS):
            landed(chunk_of(2 * other + i, 1 - core, chunk), mate_recv.at[i, chunk])
        widen(2 * other + i)

    relay(0, range(CHUNKS))
    receive(0)
    relay(1, range(EARLY))

    def fill(slot, store):
        for c in range(3):
            for row in range(4):
                high, low = split_parts(ext[slot, row, 7 + c : 135 + c, :])
                for y in range(2):
                    b = row - y
                    if 0 <= b <= 2:
                        tap = b * 3 + c
                        store(y, tap, high, low)

    def hand_out(value, keeper, kind, result):
        def put(ref, lead):
            for y in range(2):
                block = value[y * 128 : (y + 1) * 128, :].T
                for x in range(2):
                    where = pl.ds(2 * x + y, 64, stride=4)
                    ref[lead, where, :] = block[x * 64 : (x + 1) * 64, :]

        @pl.when(sec == keeper)
        def _():
            put(result, sec)

        @pl.when(sec != keeper)
        def _():
            put(stage, kind)
            pltpu.make_async_remote_copy(
                src_ref=stage.at[kind],
                dst_ref=result.at[sec],
                send_sem=out_send.at[kind],
                recv_sem=out_recv.at[kind],
                device_id=(other, gy, gz),
                device_id_type=MESH,
            ).start()

    def joined(product):
        return (
            product[0:256, 0:128]
            + product[0:256, 128:256]
            + product[256:512, 0:128]
            + product[256:512, 128:256]
        )

    def forward(layer, carry):
        await_rims(layer)

        def store(y, tap, high, low):
            cols = slice(tap * 128, tap * 128 + 128)
            patch[layer, y * 128 : y * 128 + 128, cols] = high
            patch[layer, 256 + y * 128 : 384 + y * 128, cols] = low

        fill(layer, store)
        product = lax.dot_general(
            patch[layer],
            wide_f[layer],
            (((1,), (1,)), ((), ())),
            preferred_element_type=F32,
        )
        value = joined(product) + packed[layer, 864:865, :]
        pre[layer] = value
        active = value * (1.0 / (1.0 + jnp.exp(-value)))

        @pl.when(layer < LAYERS - 1)
        def _():
            for y in range(2):
                ext[layer + 1, 1 + y, 8:136, :] = active[y * 128 : (y + 1) * 128, :]
            send_rims(layer + 1)

        @pl.when(layer == 0)
        def _():
            relay(1, range(EARLY, CHUNKS))
            receive(1)

        @pl.when(layer == 1)
        def _():
            hand_out(active, 0, 0, out_act)

        @pl.when(layer == 3)
        def _():
            hand_out(active, 1, 0, out_act)

        return carry

    lax.fori_loop(0, LAYERS, forward, 0)

    index_one = px + core * (gz - px)
    index_two = gz + core * (px - gz)
    offset_half = core * 512
    offset_one = offset_half + index_one * 128
    offset_two = offset_one + index_two * 32

    def rows_at(ref, layer, start, size):
        return ref.at[layer, pl.ds(pl.multiple_of(start, 8), size), :]

    def push(source, target, send, recv, device):
        pltpu.make_async_remote_copy(
            src_ref=source,
            dst_ref=target,
            send_sem=send,
            recv_sem=recv,
            device_id=device,
            device_id_type=MESH,
        ).start()

    def reduce_start(layer):
        push(
            rows_at(part, layer, (1 - core) * 512, 512),
            half_in.at[layer],
            pair_send.at[0, layer],
            pair_recv.at[0, layer],
            mate,
        )

    def reduce_half(layer):
        landed(half_in.at[layer], pair_recv.at[0, layer])
        half_sum[layer] = (
            part[layer, pl.ds(pl.multiple_of(offset_half, 8), 512), :] + half_in[layer]
        )
        for d in range(1, 4):
            peer = (index_one + d) % 4
            push(
                rows_at(half_sum, layer, peer * 128, 128),
                one_in.at[layer, 3 - d],
                group_send.at[0, layer, 3 - d],
                group_recv.at[0, layer, 3 - d],
                in_plane(True, peer),
            )

    def reduce_one(layer):
        for s in range(3):
            landed(one_in.at[layer, s], group_recv.at[0, layer, s])
        own = half_sum[layer, pl.ds(pl.multiple_of(index_one * 128, 8), 128), :]
        one_sum[layer] = (own + one_in[layer, 0]) + (one_in[layer, 1] + one_in[layer, 2])
        for d in range(1, 4):
            peer = (index_two + d) % 4
            push(
                rows_at(one_sum, layer, peer * 32, 32),
                two_in.at[layer, 3 - d],
                group_send.at[1, layer, 3 - d],
                group_recv.at[1, layer, 3 - d],
                in_plane(False, peer),
            )

    def reduce_two(layer):
        for s in range(3):
            landed(two_in.at[layer, s], group_recv.at[1, layer, s])
        own = one_sum[layer, pl.ds(pl.multiple_of(index_two * 32, 8), 32), :]
        two_sum[layer] = (own + two_in[layer, 0]) + (two_in[layer, 1] + two_in[layer, 2])
        for d in range(1, 8):
            peer = (depth + d) % 8

            @pl.when(peer // 4 == layer // 2)
            def _():
                push(
                    two_sum.at[layer],
                    three_in.at[layer, depth],
                    deep_send.at[layer, d - 1],
                    deep_recv.at[layer, d - 1],
                    at_depth(peer, core),
                )

    def gathered(layer, stage_at, base, index, size):
        for s in range(3):
            sender = (index + 1 + s) % 4
            piece = rows_at(final, layer % 2, base + sender * size, size)
            landed(piece, group_recv.at[stage_at, layer, s])

    def gather_two(layer):
        for d in range(1, 8):
            landed(three_in.at[layer, (depth + 8 - d) % 8], deep_recv.at[layer, d - 1])
        three_in[layer, depth] = two_sum[layer]
        total = three_in[layer, 0]
        for level in range(1, 8):
            total = total + three_in[layer, level]
        final[layer % 2, pl.ds(pl.multiple_of(offset_two, 8), 32), :] = total * scale
        for d in range(1, 4):
            piece = rows_at(final, layer % 2, offset_two, 32)
            push(
                piece,
                piece,
                group_send.at[2, layer, 3 - d],
                group_recv.at[2, layer, 3 - d],
                in_plane(False, (index_two + d) % 4),
            )

    def gather_one(layer):
        gathered(layer, 2, offset_one, index_two, 32)
        for d in range(1, 4):
            piece = rows_at(final, layer % 2, offset_one, 128)
            push(
                piece,
                piece,
                group_send.at[3, layer, 3 - d],
                group_recv.at[3, layer, 3 - d],
                in_plane(True, (index_one + d) % 4),
            )

    def gather_half(layer):
        gathered(layer, 3, offset_half, index_one, 128)
        piece = rows_at(final, layer % 2, offset_half, 512)
        push(piece, piece, pair_send.at[1, layer], pair_recv.at[1, layer], mate)

    def finish(layer):
        piece = rows_at(final, layer % 2, (1 - core) * 512, 512)
        landed(piece, pair_recv.at[1, layer])

    everywhere = [reduce_half, reduce_one, reduce_two]
    at_home = [gather_two, gather_one, gather_half, finish]

    def backward(step, carry):
        layer = LAYERS - 1 - step
        slot = LAYERS + layer
        value = pre[layer]
        sigma = 1.0 / (1.0 + jnp.exp(-value))
        slope = flow[...] * sigma * (1.0 + value * (1.0 - sigma))
        for y in range(2):
            ext[slot, 1 + y, 8:136, :] = slope[y * 128 : (y + 1) * 128, :]
        send_rims(slot)

        across = jnp.concatenate([slope[0:128, :].T, slope[128:256, :].T], axis=1)
        high, low = split_parts(across)
        sides = jnp.concatenate(
            [
                jnp.concatenate([high, high], axis=1),
                jnp.concatenate([low, low], axis=1),
            ],
            axis=0,
        )
        product = jnp.dot(sides, patch[layer], preferred_element_type=F32)
        for tap in range(TAPS):
            cols = slice(tap * 128, tap * 128 + 128)
            block = product[0:128, cols] + product[128:256, cols]
            base = tap * TAP_ROWS
            flipped = turned(block[64:128, :])
            part[layer, base : base + 64, :] = block[0:64, :] + jnp.where(left, flipped, 0.0)
            part[layer, base + 64 : base + 96, :] = jnp.where(
                left, block[64:96, :], flipped[32:64, :]
            )
        sums = jnp.sum(slope, axis=0, keepdims=True)
        part[layer, 864:865, :] = sums + turned(sums)
        reduce_start(layer)
        for k, tick in enumerate(everywhere):

            @pl.when(layer + k + 1 < LAYERS)
            def _():
                tick(layer + k + 1)

        await_rims(slot)

        def store(y, tap, high, low):
            cols = slice(tap * 128, tap * 128 + 128)
            slope_patch[y * 128 : y * 128 + 128, cols] = high
            slope_patch[256 + y * 128 : 384 + y * 128, cols] = low

        fill(slot, store)
        gradient = joined(
            jnp.dot(slope_patch[...], wide_b[layer], preferred_element_type=F32)
        )
        flow[...] = gradient

        @pl.when(layer == 2)
        def _():
            hand_out(gradient, 1, 1, out_grad)

        @pl.when(layer == 0)
        def _():
            hand_out(gradient, 0, 1, out_grad)

        return carry

    lax.fori_loop(0, LAYERS, backward, 0)

    for round_at in range(7):
        for layer in reversed(range(LAYERS)):
            tick = layer + round_at
            if tick < 3:
                everywhere[tick](layer)
            elif tick < 7:

                @pl.when(sec == layer // 2)
                def _():
                    at_home[tick - 3](layer)

    landed(out_act.at[1 - sec], out_recv.at[0])
    landed(out_grad.at[1 - sec], out_recv.at[1])

    def drain_rims(slot, carry):
        for d, (dy, dz) in enumerate(DIRS):
            rows, cells = source_window(dy, dz)

            @pl.when(exists(dy, dz))
            def _():
                landed(ext.at[slot, rows, cells, :], halo_send.at[slot, d])

        return carry

    lax.fori_loop(0, 8, drain_rims, 0)
    for i in range(2):
        for chunk in range(CHUNKS):

            @pl.when(at_end)
            def _():
                landed(chunk_of(2 * sec + i, core, chunk), source_send.at[i, chunk])

            @pl.when(at_end)
            def _():
                landed(chunk_of(2 * other + i, core, chunk), relay_send.at[i, chunk])

            landed(chunk_of(2 * other + i, core, chunk), mate_send.at[i, chunk])
    for kind in range(2):
        landed(stage.at[kind], out_send.at[kind])

    def drain_sums(layer, carry):
        home = sec == layer // 2
        landed(half_in.at[layer], pair_send.at[0, layer])
        for s in range(3):
            landed(one_in.at[layer, s], group_send.at[0, layer, s])
            landed(two_in.at[layer, s], group_send.at[1, layer, s])
        for d in range(1, 8):

            @pl.when(((depth + d) % 8) // 4 == layer // 2)
            def _():
                landed(two_sum.at[layer], deep_send.at[layer, d - 1])

        @pl.when(home)
        def _():
            for s in range(3):
                landed(two_in.at[layer, s], group_send.at[2, layer, s])
                landed(one_in.at[layer, s], group_send.at[3, layer, s])
            landed(half_in.at[layer], pair_send.at[1, layer])

        return carry

    lax.fori_loop(0, LAYERS, drain_sums, 0)


def unpack(act, grad, total, out_act, out_grad, out_weight, out_bias, spread, sem):
    copies = [
        pltpu.make_async_copy(act, out_act, sem.at[0]),
        pltpu.make_async_copy(grad, out_grad, sem.at[1]),
    ]
    for copy in copies:
        copy.start()
    for i in range(2):
        for tap in range(TAPS):
            base = tap * TAP_ROWS
            top = total[i, base : base + 64, :]
            near = total[i, base + 64 : base + 96, :]
            spread[i, 9 + tap] = top[:, 0:64]
            spread[i, 18 + tap] = pltpu.roll(top, 64, 1)[:, 0:64]
            spread[i, tap, 0:32, :] = near[:, 0:64]
            spread[i, tap, 32:64, :] = pltpu.roll(near, 64, 1)[:, 0:64]
        copies.append(pltpu.make_async_copy(spread.at[i], out_weight.at[i], sem.at[2 + i]))
        copies[-1].start()
    out_bias[...] = total[:, 864, 0:64]
    for copy in copies:
        copy.wait()


def per_device(inflow, weights, biases, cotangent):
    micro, channels, nx, ny, nz = inflow.shape
    cells = micro * nx * ny * lax.axis_size("gy") * nz * lax.axis_size("gz")
    scale = 1.0 / math.sqrt(cells)
    rows = channels * nx * ny
    vmem = pltpu.VMEM
    dma = pltpu.SemaphoreType.DMA
    scratch = [
        vmem((rows, nz), F32),
        vmem(weights.shape, F32),
        vmem((rows, nz), F32),
        vmem((8, 4, 144, 128), F32),
        vmem((LAYERS, 512, TAPS * 128), BF16),
        vmem((512, TAPS * 128), BF16),
        vmem((LAYERS, 256, TAPS * 128), BF16),
        vmem((LAYERS, TAPS * 128, 256), BF16),
        vmem((LAYERS, PACK, 128), F32),
        vmem((LAYERS, 256, 128), F32),
        vmem((256, 128), F32),
        vmem((2, 256, 128), F32),
        vmem((LAYERS, GRAD, 128), F32),
        vmem((LAYERS, 512, 128), F32),
        vmem((LAYERS, 512, 128), F32),
        vmem((LAYERS, 3, 128, 128), F32),
        vmem((LAYERS, 128, 128), F32),
        vmem((LAYERS, 3, 32, 128), F32),
        vmem((LAYERS, 32, 128), F32),
        vmem((LAYERS, 8, 32, 128), F32),
        dma((3,)),
        dma((8, 8)),
        dma((8, 8)),
        dma((2, CHUNKS)),
        dma((2, CHUNKS)),
        dma((2, CHUNKS)),
        dma((2, CHUNKS)),
        dma((2, CHUNKS)),
        dma((2,)),
        dma((2,)),
        dma((2, LAYERS)),
        dma((2, LAYERS)),
        dma((4, LAYERS, 3)),
        dma((4, LAYERS, 3)),
        dma((LAYERS, 7)),
        dma((LAYERS, 7)),
    ]
    near = pl.BlockSpec(memory_space=pltpu.VMEM)
    far = pl.BlockSpec(memory_space=pl.ANY)

    def body(*refs):
        kernel(scale, *refs)

    act, grad, total = pl.pallas_call(
        body,
        name="encoder_sections",
        out_shape=(
            vmem((micro, rows, nz), F32),
            vmem((micro, rows, nz), F32),
            vmem((2, GRAD, 128), F32),
        ),
        in_specs=[far, far, near, far],
        out_specs=(near,) * 3,
        scratch_shapes=scratch,
        compiler_params=pltpu.CompilerParams(
            collective_id=0, has_side_effects=True, vmem_limit_bytes=56 << 20
        ),
    )(
        inflow.reshape(micro, rows, nz),
        weights,
        biases,
        cotangent.reshape(micro, rows, nz),
    )
    act, grad, weight, bias = pl.pallas_call(
        unpack,
        name="write_results",
        out_shape=(
            jax.ShapeDtypeStruct(act.shape, F32),
            jax.ShapeDtypeStruct(grad.shape, F32),
            jax.ShapeDtypeStruct(weights.shape, F32),
            jax.ShapeDtypeStruct(biases.shape, F32),
        ),
        in_specs=[near] * 3,
        out_specs=(far, far, far, near),
        scratch_shapes=[vmem(weights.shape, F32), dma((4,))],
        compiler_params=pltpu.CompilerParams(vmem_limit_bytes=8 << 20),
    )(act, grad, total)
    shape = (1, micro, channels, nx, ny, nz)
    return act.reshape(shape), grad.reshape(shape), weight, bias


def solution(mesh):
    return jax.shard_map(
        per_device,
        mesh=mesh,
        in_specs=(
            P(None, None, None, "gy", "gz"),
            P("section", None, None, None),
            P("section", None),
            P(None, None, None, "gy", "gz"),
        ),
        out_specs=(
            P("section", None, None, None, "gy", "gz"),
            P("section", None, None, None, "gy", "gz"),
            P("section", None, None, None),
            P("section", None),
        ),
        check_vma=False,
    )
```

```python
import math

import jax
import jax.numpy as jnp
from jax import lax
from jax.experimental import pallas as pl
from jax.experimental.pallas import tpu as pltpu
from jax.sharding import PartitionSpec as P

MESH = pl.DeviceIdType.MESH
F32 = jnp.float32
BF16 = jnp.bfloat16
LAYERS = 4
TAPS = 9
DIRS = [(dy, dz) for dy in (-1, 0, 1) for dz in (-1, 0, 1) if (dy, dz) != (0, 0)]
TAP_ROWS = 96
PACK = 880
CHUNKS = 5
CHUNK = PACK // 2 // CHUNKS
EARLY = 3
GRAD = 1024
WIDE = 576


def split_parts(value):
    high = value.astype(BF16)
    return high, (value - high.astype(F32)).astype(BF16)


def source_window(dy, dz):
    cells = {1: pl.ds(136, 8), -1: pl.ds(16, 8), 0: pl.ds(16, 128)}[dz]
    return pl.ds(2, 2), cells


def target_window(dy, dz):
    rows = {1: pl.ds(0, 2), -1: pl.ds(4, 2), 0: pl.ds(2, 2)}[dy]
    cells = {1: pl.ds(8, 8), -1: pl.ds(144, 8), 0: pl.ds(16, 128)}[dz]
    return rows, cells


def landed(ref, sem):
    pltpu.make_async_copy(ref, ref, sem).wait()


def kernel(
    scale,
    inflow_hbm,
    weights_hbm,
    biases,
    cotangent_hbm,
    out_act,
    out_grad,
    final,
    inflow,
    weights,
    cotangent,
    ext,
    inner,
    wide_patch,
    patch,
    slope_patch,
    wide_f,
    wide_b,
    packed,
    wide_pre,
    pre,
    flow,
    stage,
    part,
    half_in,
    half_sum,
    one_in,
    one_sum,
    two_in,
    two_sum,
    three_in,
    load_sem,
    halo_send,
    halo_recv,
    source_send,
    relay_send,
    relay_recv,
    mate_send,
    mate_recv,
    out_send,
    out_recv,
    pair_send,
    pair_recv,
    group_send,
    group_recv,
    deep_send,
    deep_recv,
):
    sec = lax.axis_index("section")
    gy = lax.axis_index("gy")
    gz = lax.axis_index("gz")
    core = gy % 2
    px = (gy // 2) % 4
    zlo = gy // 8
    depth = sec * 4 + zlo
    other = 1 - sec

    def at_depth(level, parity):
        return (level // 4, (level % 4) * 8 + px * 2 + parity, gz)

    def in_plane(first, index):
        on_x = (1 - core) if first else core
        new_gy = gy + on_x * 2 * (index - px)
        new_gz = gz + (1 - on_x) * (index - gz)
        return (sec, new_gy, new_gz)

    mate = (sec, gy + 1 - 2 * core, gz)
    first_plane = zlo == 0
    last_plane = zlo == 3
    at_end = jnp.logical_or(first_plane, last_plane)
    outward = at_depth((depth + jnp.where(last_plane, 1, 7)) % 8, core)
    inward = at_depth((depth + jnp.where(last_plane, 7, 1)) % 8, core)

    def exists(dy, dz):
        ok = None
        for index, delta, count in ((gy, dy, 32), (gz, dz, 4)):
            if delta == 0:
                continue
            good = index > 0 if delta < 0 else index < count - 1
            ok = good if ok is None else jnp.logical_and(ok, good)
        return ok

    lane = lax.broadcasted_iota(jnp.int32, (1, 128), 1)
    left = lane < 64

    def turned(value):
        return pltpu.roll(value, 64, 1)

    loads = [
        pltpu.make_async_copy(weights_hbm, weights, load_sem.at[0]),
        pltpu.make_async_copy(inflow_hbm.at[sec], inflow, load_sem.at[1]),
        pltpu.make_async_copy(cotangent_hbm.at[sec], cotangent, load_sem.at[2]),
    ]
    for load in loads:
        load.start()

    barrier = pltpu.get_barrier_semaphore()

    def greet(device):
        pl.semaphore_signal(barrier, inc=1, device_id=device, device_id_type=MESH)

    for d in range(1, 8):
        greet(at_depth((depth + d) % 8, core))
    for d in range(1, 4):
        greet((sec, gy + 2 * ((px + d) % 4 - px), gz))
        greet((sec, gy, (gz + d) % 4))
    for dy, dz in DIRS:
        if dy != 0:

            @pl.when(exists(dy, dz))
            def _():
                greet((sec, gy + dy, gz + dz))

    sides_y = 2 - jnp.where(gy == 0, 1, 0) - jnp.where(gy == 31, 1, 0)
    sides_z = 2 - jnp.where(gz == 0, 1, 0) - jnp.where(gz == 3, 1, 0)
    def clear(rows, cells):
        ext[:, rows, cells, :] = jnp.zeros((4, rows.size, cells.size, 128), F32)

    clear(pl.ds(0, 6), pl.ds(0, 8))
    clear(pl.ds(0, 6), pl.ds(152, 8))

    @pl.when(gy == 0)
    def _():
        clear(pl.ds(0, 2), pl.ds(8, 144))

    @pl.when(gy == 31)
    def _():
        clear(pl.ds(4, 2), pl.ds(8, 144))

    @pl.when(gz == 0)
    def _():
        clear(pl.ds(0, 6), pl.ds(8, 8))

    @pl.when(gz == 3)
    def _():
        clear(pl.ds(0, 6), pl.ds(144, 8))

    def turned_in(ref, y):
        rows = [ref[pl.ds(2 * x + y, 64, stride=4), :] for x in range(2)]
        return jnp.concatenate(rows, axis=0).T

    loads[1].wait()
    for y in range(2):
        ext[0, 2 + y, 16:144, :] = turned_in(inflow, y)
    loads[0].wait()
    for i in range(2):
        for b in range(3):
            for c in range(3):
                tap = b * 3 + c
                base = tap * TAP_ROWS
                middle = weights[i, 9 + tap]
                far = weights[i, 18 + tap]
                near = weights[i, tap]
                packed[2 * sec + i, base : base + 64, :] = jnp.concatenate([middle, far], axis=1)
                packed[2 * sec + i, base + 64 : base + 96, :] = jnp.concatenate(
                    [near[0:32], near[32:64]], axis=1
                )
        row = biases[i : i + 1, :]
        packed[2 * sec + i, 864:880, :] = jnp.broadcast_to(
            jnp.concatenate([row, row], axis=1), (16, 128)
        )

    pl.semaphore_wait(barrier, 13 + sides_y * (1 + sides_z))

    def send_rims(slot):
        for d, (dy, dz) in enumerate(DIRS):
            rows, cells = source_window(dy, dz)
            rows_to, cells_to = target_window(dy, dz)

            @pl.when(exists(dy, dz))
            def _():
                pltpu.make_async_remote_copy(
                    src_ref=ext.at[slot, rows, cells, :],
                    dst_ref=ext.at[slot, rows_to, cells_to, :],
                    send_sem=halo_send.at[slot, d],
                    recv_sem=halo_recv.at[slot, d],
                    device_id=(sec, gy + dy, gz + dz),
                    device_id_type=MESH,
                ).start()

    def await_rims(slot):
        for d, (dy, dz) in enumerate(DIRS):
            rows_to, cells_to = target_window(dy, dz)

            @pl.when(exists(-dy, -dz))
            def _():
                landed(ext.at[slot, rows_to, cells_to, :], halo_recv.at[slot, d])

    send_rims(0)

    def chunk_of(layer, parity, chunk):
        start = parity * (PACK // 2) + chunk * CHUNK
        return packed.at[layer, pl.ds(pl.multiple_of(start, 8), CHUNK), :]

    def pass_on(layer, i, chunk, send, recv, device):
        piece = chunk_of(layer, core, chunk)
        pltpu.make_async_remote_copy(
            src_ref=piece,
            dst_ref=piece,
            send_sem=send.at[i, chunk],
            recv_sem=recv.at[i, chunk],
            device_id=device,
            device_id_type=MESH,
        ).start()

    @pl.when(at_end)
    def _():
        for i in range(2):
            for chunk in range(CHUNKS):
                pass_on(2 * sec + i, i, chunk, source_send, relay_recv, outward)

    def widen(layer):
        for tap in range(TAPS):
            base = tap * TAP_ROWS
            top = packed[layer, base : base + 64, :]
            near = packed[layer, base + 64 : base + 96, :]
            bottom = jnp.where(
                left, jnp.concatenate([near, turned(near)], axis=0), turned(top)
            )
            high, low = split_parts(jnp.concatenate([top, bottom], axis=0))
            cols = slice(tap * 128, tap * 128 + 128)
            wide_f[layer, 0:128, cols] = high
            wide_f[layer, 128:256, cols] = low
            rows = slice((8 - tap) * 128, (8 - tap) * 128 + 128)
            wide_b[layer, rows, 0:128] = high
            wide_b[layer, rows, 128:256] = low

    def widen_own(i, carry):
        widen(2 * sec + i)
        return carry

    lax.fori_loop(0, 2, widen_own, 0)

    loads[2].wait()
    for y in range(2):
        flow[y * 128 : (y + 1) * 128, :] = turned_in(cotangent, y)
    for layer in range(LAYERS):
        part[layer, 864:GRAD, :] = jnp.zeros((GRAD - 864, 128), F32)

    def relay(i, chunks):
        for chunk in chunks:
            landed(chunk_of(2 * other + i, core, chunk), relay_recv.at[i, chunk])

            @pl.when(at_end)
            def _():
                pass_on(2 * other + i, i, chunk, relay_send, relay_recv, inward)

            pass_on(2 * other + i, i, chunk, mate_send, mate_recv, mate)

    def receive(i):
        for chunk in range(CHUNKS):
            landed(chunk_of(2 * other + i, 1 - core, chunk), mate_recv.at[i, chunk])
        widen(2 * other + i)

    relay(0, range(CHUNKS))
    receive(0)
    relay(1, range(EARLY))

    def reach(condition):
        return lane < jnp.where(condition, 128, 0)

    inside_low, inside_high = reach(gz > 0), reach(gz < 3)
    inside_line = [reach(gy > 0), None, None, reach(gy < 31)]

    def fill_wide(slot, put):
        for c in range(3):
            for row in range(6):
                line = ext[slot, row, 15 + c : 143 + c, :]
                edge = jnp.concatenate(
                    [ext[slot, row, 7 + c : 15 + c, :], ext[slot, row, 143 + c : 151 + c, :]],
                    axis=0,
                )
                parts = zip(split_parts(line), split_parts(edge))
                for at, (line_part, edge_part) in enumerate(parts):
                    for y in range(4):
                        b = row - y
                        if 0 <= b <= 2:
                            cols = slice((b * 3 + c) * 128, (b * 3 + c) * 128 + 128)
                            start = at * WIDE + y * 128
                            put(slice(start, start + 128), cols, line_part)
                            start = at * WIDE + 512 + y * 16
                            put(slice(start, start + 16), cols, edge_part)

    def fill_inner(put):
        for c in range(3):
            for row in range(4):
                line = inner[row, 15 + c : 143 + c, :]
                for at, line_part in enumerate(split_parts(line)):
                    for y in range(2):
                        b = row - y
                        if 0 <= b <= 2:
                            cols = slice((b * 3 + c) * 128, (b * 3 + c) * 128 + 128)
                            start = at * 256 + y * 128
                            put(slice(start, start + 128), cols, line_part)

    def keep_inner(value):
        for y in range(4):
            line = value[y * 128 : (y + 1) * 128, :]
            low = value[512 + y * 16 : 520 + y * 16, :]
            high = value[520 + y * 16 : 528 + y * 16, :]
            low = jnp.where(inside_low, low, 0.0)
            high = jnp.where(inside_high, high, 0.0)
            if inside_line[y] is not None:
                line, low, high = (jnp.where(inside_line[y], v, 0.0) for v in (line, low, high))
            inner[y, 16:144, :] = line
            inner[y, 8:16, :] = low
            inner[y, 144:152, :] = high

    def hand_out(value, keeper, kind, result):
        def put(ref, lead):
            for y in range(2):
                block = value[y * 128 : (y + 1) * 128, :].T
                for x in range(2):
                    where = pl.ds(2 * x + y, 64, stride=4)
                    ref[lead, where, :] = block[x * 64 : (x + 1) * 64, :]

        @pl.when(sec == keeper)
        def _():
            put(result, sec)

        @pl.when(sec != keeper)
        def _():
            put(stage, kind)
            pltpu.make_async_remote_copy(
                src_ref=stage.at[kind],
                dst_ref=result.at[sec],
                send_sem=out_send.at[kind],
                recv_sem=out_recv.at[kind],
                device_id=(other, gy, gz),
                device_id_type=MESH,
            ).start()

    def joined(product):
        cells = product.shape[0] // 2
        return (product[:cells, 0:128] + product[:cells, 128:256]) + (
            product[cells:, 0:128] + product[cells:, 128:256]
        )

    def across(patches, layer):
        product = lax.dot_general(
            patches, wide_f[layer], (((1,), (1,)), ((), ())), preferred_element_type=F32
        )
        return joined(product) + packed[layer, 864:865, :]

    def back_across(patches, layer):
        return joined(jnp.dot(patches, wide_b[layer], preferred_element_type=F32))

    def active(value):
        return value * (1.0 / (1.0 + jnp.exp(-value)))

    def slope_of(gradient, value):
        sigma = 1.0 / (1.0 + jnp.exp(-value))
        return gradient * sigma * (1.0 + value * (1.0 - sigma))

    def keep_own(slot, value):
        for y in range(2):
            ext[slot, 2 + y, 16:144, :] = value[y * 128 : (y + 1) * 128, :]

    def forward(pair, carry):
        first = 2 * pair
        await_rims(pair)

        def put_wide(rows, cols, value):
            wide_patch[pair, rows, cols] = value

        fill_wide(pair, put_wide)
        value = across(wide_patch[pair], first)
        wide_pre[pair] = value
        keep_inner(active(value))

        @pl.when(pair == 0)
        def _():
            relay(1, range(EARLY, CHUNKS))
            receive(1)

        def put(rows, cols, value):
            patch[pair, rows, cols] = value

        fill_inner(put)
        value = across(patch[pair], first + 1)
        pre[pair] = value
        result = active(value)

        @pl.when(pair == 0)
        def _():
            keep_own(1, result)
            send_rims(1)
            hand_out(result, 0, 0, out_act)

        @pl.when(pair == 1)
        def _():
            hand_out(result, 1, 0, out_act)

        return carry

    lax.fori_loop(0, 2, forward, 0)

    index_one = px + core * (gz - px)
    index_two = gz + core * (px - gz)
    offset_half = core * 512
    offset_one = offset_half + index_one * 128
    offset_two = offset_one + index_two * 32

    def rows_at(ref, layer, start, size):
        return ref.at[layer, pl.ds(pl.multiple_of(start, 8), size), :]

    def push(source, target, send, recv, device):
        pltpu.make_async_remote_copy(
            src_ref=source,
            dst_ref=target,
            send_sem=send,
            recv_sem=recv,
            device_id=device,
            device_id_type=MESH,
        ).start()

    def reduce_start(layer):
        push(
            rows_at(part, layer, (1 - core) * 512, 512),
            half_in.at[layer],
            pair_send.at[0, layer],
            pair_recv.at[0, layer],
            mate,
        )

    def reduce_half(layer):
        landed(half_in.at[layer], pair_recv.at[0, layer])
        half_sum[layer] = (
            part[layer, pl.ds(pl.multiple_of(offset_half, 8), 512), :] + half_in[layer]
        )
        for d in range(1, 4):
            peer = (index_one + d) % 4
            push(
                rows_at(half_sum, layer, peer * 128, 128),
                one_in.at[layer, 3 - d],
                group_send.at[0, layer, 3 - d],
                group_recv.at[0, layer, 3 - d],
                in_plane(True, peer),
            )

    def reduce_one(layer):
        for s in range(3):
            landed(one_in.at[layer, s], group_recv.at[0, layer, s])
        own = half_sum[layer, pl.ds(pl.multiple_of(index_one * 128, 8), 128), :]
        one_sum[layer] = (own + one_in[layer, 0]) + (one_in[layer, 1] + one_in[layer, 2])
        for d in range(1, 4):
            peer = (index_two + d) % 4
            push(
                rows_at(one_sum, layer, peer * 32, 32),
                two_in.at[layer, 3 - d],
                group_send.at[1, layer, 3 - d],
                group_recv.at[1, layer, 3 - d],
                in_plane(False, peer),
            )

    def reduce_two(layer):
        for s in range(3):
            landed(two_in.at[layer, s], group_recv.at[1, layer, s])
        own = one_sum[layer, pl.ds(pl.multiple_of(index_two * 32, 8), 32), :]
        two_sum[layer] = (own + two_in[layer, 0]) + (two_in[layer, 1] + two_in[layer, 2])
        for d in range(1, 8):
            peer = (depth + d) % 8

            @pl.when(peer // 4 == layer // 2)
            def _():
                push(
                    two_sum.at[layer],
                    three_in.at[layer, depth],
                    deep_send.at[layer, d - 1],
                    deep_recv.at[layer, d - 1],
                    at_depth(peer, core),
                )

    def gathered(layer, stage_at, base, index, size):
        for s in range(3):
            sender = (index + 1 + s) % 4
            piece = rows_at(final, layer % 2, base + sender * size, size)
            landed(piece, group_recv.at[stage_at, layer, s])

    def gather_two(layer):
        for d in range(1, 8):
            landed(three_in.at[layer, (depth + 8 - d) % 8], deep_recv.at[layer, d - 1])
        three_in[layer, depth] = two_sum[layer]
        total = three_in[layer, 0]
        for level in range(1, 8):
            total = total + three_in[layer, level]
        final[layer % 2, pl.ds(pl.multiple_of(offset_two, 8), 32), :] = total * scale
        for d in range(1, 4):
            piece = rows_at(final, layer % 2, offset_two, 32)
            push(
                piece,
                piece,
                group_send.at[2, layer, 3 - d],
                group_recv.at[2, layer, 3 - d],
                in_plane(False, (index_two + d) % 4),
            )

    def gather_one(layer):
        gathered(layer, 2, offset_one, index_two, 32)
        for d in range(1, 4):
            piece = rows_at(final, layer % 2, offset_one, 128)
            push(
                piece,
                piece,
                group_send.at[3, layer, 3 - d],
                group_recv.at[3, layer, 3 - d],
                in_plane(True, (index_one + d) % 4),
            )

    def gather_half(layer):
        gathered(layer, 3, offset_half, index_one, 128)
        piece = rows_at(final, layer % 2, offset_half, 512)
        push(piece, piece, pair_send.at[1, layer], pair_recv.at[1, layer], mate)

    def finish(layer):
        piece = rows_at(final, layer % 2, (1 - core) * 512, 512)
        landed(piece, pair_recv.at[1, layer])

    everywhere = [reduce_half, reduce_one, reduce_two]
    at_home = [gather_two, gather_one, gather_half, finish]

    def weigh(layer, slope, high_patch, low_patch):
        turned_slope = jnp.concatenate([slope[0:128, :].T, slope[128:256, :].T], axis=1)
        sides = jnp.concatenate(split_parts(turned_slope), axis=0)
        product = jnp.dot(sides, high_patch, preferred_element_type=F32) + jnp.dot(
            sides, low_patch, preferred_element_type=F32
        )
        for tap in range(TAPS):
            cols = slice(tap * 128, tap * 128 + 128)
            block = product[0:128, cols] + product[128:256, cols]
            base = tap * TAP_ROWS
            flipped = turned(block[64:128, :])
            part[layer, base : base + 64, :] = block[0:64, :] + jnp.where(left, flipped, 0.0)
            part[layer, base + 64 : base + 96, :] = jnp.where(
                left, block[64:96, :], flipped[32:64, :]
            )
        sums = jnp.sum(slope, axis=0, keepdims=True)
        part[layer, 864:865, :] = sums + turned(sums)
        reduce_start(layer)

    def put_slope(rows, cols, value):
        slope_patch[rows, cols] = value

    def backward(step, carry):
        pair = 1 - step
        first = 2 * pair
        slot = 2 + step
        slope = slope_of(flow[...], pre[pair])
        keep_own(slot, slope)
        send_rims(slot)
        weigh(first + 1, slope, patch[pair, 0:256, :], patch[pair, 256:512, :])

        @pl.when(pair == 0)
        def _():
            reduce_half(2)
            reduce_one(3)

        await_rims(slot)
        fill_wide(slot, put_slope)
        gradient = back_across(slope_patch[...], first + 1)
        slope = slope_of(gradient, wide_pre[pair])
        keep_inner(slope)
        weigh(
            first,
            slope[128:384, :],
            wide_patch[pair, 128:384, :],
            wide_patch[pair, WIDE + 128 : WIDE + 384, :],
        )

        @pl.when(pair == 1)
        def _():
            reduce_half(3)

        @pl.when(pair == 0)
        def _():
            reduce_half(1)
            reduce_one(2)
            reduce_two(3)

        fill_inner(put_slope)
        gradient = back_across(slope_patch[0:512, :], first)
        flow[...] = gradient

        @pl.when(pair == 1)
        def _():
            hand_out(gradient, 1, 1, out_grad)

        @pl.when(pair == 0)
        def _():
            hand_out(gradient, 0, 1, out_grad)

        return carry

    lax.fori_loop(0, 2, backward, 0)

    for round_at in range(7):
        for layer in reversed(range(LAYERS)):
            tick = layer + round_at
            if tick < 3:
                everywhere[tick](layer)
            elif tick < 7:

                @pl.when(sec == layer // 2)
                def _():
                    at_home[tick - 3](layer)

    landed(out_act.at[1 - sec], out_recv.at[0])
    landed(out_grad.at[1 - sec], out_recv.at[1])

    def drain_rims(slot, carry):
        for d, (dy, dz) in enumerate(DIRS):
            rows, cells = source_window(dy, dz)

            @pl.when(exists(dy, dz))
            def _():
                landed(ext.at[slot, rows, cells, :], halo_send.at[slot, d])

        return carry

    lax.fori_loop(0, 4, drain_rims, 0)
    for i in range(2):
        for chunk in range(CHUNKS):

            @pl.when(at_end)
            def _():
                landed(chunk_of(2 * sec + i, core, chunk), source_send.at[i, chunk])

            @pl.when(at_end)
            def _():
                landed(chunk_of(2 * other + i, core, chunk), relay_send.at[i, chunk])

            landed(chunk_of(2 * other + i, core, chunk), mate_send.at[i, chunk])
    for kind in range(2):
        landed(stage.at[kind], out_send.at[kind])

    def drain_sums(layer, carry):
        home = sec == layer // 2
        landed(half_in.at[layer], pair_send.at[0, layer])
        for s in range(3):
            landed(one_in.at[layer, s], group_send.at[0, layer, s])
            landed(two_in.at[layer, s], group_send.at[1, layer, s])
        for d in range(1, 8):

            @pl.when(((depth + d) % 8) // 4 == layer // 2)
            def _():
                landed(two_sum.at[layer], deep_send.at[layer, d - 1])

        @pl.when(home)
        def _():
            for s in range(3):
                landed(two_in.at[layer, s], group_send.at[2, layer, s])
                landed(one_in.at[layer, s], group_send.at[3, layer, s])
            landed(half_in.at[layer], pair_send.at[1, layer])

        return carry

    lax.fori_loop(0, LAYERS, drain_sums, 0)


def unpack(act, grad, total, out_act, out_grad, out_weight, out_bias, spread, sem):
    copies = [
        pltpu.make_async_copy(act, out_act, sem.at[0]),
        pltpu.make_async_copy(grad, out_grad, sem.at[1]),
    ]
    for copy in copies:
        copy.start()
    for i in range(2):
        for tap in range(TAPS):
            base = tap * TAP_ROWS
            top = total[i, base : base + 64, :]
            near = total[i, base + 64 : base + 96, :]
            spread[i, 9 + tap] = top[:, 0:64]
            spread[i, 18 + tap] = pltpu.roll(top, 64, 1)[:, 0:64]
            spread[i, tap, 0:32, :] = near[:, 0:64]
            spread[i, tap, 32:64, :] = pltpu.roll(near, 64, 1)[:, 0:64]
        copies.append(pltpu.make_async_copy(spread.at[i], out_weight.at[i], sem.at[2 + i]))
        copies[-1].start()
    out_bias[...] = total[:, 864, 0:64]
    for copy in copies:
        copy.wait()


def per_device(inflow, weights, biases, cotangent):
    micro, channels, nx, ny, nz = inflow.shape
    cells = micro * nx * ny * lax.axis_size("gy") * nz * lax.axis_size("gz")
    scale = 1.0 / math.sqrt(cells)
    rows = channels * nx * ny
    vmem = pltpu.VMEM
    dma = pltpu.SemaphoreType.DMA
    scratch = [
        vmem((rows, nz), F32),
        vmem(weights.shape, F32),
        vmem((rows, nz), F32),
        vmem((4, 6, 160, 128), F32),
        vmem((4, 160, 128), F32),
        vmem((2, 2 * WIDE, TAPS * 128), BF16),
        vmem((2, 512, TAPS * 128), BF16),
        vmem((2 * WIDE, TAPS * 128), BF16),
        vmem((LAYERS, 256, TAPS * 128), BF16),
        vmem((LAYERS, TAPS * 128, 256), BF16),
        vmem((LAYERS, PACK, 128), F32),
        vmem((2, WIDE, 128), F32),
        vmem((2, 256, 128), F32),
        vmem((256, 128), F32),
        vmem((2, 256, 128), F32),
        vmem((LAYERS, GRAD, 128), F32),
        vmem((LAYERS, 512, 128), F32),
        vmem((LAYERS, 512, 128), F32),
        vmem((LAYERS, 3, 128, 128), F32),
        vmem((LAYERS, 128, 128), F32),
        vmem((LAYERS, 3, 32, 128), F32),
        vmem((LAYERS, 32, 128), F32),
        vmem((LAYERS, 8, 32, 128), F32),
        dma((3,)),
        dma((4, 8)),
        dma((4, 8)),
        dma((2, CHUNKS)),
        dma((2, CHUNKS)),
        dma((2, CHUNKS)),
        dma((2, CHUNKS)),
        dma((2, CHUNKS)),
        dma((2,)),
        dma((2,)),
        dma((2, LAYERS)),
        dma((2, LAYERS)),
        dma((4, LAYERS, 3)),
        dma((4, LAYERS, 3)),
        dma((LAYERS, 7)),
        dma((LAYERS, 7)),
    ]
    near = pl.BlockSpec(memory_space=pltpu.VMEM)
    far = pl.BlockSpec(memory_space=pl.ANY)

    def body(*refs):
        kernel(scale, *refs)

    act, grad, total = pl.pallas_call(
        body,
        name="encoder_sections",
        out_shape=(
            vmem((micro, rows, nz), F32),
            vmem((micro, rows, nz), F32),
            vmem((2, GRAD, 128), F32),
        ),
        in_specs=[far, far, near, far],
        out_specs=(near,) * 3,
        scratch_shapes=scratch,
        compiler_params=pltpu.CompilerParams(
            collective_id=0, has_side_effects=True, vmem_limit_bytes=56 << 20
        ),
    )(
        inflow.reshape(micro, rows, nz),
        weights,
        biases,
        cotangent.reshape(micro, rows, nz),
    )
    act, grad, weight, bias = pl.pallas_call(
        unpack,
        name="write_results",
        out_shape=(
            jax.ShapeDtypeStruct(act.shape, F32),
            jax.ShapeDtypeStruct(grad.shape, F32),
            jax.ShapeDtypeStruct(weights.shape, F32),
            jax.ShapeDtypeStruct(biases.shape, F32),
        ),
        in_specs=[near] * 3,
        out_specs=(far, far, far, near),
        scratch_shapes=[vmem(weights.shape, F32), dma((4,))],
        compiler_params=pltpu.CompilerParams(vmem_limit_bytes=8 << 20),
    )(act, grad, total)
    shape = (1, micro, channels, nx, ny, nz)
    return act.reshape(shape), grad.reshape(shape), weight, bias


def solution(mesh):
    return jax.shard_map(
        per_device,
        mesh=mesh,
        in_specs=(
            P(None, None, None, "gy", "gz"),
            P("section", None, None, None),
            P("section", None),
            P(None, None, None, "gy", "gz"),
        ),
        out_specs=(
            P("section", None, None, None, "gy", "gz"),
            P("section", None, None, None, "gy", "gz"),
            P("section", None, None, None),
            P("section", None),
        ),
        check_vma=False,
    )
```

```python
import math

import jax
import jax.numpy as jnp
from jax import lax
from jax.experimental import pallas as pl
from jax.experimental.pallas import tpu as pltpu
from jax.sharding import PartitionSpec as P

MESH = pl.DeviceIdType.MESH
F32 = jnp.float32
BF16 = jnp.bfloat16
LAYERS = 4
TAPS = 9
DIRS = [(dy, dz) for dy in (-1, 0, 1) for dz in (-1, 0, 1) if (dy, dz) != (0, 0)]
TAP_ROWS = 96
PACK = 880
CHUNKS = 5
CHUNK = PACK // 2 // CHUNKS
EARLY = 3
GRAD = 1024
WIDE = 576


def split_parts(value):
    high = value.astype(BF16)
    return high, (value - high.astype(F32)).astype(BF16)


def source_window(dy, dz):
    cells = {1: pl.ds(136, 8), -1: pl.ds(16, 8), 0: pl.ds(16, 128)}[dz]
    return pl.ds(2, 2), cells


def target_window(dy, dz):
    rows = {1: pl.ds(0, 2), -1: pl.ds(4, 2), 0: pl.ds(2, 2)}[dy]
    cells = {1: pl.ds(8, 8), -1: pl.ds(144, 8), 0: pl.ds(16, 128)}[dz]
    return rows, cells


def landed(ref, sem):
    pltpu.make_async_copy(ref, ref, sem).wait()


def kernel(
    scale,
    inflow_hbm,
    weights_hbm,
    biases,
    cotangent_hbm,
    out_act,
    out_grad,
    final,
    inflow,
    weights,
    cotangent,
    ext,
    inner,
    wide_lines,
    wide_rims,
    lines,
    slope_lines,
    slope_rims,
    wide_f,
    wide_b,
    packed,
    wide_pre,
    pre,
    flow,
    stage,
    midway,
    part,
    half_in,
    half_sum,
    one_in,
    one_sum,
    two_in,
    two_sum,
    three_in,
    load_sem,
    halo_send,
    halo_recv,
    source_send,
    relay_send,
    relay_recv,
    mate_send,
    mate_recv,
    out_send,
    out_recv,
    mid_send,
    mid_recv,
    pair_send,
    pair_recv,
    group_send,
    group_recv,
    deep_send,
    deep_recv,
):
    sec = lax.axis_index("section")
    gy = lax.axis_index("gy")
    gz = lax.axis_index("gz")
    core = gy % 2
    px = (gy // 2) % 4
    zlo = gy // 8
    depth = sec * 4 + zlo
    other = 1 - sec

    def at_depth(level, parity):
        return (level // 4, (level % 4) * 8 + px * 2 + parity, gz)

    def in_plane(first, index):
        on_x = (1 - core) if first else core
        new_gy = gy + on_x * 2 * (index - px)
        new_gz = gz + (1 - on_x) * (index - gz)
        return (sec, new_gy, new_gz)

    mate = (sec, gy + 1 - 2 * core, gz)
    first_plane = zlo == 0
    last_plane = zlo == 3
    at_end = jnp.logical_or(first_plane, last_plane)
    outward = at_depth((depth + jnp.where(last_plane, 1, 7)) % 8, core)
    inward = at_depth((depth + jnp.where(last_plane, 7, 1)) % 8, core)

    def exists(dy, dz):
        ok = None
        for index, delta, count in ((gy, dy, 32), (gz, dz, 4)):
            if delta == 0:
                continue
            good = index > 0 if delta < 0 else index < count - 1
            ok = good if ok is None else jnp.logical_and(ok, good)
        return ok

    lane = lax.broadcasted_iota(jnp.int32, (1, 128), 1)
    left = lane < 64

    def turned(value):
        return pltpu.roll(value, 64, 1)

    loads = [
        pltpu.make_async_copy(weights_hbm, weights, load_sem.at[0]),
        pltpu.make_async_copy(inflow_hbm.at[sec], inflow, load_sem.at[1]),
        pltpu.make_async_copy(cotangent_hbm.at[sec], cotangent, load_sem.at[2]),
    ]
    for load in loads:
        load.start()

    barrier = pltpu.get_barrier_semaphore()

    def greet(device):
        pl.semaphore_signal(barrier, inc=1, device_id=device, device_id_type=MESH)

    for d in range(1, 8):
        greet(at_depth((depth + d) % 8, core))
    for d in range(1, 4):
        greet((sec, gy + 2 * ((px + d) % 4 - px), gz))
        greet((sec, gy, (gz + d) % 4))
    for dy, dz in DIRS:
        if dy != 0:

            @pl.when(exists(dy, dz))
            def _():
                greet((sec, gy + dy, gz + dz))

    sides_y = 2 - jnp.where(gy == 0, 1, 0) - jnp.where(gy == 31, 1, 0)
    sides_z = 2 - jnp.where(gz == 0, 1, 0) - jnp.where(gz == 3, 1, 0)
    def clear(rows, cells):
        ext[:, rows, cells, :] = jnp.zeros((4, rows.size, cells.size, 128), F32)

    clear(pl.ds(0, 6), pl.ds(0, 8))
    clear(pl.ds(0, 6), pl.ds(152, 8))

    @pl.when(gy == 0)
    def _():
        clear(pl.ds(0, 2), pl.ds(8, 144))

    @pl.when(gy == 31)
    def _():
        clear(pl.ds(4, 2), pl.ds(8, 144))

    @pl.when(gz == 0)
    def _():
        clear(pl.ds(0, 6), pl.ds(8, 8))

    @pl.when(gz == 3)
    def _():
        clear(pl.ds(0, 6), pl.ds(144, 8))

    def turned_in(ref, y):
        rows = [ref[pl.ds(2 * x + y, 64, stride=4), :] for x in range(2)]
        return jnp.concatenate(rows, axis=0).T

    loads[1].wait()
    for y in range(2):
        ext[0, 2 + y, 16:144, :] = turned_in(inflow, y)
    loads[0].wait()
    for i in range(2):
        for b in range(3):
            for c in range(3):
                tap = b * 3 + c
                base = tap * TAP_ROWS
                middle = weights[i, 9 + tap]
                far = weights[i, 18 + tap]
                near = weights[i, tap]
                packed[2 * sec + i, base : base + 64, :] = jnp.concatenate([middle, far], axis=1)
                packed[2 * sec + i, base + 64 : base + 96, :] = jnp.concatenate(
                    [near[0:32], near[32:64]], axis=1
                )
        row = biases[i : i + 1, :]
        packed[2 * sec + i, 864:880, :] = jnp.broadcast_to(
            jnp.concatenate([row, row], axis=1), (16, 128)
        )

    pl.semaphore_wait(barrier, 13 + sides_y * (1 + sides_z))

    def send_rims(slot):
        for d, (dy, dz) in enumerate(DIRS):
            rows, cells = source_window(dy, dz)
            rows_to, cells_to = target_window(dy, dz)

            @pl.when(exists(dy, dz))
            def _():
                pltpu.make_async_remote_copy(
                    src_ref=ext.at[slot, rows, cells, :],
                    dst_ref=ext.at[slot, rows_to, cells_to, :],
                    send_sem=halo_send.at[slot, d],
                    recv_sem=halo_recv.at[slot, d],
                    device_id=(sec, gy + dy, gz + dz),
                    device_id_type=MESH,
                ).start()

    def await_rims(slot):
        for d, (dy, dz) in enumerate(DIRS):
            rows_to, cells_to = target_window(dy, dz)

            @pl.when(exists(-dy, -dz))
            def _():
                landed(ext.at[slot, rows_to, cells_to, :], halo_recv.at[slot, d])

    send_rims(0)

    def chunk_of(layer, parity, chunk):
        start = parity * (PACK // 2) + chunk * CHUNK
        return packed.at[layer, pl.ds(pl.multiple_of(start, 8), CHUNK), :]

    def pass_on(layer, i, chunk, send, recv, device):
        piece = chunk_of(layer, core, chunk)
        pltpu.make_async_remote_copy(
            src_ref=piece,
            dst_ref=piece,
            send_sem=send.at[i, chunk],
            recv_sem=recv.at[i, chunk],
            device_id=device,
            device_id_type=MESH,
        ).start()

    @pl.when(at_end)
    def _():
        for i in range(2):
            for chunk in range(CHUNKS):
                pass_on(2 * sec + i, i, chunk, source_send, relay_recv, outward)

    def widen(layer):
        for tap in range(TAPS):
            base = tap * TAP_ROWS
            top = packed[layer, base : base + 64, :]
            near = packed[layer, base + 64 : base + 96, :]
            bottom = jnp.where(
                left, jnp.concatenate([near, turned(near)], axis=0), turned(top)
            )
            high, low = split_parts(jnp.concatenate([top, bottom], axis=0))
            cols = slice(tap * 128, tap * 128 + 128)
            wide_f[layer, 0:128, cols] = high
            wide_f[layer, 128:256, cols] = low
            rows = slice((8 - tap) * 128, (8 - tap) * 128 + 128)
            wide_b[layer, rows, 0:128] = high
            wide_b[layer, rows, 128:256] = low

    def widen_own(i, carry):
        widen(2 * sec + i)
        return carry

    lax.fori_loop(0, 2, widen_own, 0)

    loads[2].wait()
    for y in range(2):
        flow[y * 128 : (y + 1) * 128, :] = turned_in(cotangent, y)
    for layer in range(LAYERS):
        part[layer, 864:GRAD, :] = jnp.zeros((GRAD - 864, 128), F32)

    def relay(i, chunks):
        for chunk in chunks:
            landed(chunk_of(2 * other + i, core, chunk), relay_recv.at[i, chunk])

            @pl.when(at_end)
            def _():
                pass_on(2 * other + i, i, chunk, relay_send, relay_recv, inward)

            pass_on(2 * other + i, i, chunk, mate_send, mate_recv, mate)

    def receive(i):
        for chunk in range(CHUNKS):
            landed(chunk_of(2 * other + i, 1 - core, chunk), mate_recv.at[i, chunk])
        widen(2 * other + i)

    relay(0, range(CHUNKS))
    receive(0)
    relay(1, range(EARLY))

    def reach(condition):
        return lane < jnp.where(condition, 128, 0)

    inside_low, inside_high = reach(gz > 0), reach(gz < 3)
    inside_line = [reach(gy > 0), None, None, reach(gy < 31)]

    def fill_wide(slot, line_ref, edge_ref):
        for c in range(3):
            for row in range(6):
                line = ext[slot, row, 15 + c : 143 + c, :]
                edge = jnp.concatenate(
                    [ext[slot, row, 7 + c : 15 + c, :], ext[slot, row, 143 + c : 151 + c, :]],
                    axis=0,
                )
                for at, value in enumerate(split_parts(line)):
                    line_ref[at, c, row * 128 : row * 128 + 128, :] = value
                for at, value in enumerate(split_parts(edge)):
                    edge_ref[at, c, row * 16 : row * 16 + 16, :] = value

    def fill_inner(line_ref):
        for c in range(3):
            for row in range(4):
                line = inner[row, 15 + c : 143 + c, :]
                for at, value in enumerate(split_parts(line)):
                    line_ref[at, c, row * 128 : row * 128 + 128, :] = value

    def taps_of(ref, at, size, first, count):
        return jnp.concatenate(
            [
                ref[at, c, (first + b) * size : (first + b + count) * size, :]
                for b in range(3)
                for c in range(3)
            ],
            axis=1,
        )

    def wide_taps(line_ref, edge_ref):
        blocks = []
        for at in range(2):
            blocks.append(taps_of(line_ref, at, 128, 0, 4))
            blocks.append(taps_of(edge_ref, at, 16, 0, 4))
        return jnp.concatenate(blocks, axis=0)

    def inner_taps(line_ref):
        return jnp.concatenate([taps_of(line_ref, at, 128, 0, 2) for at in range(2)], axis=0)

    def keep_inner(value):
        for y in range(4):
            line = value[y * 128 : (y + 1) * 128, :]
            low = value[512 + y * 16 : 520 + y * 16, :]
            high = value[520 + y * 16 : 528 + y * 16, :]
            low = jnp.where(inside_low, low, 0.0)
            high = jnp.where(inside_high, high, 0.0)
            if inside_line[y] is not None:
                line, low, high = (jnp.where(inside_line[y], v, 0.0) for v in (line, low, high))
            inner[y, 16:144, :] = line
            inner[y, 8:16, :] = low
            inner[y, 144:152, :] = high

    def settle(value, keeper, kind, result):
        def put(ref, lead):
            for y in range(2):
                block = value[y * 128 : (y + 1) * 128, :].T
                for x in range(2):
                    where = pl.ds(2 * x + y, 64, stride=4)
                    ref[lead, where, :] = block[x * 64 : (x + 1) * 64, :]

        @pl.when(sec == keeper)
        def _():
            put(result, sec)

        @pl.when(sec != keeper)
        def _():
            put(stage, kind)

    two_on = at_depth((depth + 2 + 4 * core) % 8, core)
    origin = ((depth + 6 - 4 * core) % 8) // 4

    def hand_on(kind):
        pltpu.make_async_remote_copy(
            src_ref=stage.at[kind],
            dst_ref=midway.at[kind],
            send_sem=out_send.at[kind],
            recv_sem=mid_recv.at[kind],
            device_id=two_on,
            device_id_type=MESH,
        ).start()

    def hand_over(kind, result):
        landed(midway.at[kind], mid_recv.at[kind])
        pltpu.make_async_remote_copy(
            src_ref=midway.at[kind],
            dst_ref=result.at[origin],
            send_sem=mid_send.at[kind],
            recv_sem=out_recv.at[kind],
            device_id=two_on,
            device_id_type=MESH,
        ).start()

    def joined(product):
        cells = product.shape[0] // 2
        return (product[:cells, 0:128] + product[:cells, 128:256]) + (
            product[cells:, 0:128] + product[cells:, 128:256]
        )

    def across(patches, layer):
        product = lax.dot_general(
            patches, wide_f[layer], (((1,), (1,)), ((), ())), preferred_element_type=F32
        )
        return joined(product) + packed[layer, 864:865, :]

    def back_across(patches, layer):
        return joined(jnp.dot(patches, wide_b[layer], preferred_element_type=F32))

    def active(value):
        return value * (1.0 / (1.0 + jnp.exp(-value)))

    def slope_of(gradient, value):
        sigma = 1.0 / (1.0 + jnp.exp(-value))
        return gradient * sigma * (1.0 + value * (1.0 - sigma))

    def keep_own(slot, value):
        for y in range(2):
            ext[slot, 2 + y, 16:144, :] = value[y * 128 : (y + 1) * 128, :]

    def forward(pair, carry):
        first = 2 * pair
        await_rims(pair)

        fill_wide(pair, wide_lines.at[pair], wide_rims.at[pair])
        value = across(wide_taps(wide_lines.at[pair], wide_rims.at[pair]), first)
        wide_pre[pair] = value
        keep_inner(active(value))

        @pl.when(pair == 0)
        def _():
            relay(1, range(EARLY, CHUNKS))
            receive(1)

        fill_inner(lines.at[pair])
        value = across(inner_taps(lines.at[pair]), first + 1)
        pre[pair] = value
        result = active(value)

        @pl.when(pair == 0)
        def _():
            keep_own(1, result)
            send_rims(1)
            settle(result, 0, 0, out_act)

        @pl.when(pair == 1)
        def _():
            settle(result, 1, 0, out_act)

        return carry

    lax.fori_loop(0, 2, forward, 0)

    index_one = px + core * (gz - px)
    index_two = gz + core * (px - gz)
    offset_half = core * 512
    offset_one = offset_half + index_one * 128
    offset_two = offset_one + index_two * 32

    def rows_at(ref, layer, start, size):
        return ref.at[layer, pl.ds(pl.multiple_of(start, 8), size), :]

    def push(source, target, send, recv, device):
        pltpu.make_async_remote_copy(
            src_ref=source,
            dst_ref=target,
            send_sem=send,
            recv_sem=recv,
            device_id=device,
            device_id_type=MESH,
        ).start()

    def reduce_start(layer):
        push(
            rows_at(part, layer, (1 - core) * 512, 512),
            half_in.at[layer],
            pair_send.at[0, layer],
            pair_recv.at[0, layer],
            mate,
        )

    def reduce_half(layer):
        landed(half_in.at[layer], pair_recv.at[0, layer])
        half_sum[layer] = (
            part[layer, pl.ds(pl.multiple_of(offset_half, 8), 512), :] + half_in[layer]
        )
        for d in range(1, 4):
            peer = (index_one + d) % 4
            push(
                rows_at(half_sum, layer, peer * 128, 128),
                one_in.at[layer, 3 - d],
                group_send.at[0, layer, 3 - d],
                group_recv.at[0, layer, 3 - d],
                in_plane(True, peer),
            )

    def reduce_one(layer):
        for s in range(3):
            landed(one_in.at[layer, s], group_recv.at[0, layer, s])
        own = half_sum[layer, pl.ds(pl.multiple_of(index_one * 128, 8), 128), :]
        one_sum[layer] = (own + one_in[layer, 0]) + (one_in[layer, 1] + one_in[layer, 2])
        for d in range(1, 4):
            peer = (index_two + d) % 4
            push(
                rows_at(one_sum, layer, peer * 32, 32),
                two_in.at[layer, 3 - d],
                group_send.at[1, layer, 3 - d],
                group_recv.at[1, layer, 3 - d],
                in_plane(False, peer),
            )

    def reduce_two(layer):
        for s in range(3):
            landed(two_in.at[layer, s], group_recv.at[1, layer, s])
        own = one_sum[layer, pl.ds(pl.multiple_of(index_two * 32, 8), 32), :]
        two_sum[layer] = (own + two_in[layer, 0]) + (two_in[layer, 1] + two_in[layer, 2])
        for d in range(1, 8):
            peer = (depth + d) % 8

            @pl.when(peer // 4 == layer // 2)
            def _():
                push(
                    two_sum.at[layer],
                    three_in.at[layer, depth],
                    deep_send.at[layer, d - 1],
                    deep_recv.at[layer, d - 1],
                    at_depth(peer, core),
                )

    def gathered(layer, stage_at, base, index, size):
        for s in range(3):
            sender = (index + 1 + s) % 4
            piece = rows_at(final, layer % 2, base + sender * size, size)
            landed(piece, group_recv.at[stage_at, layer, s])

    def gather_two(layer):
        for d in range(1, 8):
            landed(three_in.at[layer, (depth + 8 - d) % 8], deep_recv.at[layer, d - 1])
        three_in[layer, depth] = two_sum[layer]
        total = three_in[layer, 0]
        for level in range(1, 8):
            total = total + three_in[layer, level]
        final[layer % 2, pl.ds(pl.multiple_of(offset_two, 8), 32), :] = total * scale
        for d in range(1, 4):
            piece = rows_at(final, layer % 2, offset_two, 32)
            push(
                piece,
                piece,
                group_send.at[2, layer, 3 - d],
                group_recv.at[2, layer, 3 - d],
                in_plane(False, (index_two + d) % 4),
            )

    def gather_one(layer):
        gathered(layer, 2, offset_one, index_two, 32)
        for d in range(1, 4):
            piece = rows_at(final, layer % 2, offset_one, 128)
            push(
                piece,
                piece,
                group_send.at[3, layer, 3 - d],
                group_recv.at[3, layer, 3 - d],
                in_plane(True, (index_one + d) % 4),
            )

    def gather_half(layer):
        gathered(layer, 3, offset_half, index_one, 128)
        piece = rows_at(final, layer % 2, offset_half, 512)
        push(piece, piece, pair_send.at[1, layer], pair_recv.at[1, layer], mate)

    def finish(layer):
        piece = rows_at(final, layer % 2, (1 - core) * 512, 512)
        landed(piece, pair_recv.at[1, layer])

    everywhere = [reduce_half, reduce_one, reduce_two]
    at_home = [gather_two, gather_one, gather_half, finish]

    def weigh(layer, slope, high_patch, low_patch):
        turned_slope = jnp.concatenate([slope[0:128, :].T, slope[128:256, :].T], axis=1)
        sides = jnp.concatenate(split_parts(turned_slope), axis=0)
        product = jnp.dot(sides, high_patch, preferred_element_type=F32) + jnp.dot(
            sides, low_patch, preferred_element_type=F32
        )
        for tap in range(TAPS):
            cols = slice(tap * 128, tap * 128 + 128)
            block = product[0:128, cols] + product[128:256, cols]
            base = tap * TAP_ROWS
            flipped = turned(block[64:128, :])
            part[layer, base : base + 64, :] = block[0:64, :] + jnp.where(left, flipped, 0.0)
            part[layer, base + 64 : base + 96, :] = jnp.where(
                left, block[64:96, :], flipped[32:64, :]
            )
        sums = jnp.sum(slope, axis=0, keepdims=True)
        part[layer, 864:865, :] = sums + turned(sums)
        reduce_start(layer)

    def backward(step, carry):
        pair = 1 - step
        first = 2 * pair
        slot = 2 + step
        slope = slope_of(flow[...], pre[pair])
        keep_own(slot, slope)
        send_rims(slot)
        weigh(first + 1, slope, *[taps_of(lines.at[pair], at, 128, 0, 2) for at in range(2)])

        @pl.when(pair == 0)
        def _():
            reduce_half(2)
            reduce_one(3)

        await_rims(slot)

        @pl.when(pair == 1)
        def _():
            hand_on(0)

        @pl.when(pair == 0)
        def _():
            hand_over(0, out_act)
            reduce_half(1)
            reduce_one(2)
            reduce_two(3)

        fill_wide(slot, slope_lines, slope_rims)
        gradient = back_across(wide_taps(slope_lines, slope_rims), first + 1)
        slope = slope_of(gradient, wide_pre[pair])
        keep_inner(slope)
        weigh(
            first,
            slope[128:384, :],
            *[taps_of(wide_lines.at[pair], at, 128, 1, 2) for at in range(2)],
        )

        @pl.when(pair == 1)
        def _():
            reduce_half(3)

        @pl.when(pair == 0)
        def _():
            reduce_one(1)
            reduce_two(2)

        fill_inner(slope_lines)
        gradient = back_across(inner_taps(slope_lines), first)
        flow[...] = gradient

        @pl.when(pair == 1)
        def _():
            settle(gradient, 1, 1, out_grad)

        @pl.when(pair == 0)
        def _():
            settle(gradient, 0, 1, out_grad)

        return carry

    lax.fori_loop(0, 2, backward, 0)

    hand_on(1)
    for round_at in range(7):
        for layer, tick, ready in ((0, round_at, 0), (1, round_at + 2, 0), (2, round_at, 3), (3, round_at, 3)):
            if round_at < ready:
                continue
            if tick < 3:
                everywhere[tick](layer)
            elif tick < 7:

                @pl.when(sec == layer // 2)
                def _():
                    at_home[tick - 3](layer)

        if round_at == 2:
            hand_over(1, out_grad)

    landed(out_act.at[1 - sec], out_recv.at[0])
    landed(out_grad.at[1 - sec], out_recv.at[1])

    def drain_rims(slot, carry):
        for d, (dy, dz) in enumerate(DIRS):
            rows, cells = source_window(dy, dz)

            @pl.when(exists(dy, dz))
            def _():
                landed(ext.at[slot, rows, cells, :], halo_send.at[slot, d])

        return carry

    lax.fori_loop(0, 4, drain_rims, 0)
    for i in range(2):
        for chunk in range(CHUNKS):

            @pl.when(at_end)
            def _():
                landed(chunk_of(2 * sec + i, core, chunk), source_send.at[i, chunk])

            @pl.when(at_end)
            def _():
                landed(chunk_of(2 * other + i, core, chunk), relay_send.at[i, chunk])

            landed(chunk_of(2 * other + i, core, chunk), mate_send.at[i, chunk])
    for kind in range(2):
        landed(stage.at[kind], out_send.at[kind])
        landed(midway.at[kind], mid_send.at[kind])

    def drain_sums(layer, carry):
        home = sec == layer // 2
        landed(half_in.at[layer], pair_send.at[0, layer])
        for s in range(3):
            landed(one_in.at[layer, s], group_send.at[0, layer, s])
            landed(two_in.at[layer, s], group_send.at[1, layer, s])
        for d in range(1, 8):

            @pl.when(((depth + d) % 8) // 4 == layer // 2)
            def _():
                landed(two_sum.at[layer], deep_send.at[layer, d - 1])

        @pl.when(home)
        def _():
            for s in range(3):
                landed(two_in.at[layer, s], group_send.at[2, layer, s])
                landed(one_in.at[layer, s], group_send.at[3, layer, s])
            landed(half_in.at[layer], pair_send.at[1, layer])

        return carry

    lax.fori_loop(0, LAYERS, drain_sums, 0)


def unpack(act, grad, total, out_act, out_grad, out_weight, out_bias, spread, sem):
    copies = [
        pltpu.make_async_copy(act, out_act, sem.at[0]),
        pltpu.make_async_copy(grad, out_grad, sem.at[1]),
    ]
    for copy in copies:
        copy.start()
    for i in range(2):
        for tap in range(TAPS):
            base = tap * TAP_ROWS
            top = total[i, base : base + 64, :]
            near = total[i, base + 64 : base + 96, :]
            spread[i, 9 + tap] = top[:, 0:64]
            spread[i, 18 + tap] = pltpu.roll(top, 64, 1)[:, 0:64]
            spread[i, tap, 0:32, :] = near[:, 0:64]
            spread[i, tap, 32:64, :] = pltpu.roll(near, 64, 1)[:, 0:64]
        copies.append(pltpu.make_async_copy(spread.at[i], out_weight.at[i], sem.at[2 + i]))
        copies[-1].start()
    out_bias[...] = total[:, 864, 0:64]
    for copy in copies:
        copy.wait()


def per_device(inflow, weights, biases, cotangent):
    micro, channels, nx, ny, nz = inflow.shape
    cells = micro * nx * ny * lax.axis_size("gy") * nz * lax.axis_size("gz")
    scale = 1.0 / math.sqrt(cells)
    rows = channels * nx * ny
    vmem = pltpu.VMEM
    dma = pltpu.SemaphoreType.DMA
    scratch = [
        vmem((rows, nz), F32),
        vmem(weights.shape, F32),
        vmem((rows, nz), F32),
        vmem((4, 6, 160, 128), F32),
        vmem((4, 160, 128), F32),
        vmem((2, 2, 3, 768, 128), BF16),
        vmem((2, 2, 3, 96, 128), BF16),
        vmem((2, 2, 3, 512, 128), BF16),
        vmem((2, 3, 768, 128), BF16),
        vmem((2, 3, 96, 128), BF16),
        vmem((LAYERS, 256, TAPS * 128), BF16),
        vmem((LAYERS, TAPS * 128, 256), BF16),
        vmem((LAYERS, PACK, 128), F32),
        vmem((2, WIDE, 128), F32),
        vmem((2, 256, 128), F32),
        vmem((256, 128), F32),
        vmem((2, 256, 128), F32),
        vmem((2, 256, 128), F32),
        vmem((LAYERS, GRAD, 128), F32),
        vmem((LAYERS, 512, 128), F32),
        vmem((LAYERS, 512, 128), F32),
        vmem((LAYERS, 3, 128, 128), F32),
        vmem((LAYERS, 128, 128), F32),
        vmem((LAYERS, 3, 32, 128), F32),
        vmem((LAYERS, 32, 128), F32),
        vmem((LAYERS, 8, 32, 128), F32),
        dma((3,)),
        dma((4, 8)),
        dma((4, 8)),
        dma((2, CHUNKS)),
        dma((2, CHUNKS)),
        dma((2, CHUNKS)),
        dma((2, CHUNKS)),
        dma((2, CHUNKS)),
        dma((2,)),
        dma((2,)),
        dma((2,)),
        dma((2,)),
        dma((2, LAYERS)),
        dma((2, LAYERS)),
        dma((4, LAYERS, 3)),
        dma((4, LAYERS, 3)),
        dma((LAYERS, 7)),
        dma((LAYERS, 7)),
    ]
    near = pl.BlockSpec(memory_space=pltpu.VMEM)
    far = pl.BlockSpec(memory_space=pl.ANY)

    def body(*refs):
        kernel(scale, *refs)

    act, grad, total = pl.pallas_call(
        body,
        name="encoder_sections",
        out_shape=(
            vmem((micro, rows, nz), F32),
            vmem((micro, rows, nz), F32),
            vmem((2, GRAD, 128), F32),
        ),
        in_specs=[far, far, near, far],
        out_specs=(near,) * 3,
        scratch_shapes=scratch,
        compiler_params=pltpu.CompilerParams(
            collective_id=0, has_side_effects=True, vmem_limit_bytes=56 << 20
        ),
    )(
        inflow.reshape(micro, rows, nz),
        weights,
        biases,
        cotangent.reshape(micro, rows, nz),
    )
    act, grad, weight, bias = pl.pallas_call(
        unpack,
        name="write_results",
        out_shape=(
            jax.ShapeDtypeStruct(act.shape, F32),
            jax.ShapeDtypeStruct(grad.shape, F32),
            jax.ShapeDtypeStruct(weights.shape, F32),
            jax.ShapeDtypeStruct(biases.shape, F32),
        ),
        in_specs=[near] * 3,
        out_specs=(far, far, far, near),
        scratch_shapes=[vmem(weights.shape, F32), dma((4,))],
        compiler_params=pltpu.CompilerParams(vmem_limit_bytes=8 << 20),
    )(act, grad, total)
    shape = (1, micro, channels, nx, ny, nz)
    return act.reshape(shape), grad.reshape(shape), weight, bias


def solution(mesh):
    return jax.shard_map(
        per_device,
        mesh=mesh,
        in_specs=(
            P(None, None, None, "gy", "gz"),
            P("section", None, None, None),
            P("section", None),
            P(None, None, None, "gy", "gz"),
        ),
        out_specs=(
            P("section", None, None, None, "gy", "gz"),
            P("section", None, None, None, "gy", "gz"),
            P("section", None, None, None),
            P("section", None),
        ),
        check_vma=False,
    )
```

```python
import math

import jax
import jax.numpy as jnp
from jax import lax
from jax.experimental import pallas as pl
from jax.experimental.pallas import tpu as pltpu
from jax.sharding import PartitionSpec as P

MESH = pl.DeviceIdType.MESH
F32 = jnp.float32
BF16 = jnp.bfloat16
LAYERS = 4
TAPS = 9
DIRS = [(dy, dz) for dy in (-1, 0, 1) for dz in (-1, 0, 1) if (dy, dz) != (0, 0)]
TAP_ROWS = 96
PACK = 880
CHUNKS = 5
CHUNK = PACK // 2 // CHUNKS
EARLY = 3
GRAD = 512
FRONT = 5
WIDE = 576


def split_parts(value):
    high = value.astype(BF16)
    return high, (value - high.astype(F32)).astype(BF16)


def source_window(dy, dz):
    cells = {1: pl.ds(136, 8), -1: pl.ds(16, 8), 0: pl.ds(16, 128)}[dz]
    return pl.ds(2, 2), cells


def target_window(dy, dz):
    rows = {1: pl.ds(0, 2), -1: pl.ds(4, 2), 0: pl.ds(2, 2)}[dy]
    cells = {1: pl.ds(8, 8), -1: pl.ds(144, 8), 0: pl.ds(16, 128)}[dz]
    return rows, cells


def landed(ref, sem):
    pltpu.make_async_copy(ref, ref, sem).wait()


def kernel(
    scale,
    inflow_hbm,
    weights_hbm,
    biases,
    cotangent_hbm,
    out_act,
    out_grad,
    final,
    inflow,
    weights,
    cotangent,
    ext,
    inner,
    wide_lines,
    wide_rims,
    lines,
    slope_lines,
    slope_rims,
    wide_f,
    wide_b,
    packed,
    wide_pre,
    pre,
    flow,
    stage,
    midway,
    part,
    half_in,
    half_sum,
    one_in,
    one_sum,
    two_in,
    two_sum,
    three_in,
    load_sem,
    halo_send,
    halo_recv,
    source_send,
    relay_send,
    relay_recv,
    mate_send,
    mate_recv,
    out_send,
    out_recv,
    mid_send,
    mid_recv,
    pair_send,
    pair_recv,
    group_send,
    group_recv,
    deep_send,
    deep_recv,
):
    sec = lax.axis_index("section")
    gy = lax.axis_index("gy")
    gz = lax.axis_index("gz")
    core = gy % 2
    px = (gy // 2) % 4
    zlo = gy // 8
    depth = sec * 4 + zlo
    other = 1 - sec

    def at_depth(level, parity):
        return (level // 4, (level % 4) * 8 + px * 2 + parity, gz)

    def in_plane(first, index):
        on_x = (1 - core) if first else core
        new_gy = gy + on_x * 2 * (index - px)
        new_gz = gz + (1 - on_x) * (index - gz)
        return (sec, new_gy, new_gz)

    mate = (sec, gy + 1 - 2 * core, gz)
    first_plane = zlo == 0
    last_plane = zlo == 3
    at_end = jnp.logical_or(first_plane, last_plane)
    outward = at_depth((depth + jnp.where(last_plane, 1, 7)) % 8, core)
    inward = at_depth((depth + jnp.where(last_plane, 7, 1)) % 8, core)

    def exists(dy, dz):
        ok = None
        for index, delta, count in ((gy, dy, 32), (gz, dz, 4)):
            if delta == 0:
                continue
            good = index > 0 if delta < 0 else index < count - 1
            ok = good if ok is None else jnp.logical_and(ok, good)
        return ok

    lane = lax.broadcasted_iota(jnp.int32, (1, 128), 1)
    left = lane < 64

    def turned(value):
        return pltpu.roll(value, 64, 1)

    loads = [
        pltpu.make_async_copy(weights_hbm, weights, load_sem.at[0]),
        pltpu.make_async_copy(inflow_hbm.at[sec], inflow, load_sem.at[1]),
        pltpu.make_async_copy(cotangent_hbm.at[sec], cotangent, load_sem.at[2]),
    ]
    for load in loads:
        load.start()

    barrier = pltpu.get_barrier_semaphore()

    def greet(device):
        pl.semaphore_signal(barrier, inc=1, device_id=device, device_id_type=MESH)

    for d in range(1, 8):
        greet(at_depth((depth + d) % 8, core))
    for d in range(1, 4):
        greet((sec, gy + 2 * ((px + d) % 4 - px), gz))
        greet((sec, gy, (gz + d) % 4))
    for dy, dz in DIRS:
        if dy != 0:

            @pl.when(exists(dy, dz))
            def _():
                greet((sec, gy + dy, gz + dz))

    sides_y = 2 - jnp.where(gy == 0, 1, 0) - jnp.where(gy == 31, 1, 0)
    sides_z = 2 - jnp.where(gz == 0, 1, 0) - jnp.where(gz == 3, 1, 0)
    def clear(rows, cells):
        ext[:, rows, cells, :] = jnp.zeros((4, rows.size, cells.size, 128), F32)

    clear(pl.ds(0, 6), pl.ds(0, 8))
    clear(pl.ds(0, 6), pl.ds(152, 8))

    @pl.when(gy == 0)
    def _():
        clear(pl.ds(0, 2), pl.ds(8, 144))

    @pl.when(gy == 31)
    def _():
        clear(pl.ds(4, 2), pl.ds(8, 144))

    @pl.when(gz == 0)
    def _():
        clear(pl.ds(0, 6), pl.ds(8, 8))

    @pl.when(gz == 3)
    def _():
        clear(pl.ds(0, 6), pl.ds(144, 8))

    def turned_in(ref, y):
        rows = [ref[pl.ds(2 * x + y, 64, stride=4), :] for x in range(2)]
        return jnp.concatenate(rows, axis=0).T

    loads[1].wait()
    for y in range(2):
        ext[0, 2 + y, 16:144, :] = turned_in(inflow, y)
    loads[0].wait()
    for i in range(2):
        for b in range(3):
            for c in range(3):
                tap = b * 3 + c
                base = tap * TAP_ROWS
                middle = weights[i, 9 + tap]
                far = weights[i, 18 + tap]
                near = weights[i, tap]
                packed[2 * sec + i, base : base + 64, :] = jnp.concatenate([middle, far], axis=1)
                packed[2 * sec + i, base + 64 : base + 96, :] = jnp.concatenate(
                    [near[0:32], near[32:64]], axis=1
                )
        row = biases[i : i + 1, :]
        packed[2 * sec + i, 864:880, :] = jnp.broadcast_to(
            jnp.concatenate([row, row], axis=1), (16, 128)
        )

    pl.semaphore_wait(barrier, 13 + sides_y * (1 + sides_z))

    def send_rims(slot):
        for d, (dy, dz) in enumerate(DIRS):
            rows, cells = source_window(dy, dz)
            rows_to, cells_to = target_window(dy, dz)

            @pl.when(exists(dy, dz))
            def _():
                pltpu.make_async_remote_copy(
                    src_ref=ext.at[slot, rows, cells, :],
                    dst_ref=ext.at[slot, rows_to, cells_to, :],
                    send_sem=halo_send.at[slot, d],
                    recv_sem=halo_recv.at[slot, d],
                    device_id=(sec, gy + dy, gz + dz),
                    device_id_type=MESH,
                ).start()

    def await_rims(slot):
        for d, (dy, dz) in enumerate(DIRS):
            rows_to, cells_to = target_window(dy, dz)

            @pl.when(exists(-dy, -dz))
            def _():
                landed(ext.at[slot, rows_to, cells_to, :], halo_recv.at[slot, d])

    send_rims(0)

    def chunk_of(layer, parity, chunk):
        start = parity * (PACK // 2) + chunk * CHUNK
        return packed.at[layer, pl.ds(pl.multiple_of(start, 8), CHUNK), :]

    def pass_on(layer, i, chunk, send, recv, device):
        piece = chunk_of(layer, core, chunk)
        pltpu.make_async_remote_copy(
            src_ref=piece,
            dst_ref=piece,
            send_sem=send.at[i, chunk],
            recv_sem=recv.at[i, chunk],
            device_id=device,
            device_id_type=MESH,
        ).start()

    @pl.when(at_end)
    def _():
        for i in range(2):
            for chunk in range(CHUNKS):
                pass_on(2 * sec + i, i, chunk, source_send, relay_recv, outward)

    def widen(layer):
        for tap in range(TAPS):
            base = tap * TAP_ROWS
            top = packed[layer, base : base + 64, :]
            near = packed[layer, base + 64 : base + 96, :]
            bottom = jnp.where(
                left, jnp.concatenate([near, turned(near)], axis=0), turned(top)
            )
            high, low = split_parts(jnp.concatenate([top, bottom], axis=0))
            cols = slice(tap * 128, tap * 128 + 128)
            wide_f[layer, 0:128, cols] = high
            wide_f[layer, 128:256, cols] = low
            rows = slice((8 - tap) * 128, (8 - tap) * 128 + 128)
            wide_b[layer, rows, 0:128] = high
            wide_b[layer, rows, 128:256] = low

    def widen_own(i, carry):
        widen(2 * sec + i)
        return carry

    lax.fori_loop(0, 2, widen_own, 0)

    loads[2].wait()
    for y in range(2):
        flow[y * 128 : (y + 1) * 128, :] = turned_in(cotangent, y)
    for layer in range(LAYERS):
        for half, used in ((0, FRONT * TAP_ROWS), (1, (TAPS - FRONT) * TAP_ROWS)):
            part[2 * layer + half, used:GRAD, :] = jnp.zeros((GRAD - used, 128), F32)

    def relay(i, chunks):
        for chunk in chunks:
            landed(chunk_of(2 * other + i, core, chunk), relay_recv.at[i, chunk])

            @pl.when(at_end)
            def _():
                pass_on(2 * other + i, i, chunk, relay_send, relay_recv, inward)

            pass_on(2 * other + i, i, chunk, mate_send, mate_recv, mate)

    def receive(i):
        for chunk in range(CHUNKS):
            landed(chunk_of(2 * other + i, 1 - core, chunk), mate_recv.at[i, chunk])
        widen(2 * other + i)

    relay(0, range(CHUNKS))
    receive(0)
    relay(1, range(EARLY))

    def reach(condition):
        return lane < jnp.where(condition, 128, 0)

    inside_low, inside_high = reach(gz > 0), reach(gz < 3)
    inside_line = [reach(gy > 0), None, None, reach(gy < 31)]

    def fill_wide(slot, line_ref, edge_ref):
        for c in range(3):
            for row in range(6):
                line = ext[slot, row, 15 + c : 143 + c, :]
                edge = jnp.concatenate(
                    [ext[slot, row, 7 + c : 15 + c, :], ext[slot, row, 143 + c : 151 + c, :]],
                    axis=0,
                )
                for at, value in enumerate(split_parts(line)):
                    line_ref[at, c, row * 128 : row * 128 + 128, :] = value
                for at, value in enumerate(split_parts(edge)):
                    edge_ref[at, c, row * 16 : row * 16 + 16, :] = value

    def fill_inner(line_ref):
        for c in range(3):
            for row in range(4):
                line = inner[row, 15 + c : 143 + c, :]
                for at, value in enumerate(split_parts(line)):
                    line_ref[at, c, row * 128 : row * 128 + 128, :] = value

    def taps_of(ref, at, size, first, count):
        return jnp.concatenate(
            [
                ref[at, c, (first + b) * size : (first + b + count) * size, :]
                for b in range(3)
                for c in range(3)
            ],
            axis=1,
        )

    def wide_taps(line_ref, edge_ref):
        return [
            jnp.concatenate(
                [taps_of(line_ref, at, 128, 0, 4), taps_of(edge_ref, at, 16, 0, 4)], axis=0
            )
            for at in range(2)
        ]

    def inner_taps(line_ref):
        return [taps_of(line_ref, at, 128, 0, 2) for at in range(2)]

    def keep_inner(value):
        for y in range(4):
            line = value[y * 128 : (y + 1) * 128, :]
            low = value[512 + y * 16 : 520 + y * 16, :]
            high = value[520 + y * 16 : 528 + y * 16, :]
            low = jnp.where(inside_low, low, 0.0)
            high = jnp.where(inside_high, high, 0.0)
            if inside_line[y] is not None:
                line, low, high = (jnp.where(inside_line[y], v, 0.0) for v in (line, low, high))
            inner[y, 16:144, :] = line
            inner[y, 8:16, :] = low
            inner[y, 144:152, :] = high

    def settle(value, keeper, kind, result):
        def put(ref, lead):
            for y in range(2):
                block = value[y * 128 : (y + 1) * 128, :].T
                for x in range(2):
                    where = pl.ds(2 * x + y, 64, stride=4)
                    ref[lead, where, :] = block[x * 64 : (x + 1) * 64, :]

        @pl.when(sec == keeper)
        def _():
            put(result, sec)

        @pl.when(sec != keeper)
        def _():
            put(stage, kind)

    two_on = at_depth((depth + 2 + 4 * core) % 8, core)
    origin = ((depth + 6 - 4 * core) % 8) // 4

    def hand_on(kind):
        pltpu.make_async_remote_copy(
            src_ref=stage.at[kind],
            dst_ref=midway.at[kind],
            send_sem=out_send.at[kind],
            recv_sem=mid_recv.at[kind],
            device_id=two_on,
            device_id_type=MESH,
        ).start()

    def hand_over(kind, result):
        landed(midway.at[kind], mid_recv.at[kind])
        pltpu.make_async_remote_copy(
            src_ref=midway.at[kind],
            dst_ref=result.at[origin],
            send_sem=mid_send.at[kind],
            recv_sem=out_recv.at[kind],
            device_id=two_on,
            device_id_type=MESH,
        ).start()

    def joined(parts, columns, dims):
        high, low = parts
        both = lax.dot_general(high, columns(256), dims, preferred_element_type=F32)
        rest = lax.dot_general(low, columns(128), dims, preferred_element_type=F32)
        return both[:, 0:128] + (both[:, 128:256] + rest)

    def across(parts, layer):
        def columns(count):
            return wide_f[layer, 0:count, :]

        return joined(parts, columns, (((1,), (1,)), ((), ()))) + packed[layer, 864:865, :]

    def back_across(parts, layer):
        def columns(count):
            return wide_b[layer, :, 0:count]

        return joined(parts, columns, (((1,), (0,)), ((), ())))

    def active(value):
        return value * (1.0 / (1.0 + jnp.exp(-value)))

    def slope_of(gradient, value):
        sigma = 1.0 / (1.0 + jnp.exp(-value))
        return gradient * sigma * (1.0 + value * (1.0 - sigma))

    def keep_own(slot, value):
        for y in range(2):
            ext[slot, 2 + y, 16:144, :] = value[y * 128 : (y + 1) * 128, :]

    def forward(pair, carry):
        first = 2 * pair
        await_rims(pair)

        fill_wide(pair, wide_lines.at[pair], wide_rims.at[pair])
        value = across(wide_taps(wide_lines.at[pair], wide_rims.at[pair]), first)
        wide_pre[pair] = value
        keep_inner(active(value))

        @pl.when(pair == 0)
        def _():
            relay(1, range(EARLY, CHUNKS))
            receive(1)

        fill_inner(lines.at[pair])
        value = across(inner_taps(lines.at[pair]), first + 1)
        pre[pair] = value
        result = active(value)

        @pl.when(pair == 0)
        def _():
            keep_own(1, result)
            send_rims(1)
            settle(result, 0, 0, out_act)

        @pl.when(pair == 1)
        def _():
            settle(result, 1, 0, out_act)

        return carry

    lax.fori_loop(0, 2, forward, 0)

    index_one = px + core * (gz - px)
    index_two = gz + core * (px - gz)
    offset_half = core * 256
    offset_one = offset_half + index_one * 64
    offset_two = offset_one + index_two * 16

    def rows_at(ref, layer, start, size):
        return ref.at[layer, pl.ds(pl.multiple_of(start, 8), size), :]

    def push(source, target, send, recv, device):
        pltpu.make_async_remote_copy(
            src_ref=source,
            dst_ref=target,
            send_sem=send,
            recv_sem=recv,
            device_id=device,
            device_id_type=MESH,
        ).start()

    def reduce_start(layer):
        push(
            rows_at(part, layer, (1 - core) * 256, 256),
            half_in.at[layer],
            pair_send.at[0, layer],
            pair_recv.at[0, layer],
            mate,
        )

    def reduce_half(layer):
        landed(half_in.at[layer], pair_recv.at[0, layer])
        half_sum[layer] = (
            part[layer, pl.ds(pl.multiple_of(offset_half, 8), 256), :] + half_in[layer]
        )
        for d in range(1, 4):
            peer = (index_one + d) % 4
            push(
                rows_at(half_sum, layer, peer * 64, 64),
                one_in.at[layer, 3 - d],
                group_send.at[0, layer, 3 - d],
                group_recv.at[0, layer, 3 - d],
                in_plane(True, peer),
            )

    def reduce_one(layer):
        for s in range(3):
            landed(one_in.at[layer, s], group_recv.at[0, layer, s])
        own = half_sum[layer, pl.ds(pl.multiple_of(index_one * 64, 8), 64), :]
        one_sum[layer] = (own + one_in[layer, 0]) + (one_in[layer, 1] + one_in[layer, 2])
        for d in range(1, 4):
            peer = (index_two + d) % 4
            push(
                rows_at(one_sum, layer, peer * 16, 16),
                two_in.at[layer, 3 - d],
                group_send.at[1, layer, 3 - d],
                group_recv.at[1, layer, 3 - d],
                in_plane(False, peer),
            )

    def reduce_two(layer):
        for s in range(3):
            landed(two_in.at[layer, s], group_recv.at[1, layer, s])
        own = one_sum[layer, pl.ds(pl.multiple_of(index_two * 16, 8), 16), :]
        two_sum[layer] = (own + two_in[layer, 0]) + (two_in[layer, 1] + two_in[layer, 2])
        for d in range(1, 8):
            peer = (depth + d) % 8

            @pl.when(peer // 4 == layer // 4)
            def _():
                push(
                    two_sum.at[layer],
                    three_in.at[layer, depth],
                    deep_send.at[layer, d - 1],
                    deep_recv.at[layer, d - 1],
                    at_depth(peer, core),
                )

    def gathered(layer, stage_at, base, index, size):
        for s in range(3):
            sender = (index + 1 + s) % 4
            piece = rows_at(final, layer % 4, base + sender * size, size)
            landed(piece, group_recv.at[stage_at, layer, s])

    def gather_two(layer):
        for d in range(1, 8):
            landed(three_in.at[layer, (depth + 8 - d) % 8], deep_recv.at[layer, d - 1])
        three_in[layer, depth] = two_sum[layer]
        total = three_in[layer, 0]
        for level in range(1, 8):
            total = total + three_in[layer, level]
        final[layer % 4, pl.ds(pl.multiple_of(offset_two, 8), 16), :] = total * scale
        for d in range(1, 4):
            piece = rows_at(final, layer % 4, offset_two, 16)
            push(
                piece,
                piece,
                group_send.at[2, layer, 3 - d],
                group_recv.at[2, layer, 3 - d],
                in_plane(False, (index_two + d) % 4),
            )

    def gather_one(layer):
        gathered(layer, 2, offset_one, index_two, 16)
        for d in range(1, 4):
            piece = rows_at(final, layer % 4, offset_one, 64)
            push(
                piece,
                piece,
                group_send.at[3, layer, 3 - d],
                group_recv.at[3, layer, 3 - d],
                in_plane(True, (index_one + d) % 4),
            )

    def gather_half(layer):
        gathered(layer, 3, offset_half, index_one, 64)
        piece = rows_at(final, layer % 4, offset_half, 256)
        push(piece, piece, pair_send.at[1, layer], pair_recv.at[1, layer], mate)

    def finish(layer):
        piece = rows_at(final, layer % 4, (1 - core) * 256, 256)
        landed(piece, pair_recv.at[1, layer])

    everywhere = [reduce_half, reduce_one, reduce_two]
    at_home = [gather_two, gather_one, gather_half, finish]

    def weigh(layer, slope, high_patch, low_patch):
        turned_slope = jnp.concatenate([slope[0:128, :].T, slope[128:256, :].T], axis=1)
        sides = jnp.concatenate(split_parts(turned_slope), axis=0)
        product = jnp.dot(sides, high_patch, preferred_element_type=F32) + jnp.dot(
            sides, low_patch, preferred_element_type=F32
        )
        sums = jnp.sum(slope, axis=0, keepdims=True)
        part[2 * layer, FRONT * TAP_ROWS : FRONT * TAP_ROWS + 1, :] = sums + turned(sums)
        for tap in range(TAPS):
            cols = slice(tap * 128, tap * 128 + 128)
            block = product[0:128, cols] + product[128:256, cols]
            at = 2 * layer + tap // FRONT
            base = tap % FRONT * TAP_ROWS
            flipped = turned(block[64:128, :])
            part[at, base : base + 64, :] = block[0:64, :] + jnp.where(left, flipped, 0.0)
            part[at, base + 64 : base + 96, :] = jnp.where(
                left, block[64:96, :], flipped[32:64, :]
            )
            if tap == FRONT - 1:
                reduce_start(2 * layer)
        reduce_start(2 * layer + 1)

    def backward(step, carry):
        pair = 1 - step
        first = 2 * pair
        slot = 2 + step
        slope = slope_of(flow[...], pre[pair])
        keep_own(slot, slope)
        send_rims(slot)
        weigh(first + 1, slope, *[taps_of(lines.at[pair], at, 128, 0, 2) for at in range(2)])

        @pl.when(pair == 0)
        def _():
            for half in range(2):
                reduce_half(4 + half)
                reduce_one(6 + half)

        await_rims(slot)

        @pl.when(pair == 1)
        def _():
            hand_on(0)

        @pl.when(pair == 0)
        def _():
            hand_over(0, out_act)
            for half in range(2):
                reduce_half(2 + half)
                reduce_one(4 + half)
                reduce_two(6 + half)

        fill_wide(slot, slope_lines, slope_rims)
        gradient = back_across(wide_taps(slope_lines, slope_rims), first + 1)
        slope = slope_of(gradient, wide_pre[pair])
        keep_inner(slope)
        weigh(
            first,
            slope[128:384, :],
            *[taps_of(wide_lines.at[pair], at, 128, 1, 2) for at in range(2)],
        )

        @pl.when(pair == 1)
        def _():
            for half in range(2):
                reduce_half(6 + half)

        @pl.when(pair == 0)
        def _():
            for half in range(2):
                reduce_one(2 + half)
                reduce_two(4 + half)

        fill_inner(slope_lines)
        gradient = back_across(inner_taps(slope_lines), first)
        flow[...] = gradient

        @pl.when(pair == 1)
        def _():
            settle(gradient, 1, 1, out_grad)

        @pl.when(pair == 0)
        def _():
            settle(gradient, 0, 1, out_grad)

        return carry

    lax.fori_loop(0, 2, backward, 0)

    hand_on(1)
    for round_at in range(7):
        for at in range(2 * LAYERS):
            tick = round_at + (2 if at in (2, 3) else 0)
            if at >= 4 and round_at < 3:
                continue
            if tick < 3:
                everywhere[tick](at)
            elif tick < 7:

                @pl.when(sec == at // 4)
                def _():
                    at_home[tick - 3](at)

        if round_at == 2:
            hand_over(1, out_grad)

    landed(out_act.at[1 - sec], out_recv.at[0])
    landed(out_grad.at[1 - sec], out_recv.at[1])

    def drain_rims(slot, carry):
        for d, (dy, dz) in enumerate(DIRS):
            rows, cells = source_window(dy, dz)

            @pl.when(exists(dy, dz))
            def _():
                landed(ext.at[slot, rows, cells, :], halo_send.at[slot, d])

        return carry

    lax.fori_loop(0, 4, drain_rims, 0)
    for i in range(2):
        for chunk in range(CHUNKS):

            @pl.when(at_end)
            def _():
                landed(chunk_of(2 * sec + i, core, chunk), source_send.at[i, chunk])

            @pl.when(at_end)
            def _():
                landed(chunk_of(2 * other + i, core, chunk), relay_send.at[i, chunk])

            landed(chunk_of(2 * other + i, core, chunk), mate_send.at[i, chunk])
    for kind in range(2):
        landed(stage.at[kind], out_send.at[kind])
        landed(midway.at[kind], mid_send.at[kind])

    def drain_sums(layer, carry):
        home = sec == layer // 4
        landed(half_in.at[layer], pair_send.at[0, layer])
        for s in range(3):
            landed(one_in.at[layer, s], group_send.at[0, layer, s])
            landed(two_in.at[layer, s], group_send.at[1, layer, s])
        for d in range(1, 8):

            @pl.when(((depth + d) % 8) // 4 == layer // 4)
            def _():
                landed(two_sum.at[layer], deep_send.at[layer, d - 1])

        @pl.when(home)
        def _():
            for s in range(3):
                landed(two_in.at[layer, s], group_send.at[2, layer, s])
                landed(one_in.at[layer, s], group_send.at[3, layer, s])
            landed(half_in.at[layer], pair_send.at[1, layer])

        return carry

    lax.fori_loop(0, 2 * LAYERS, drain_sums, 0)


def unpack(act, grad, total, out_act, out_grad, out_weight, out_bias, spread, sem):
    copies = [
        pltpu.make_async_copy(act, out_act, sem.at[0]),
        pltpu.make_async_copy(grad, out_grad, sem.at[1]),
    ]
    for copy in copies:
        copy.start()
    for i in range(2):
        for tap in range(TAPS):
            at = 2 * i + tap // FRONT
            base = tap % FRONT * TAP_ROWS
            top = total[at, base : base + 64, :]
            near = total[at, base + 64 : base + 96, :]
            spread[i, 9 + tap] = top[:, 0:64]
            spread[i, 18 + tap] = pltpu.roll(top, 64, 1)[:, 0:64]
            spread[i, tap, 0:32, :] = near[:, 0:64]
            spread[i, tap, 32:64, :] = pltpu.roll(near, 64, 1)[:, 0:64]
        copies.append(pltpu.make_async_copy(spread.at[i], out_weight.at[i], sem.at[2 + i]))
        copies[-1].start()
        row = FRONT * TAP_ROWS
        out_bias[i : i + 1, :] = total[2 * i, row : row + 1, 0:64]
    for copy in copies:
        copy.wait()


def per_device(inflow, weights, biases, cotangent):
    micro, channels, nx, ny, nz = inflow.shape
    cells = micro * nx * ny * lax.axis_size("gy") * nz * lax.axis_size("gz")
    scale = 1.0 / math.sqrt(cells)
    rows = channels * nx * ny
    vmem = pltpu.VMEM
    dma = pltpu.SemaphoreType.DMA
    scratch = [
        vmem((rows, nz), F32),
        vmem(weights.shape, F32),
        vmem((rows, nz), F32),
        vmem((4, 6, 160, 128), F32),
        vmem((4, 160, 128), F32),
        vmem((2, 2, 3, 768, 128), BF16),
        vmem((2, 2, 3, 96, 128), BF16),
        vmem((2, 2, 3, 512, 128), BF16),
        vmem((2, 3, 768, 128), BF16),
        vmem((2, 3, 96, 128), BF16),
        vmem((LAYERS, 256, TAPS * 128), BF16),
        vmem((LAYERS, TAPS * 128, 256), BF16),
        vmem((LAYERS, PACK, 128), F32),
        vmem((2, WIDE, 128), F32),
        vmem((2, 256, 128), F32),
        vmem((256, 128), F32),
        vmem((2, 256, 128), F32),
        vmem((2, 256, 128), F32),
        vmem((2 * LAYERS, GRAD, 128), F32),
        vmem((2 * LAYERS, 256, 128), F32),
        vmem((2 * LAYERS, 256, 128), F32),
        vmem((2 * LAYERS, 3, 64, 128), F32),
        vmem((2 * LAYERS, 64, 128), F32),
        vmem((2 * LAYERS, 3, 16, 128), F32),
        vmem((2 * LAYERS, 16, 128), F32),
        vmem((2 * LAYERS, 8, 16, 128), F32),
        dma((3,)),
        dma((4, 8)),
        dma((4, 8)),
        dma((2, CHUNKS)),
        dma((2, CHUNKS)),
        dma((2, CHUNKS)),
        dma((2, CHUNKS)),
        dma((2, CHUNKS)),
        dma((2,)),
        dma((2,)),
        dma((2,)),
        dma((2,)),
        dma((2, 2 * LAYERS)),
        dma((2, 2 * LAYERS)),
        dma((4, 2 * LAYERS, 3)),
        dma((4, 2 * LAYERS, 3)),
        dma((2 * LAYERS, 7)),
        dma((2 * LAYERS, 7)),
    ]
    near = pl.BlockSpec(memory_space=pltpu.VMEM)
    far = pl.BlockSpec(memory_space=pl.ANY)

    def body(*refs):
        kernel(scale, *refs)

    act, grad, total = pl.pallas_call(
        body,
        name="encoder_sections",
        out_shape=(
            vmem((micro, rows, nz), F32),
            vmem((micro, rows, nz), F32),
            vmem((4, GRAD, 128), F32),
        ),
        in_specs=[far, far, near, far],
        out_specs=(near,) * 3,
        scratch_shapes=scratch,
        compiler_params=pltpu.CompilerParams(
            collective_id=0, has_side_effects=True, vmem_limit_bytes=56 << 20
        ),
    )(
        inflow.reshape(micro, rows, nz),
        weights,
        biases,
        cotangent.reshape(micro, rows, nz),
    )
    act, grad, weight, bias = pl.pallas_call(
        unpack,
        name="write_results",
        out_shape=(
            jax.ShapeDtypeStruct(act.shape, F32),
            jax.ShapeDtypeStruct(grad.shape, F32),
            jax.ShapeDtypeStruct(weights.shape, F32),
            jax.ShapeDtypeStruct(biases.shape, F32),
        ),
        in_specs=[near] * 3,
        out_specs=(far, far, far, near),
        scratch_shapes=[vmem(weights.shape, F32), dma((4,))],
        compiler_params=pltpu.CompilerParams(vmem_limit_bytes=8 << 20),
    )(act, grad, total)
    shape = (1, micro, channels, nx, ny, nz)
    return act.reshape(shape), grad.reshape(shape), weight, bias


def solution(mesh):
    return jax.shard_map(
        per_device,
        mesh=mesh,
        in_specs=(
            P(None, None, None, "gy", "gz"),
            P("section", None, None, None),
            P("section", None),
            P(None, None, None, "gy", "gz"),
        ),
        out_specs=(
            P("section", None, None, None, "gy", "gz"),
            P("section", None, None, None, "gy", "gz"),
            P("section", None, None, None),
            P("section", None),
        ),
        check_vma=False,
    )
```

```python
import math

import jax
import jax.numpy as jnp
from jax import lax
from jax.experimental import pallas as pl
from jax.experimental.pallas import tpu as pltpu
from jax.sharding import PartitionSpec as P

MESH = pl.DeviceIdType.MESH
F32 = jnp.float32
BF16 = jnp.bfloat16
LAYERS = 4
TAPS = 9
DIRS = [(dy, dz) for dy in (-1, 0, 1) for dz in (-1, 0, 1) if (dy, dz) != (0, 0)]
TAP_ROWS = 96
PACK = 880
CHUNKS = 5
CHUNK = PACK // 2 // CHUNKS
EARLY = 3
GRAD = 512
FRONT = 5
WIDE = 576


def split_parts(value):
    high = value.astype(BF16)
    return high, (value - high.astype(F32)).astype(BF16)


def source_window(dy, dz):
    cells = {1: pl.ds(136, 8), -1: pl.ds(16, 8), 0: pl.ds(16, 128)}[dz]
    return pl.ds(2, 2), cells


def target_window(dy, dz):
    rows = {1: pl.ds(0, 2), -1: pl.ds(4, 2), 0: pl.ds(2, 2)}[dy]
    cells = {1: pl.ds(8, 8), -1: pl.ds(144, 8), 0: pl.ds(16, 128)}[dz]
    return rows, cells


def landed(ref, sem):
    pltpu.make_async_copy(ref, ref, sem).wait()


def kernel(
    scale,
    inflow_hbm,
    weights_hbm,
    biases,
    cotangent_hbm,
    out_act,
    out_grad,
    final,
    inflow,
    weights,
    cotangent,
    ext,
    inner,
    wide_lines,
    wide_rims,
    lines,
    slope_lines,
    slope_rims,
    wide_f,
    wide_b,
    packed,
    wide_pre,
    pre,
    flow,
    stage,
    midway,
    part,
    half_in,
    half_sum,
    one_in,
    one_sum,
    two_in,
    two_sum,
    three_in,
    load_sem,
    halo_send,
    halo_recv,
    source_send,
    relay_send,
    relay_recv,
    mate_send,
    mate_recv,
    out_send,
    out_recv,
    mid_send,
    mid_recv,
    pair_send,
    pair_recv,
    group_send,
    group_recv,
    deep_send,
    deep_recv,
):
    sec = lax.axis_index("section")
    gy = lax.axis_index("gy")
    gz = lax.axis_index("gz")
    core = gy % 2
    px = (gy // 2) % 4
    zlo = gy // 8
    depth = sec * 4 + zlo
    other = 1 - sec

    def at_depth(level, parity):
        return (level // 4, (level % 4) * 8 + px * 2 + parity, gz)

    def in_plane(first, index):
        on_x = (1 - core) if first else core
        new_gy = gy + on_x * 2 * (index - px)
        new_gz = gz + (1 - on_x) * (index - gz)
        return (sec, new_gy, new_gz)

    mate = (sec, gy + 1 - 2 * core, gz)
    first_plane = zlo == 0
    last_plane = zlo == 3
    at_end = jnp.logical_or(first_plane, last_plane)
    outward = at_depth((depth + jnp.where(last_plane, 1, 7)) % 8, core)
    inward = at_depth((depth + jnp.where(last_plane, 7, 1)) % 8, core)

    def exists(dy, dz):
        ok = None
        for index, delta, count in ((gy, dy, 32), (gz, dz, 4)):
            if delta == 0:
                continue
            good = index > 0 if delta < 0 else index < count - 1
            ok = good if ok is None else jnp.logical_and(ok, good)
        return ok

    lane = lax.broadcasted_iota(jnp.int32, (1, 128), 1)
    left = lane < 64

    def turned(value):
        return pltpu.roll(value, 64, 1)

    loads = [
        pltpu.make_async_copy(weights_hbm, weights, load_sem.at[0]),
        pltpu.make_async_copy(inflow_hbm.at[sec], inflow, load_sem.at[1]),
        pltpu.make_async_copy(cotangent_hbm.at[sec], cotangent, load_sem.at[2]),
    ]
    for load in loads:
        load.start()

    barrier = pltpu.get_barrier_semaphore()

    def greet(device):
        pl.semaphore_signal(barrier, inc=1, device_id=device, device_id_type=MESH)

    for d in range(1, 8):
        greet(at_depth((depth + d) % 8, core))
    for d in range(1, 4):
        greet((sec, gy + 2 * ((px + d) % 4 - px), gz))
        greet((sec, gy, (gz + d) % 4))
    for dy, dz in DIRS:
        if dy != 0:

            @pl.when(exists(dy, dz))
            def _():
                greet((sec, gy + dy, gz + dz))

    sides_y = 2 - jnp.where(gy == 0, 1, 0) - jnp.where(gy == 31, 1, 0)
    sides_z = 2 - jnp.where(gz == 0, 1, 0) - jnp.where(gz == 3, 1, 0)
    def clear(rows, cells):
        ext[:, rows, cells, :] = jnp.zeros((4, rows.size, cells.size, 128), F32)

    clear(pl.ds(0, 6), pl.ds(0, 8))
    clear(pl.ds(0, 6), pl.ds(152, 8))

    @pl.when(gy == 0)
    def _():
        clear(pl.ds(0, 2), pl.ds(8, 144))

    @pl.when(gy == 31)
    def _():
        clear(pl.ds(4, 2), pl.ds(8, 144))

    @pl.when(gz == 0)
    def _():
        clear(pl.ds(0, 6), pl.ds(8, 8))

    @pl.when(gz == 3)
    def _():
        clear(pl.ds(0, 6), pl.ds(144, 8))

    def turned_in(ref, y):
        rows = [ref[pl.ds(2 * x + y, 64, stride=4), :] for x in range(2)]
        return jnp.concatenate(rows, axis=0).T

    loads[1].wait()
    for y in range(2):
        ext[0, 2 + y, 16:144, :] = turned_in(inflow, y)
    loads[0].wait()
    for i in range(2):
        for b in range(3):
            for c in range(3):
                tap = b * 3 + c
                base = tap * TAP_ROWS
                middle = weights[i, 9 + tap]
                far = weights[i, 18 + tap]
                near = weights[i, tap]
                packed[2 * sec + i, base : base + 64, :] = jnp.concatenate([middle, far], axis=1)
                packed[2 * sec + i, base + 64 : base + 96, :] = jnp.concatenate(
                    [near[0:32], near[32:64]], axis=1
                )
        row = biases[i : i + 1, :]
        packed[2 * sec + i, 864:880, :] = jnp.broadcast_to(
            jnp.concatenate([row, row], axis=1), (16, 128)
        )

    pl.semaphore_wait(barrier, 13 + sides_y * (1 + sides_z))

    def send_rims(slot):
        for d, (dy, dz) in enumerate(DIRS):
            rows, cells = source_window(dy, dz)
            rows_to, cells_to = target_window(dy, dz)

            @pl.when(exists(dy, dz))
            def _():
                pltpu.make_async_remote_copy(
                    src_ref=ext.at[slot, rows, cells, :],
                    dst_ref=ext.at[slot, rows_to, cells_to, :],
                    send_sem=halo_send.at[slot, d],
                    recv_sem=halo_recv.at[slot, d],
                    device_id=(sec, gy + dy, gz + dz),
                    device_id_type=MESH,
                ).start()

    def await_rims(slot):
        for d, (dy, dz) in enumerate(DIRS):
            rows_to, cells_to = target_window(dy, dz)

            @pl.when(exists(-dy, -dz))
            def _():
                landed(ext.at[slot, rows_to, cells_to, :], halo_recv.at[slot, d])

    send_rims(0)

    def chunk_of(layer, parity, chunk):
        start = parity * (PACK // 2) + chunk * CHUNK
        return packed.at[layer, pl.ds(pl.multiple_of(start, 8), CHUNK), :]

    def pass_on(layer, i, chunk, send, recv, device):
        piece = chunk_of(layer, core, chunk)
        pltpu.make_async_remote_copy(
            src_ref=piece,
            dst_ref=piece,
            send_sem=send.at[i, chunk],
            recv_sem=recv.at[i, chunk],
            device_id=device,
            device_id_type=MESH,
        ).start()

    @pl.when(at_end)
    def _():
        for i in range(2):
            for chunk in range(CHUNKS):
                pass_on(2 * sec + i, i, chunk, source_send, relay_recv, outward)

    def widen(layer):
        for tap in range(TAPS):
            base = tap * TAP_ROWS
            top = packed[layer, base : base + 64, :]
            near = packed[layer, base + 64 : base + 96, :]
            bottom = jnp.where(
                left, jnp.concatenate([near, turned(near)], axis=0), turned(top)
            )
            high, low = split_parts(jnp.concatenate([top, bottom], axis=0))
            cols = slice(tap * 128, tap * 128 + 128)
            wide_f[layer, 0:128, cols] = high
            wide_f[layer, 128:256, cols] = low
            rows = slice((8 - tap) * 128, (8 - tap) * 128 + 128)
            wide_b[layer, rows, 0:128] = high
            wide_b[layer, rows, 128:256] = low

    def widen_own(i, carry):
        widen(2 * sec + i)
        return carry

    lax.fori_loop(0, 2, widen_own, 0)

    loads[2].wait()
    for y in range(2):
        flow[y * 128 : (y + 1) * 128, :] = turned_in(cotangent, y)
    for layer in range(LAYERS):
        for half, used in ((0, FRONT * TAP_ROWS), (1, (TAPS - FRONT) * TAP_ROWS)):
            part[2 * layer + half, used:GRAD, :] = jnp.zeros((GRAD - used, 128), F32)

    def relay(i, chunks):
        for chunk in chunks:
            landed(chunk_of(2 * other + i, core, chunk), relay_recv.at[i, chunk])

            @pl.when(at_end)
            def _():
                pass_on(2 * other + i, i, chunk, relay_send, relay_recv, inward)

            pass_on(2 * other + i, i, chunk, mate_send, mate_recv, mate)

    def receive(i):
        for chunk in range(CHUNKS):
            landed(chunk_of(2 * other + i, 1 - core, chunk), mate_recv.at[i, chunk])
        widen(2 * other + i)

    relay(0, range(CHUNKS))
    receive(0)
    relay(1, range(EARLY))

    def reach(condition):
        return lane < jnp.where(condition, 128, 0)

    inside_low, inside_high = reach(gz > 0), reach(gz < 3)
    inside_line = [reach(gy > 0), None, None, reach(gy < 31)]

    def fill_wide(slot, line_ref, edge_ref):
        for c in range(3):
            for row in range(6):
                line = ext[slot, row, 15 + c : 143 + c, :]
                edge = jnp.concatenate(
                    [ext[slot, row, 7 + c : 15 + c, :], ext[slot, row, 143 + c : 151 + c, :]],
                    axis=0,
                )
                for at, value in enumerate(split_parts(line)):
                    line_ref[at, c, row * 128 : row * 128 + 128, :] = value
                for at, value in enumerate(split_parts(edge)):
                    edge_ref[at, c, row * 16 : row * 16 + 16, :] = value

    def fill_inner(line_ref):
        for c in range(3):
            for row in range(4):
                line = inner[row, 15 + c : 143 + c, :]
                for at, value in enumerate(split_parts(line)):
                    line_ref[at, c, row * 128 : row * 128 + 128, :] = value

    def taps_of(ref, at, size, first, count):
        return jnp.concatenate(
            [
                ref[at, c, (first + b) * size : (first + b + count) * size, :]
                for b in range(3)
                for c in range(3)
            ],
            axis=1,
        )

    def wide_taps(line_ref, edge_ref):
        return [
            jnp.concatenate(
                [taps_of(line_ref, at, 128, 0, 4), taps_of(edge_ref, at, 16, 0, 4)], axis=0
            )
            for at in range(2)
        ]

    def inner_taps(line_ref):
        return [taps_of(line_ref, at, 128, 0, 2) for at in range(2)]

    def keep_inner(value):
        for y in range(4):
            line = value[y * 128 : (y + 1) * 128, :]
            low = value[512 + y * 16 : 520 + y * 16, :]
            high = value[520 + y * 16 : 528 + y * 16, :]
            low = jnp.where(inside_low, low, 0.0)
            high = jnp.where(inside_high, high, 0.0)
            if inside_line[y] is not None:
                line, low, high = (jnp.where(inside_line[y], v, 0.0) for v in (line, low, high))
            inner[y, 16:144, :] = line
            inner[y, 8:16, :] = low
            inner[y, 144:152, :] = high

    def settle(value, keeper, kind, result):
        def put(ref, lead):
            for y in range(2):
                block = value[y * 128 : (y + 1) * 128, :].T
                for x in range(2):
                    where = pl.ds(2 * x + y, 64, stride=4)
                    ref[lead, where, :] = block[x * 64 : (x + 1) * 64, :]

        @pl.when(sec == keeper)
        def _():
            put(result, sec)

        @pl.when(sec != keeper)
        def _():
            put(stage, kind)

    two_on = at_depth((depth + 2 + 4 * core) % 8, core)
    origin = ((depth + 6 - 4 * core) % 8) // 4

    def hand_on(kind):
        pltpu.make_async_remote_copy(
            src_ref=stage.at[kind],
            dst_ref=midway.at[kind],
            send_sem=out_send.at[kind],
            recv_sem=mid_recv.at[kind],
            device_id=two_on,
            device_id_type=MESH,
        ).start()

    def hand_over(kind, result):
        landed(midway.at[kind], mid_recv.at[kind])
        pltpu.make_async_remote_copy(
            src_ref=midway.at[kind],
            dst_ref=result.at[origin],
            send_sem=mid_send.at[kind],
            recv_sem=out_recv.at[kind],
            device_id=two_on,
            device_id_type=MESH,
        ).start()

    def joined(parts, columns, dims):
        high, low = parts
        both = lax.dot_general(high, columns(256), dims, preferred_element_type=F32)
        rest = lax.dot_general(low, columns(128), dims, preferred_element_type=F32)
        return both[:, 0:128] + (both[:, 128:256] + rest)

    def across(parts, layer):
        def columns(count):
            return wide_f[layer, 0:count, :]

        return joined(parts, columns, (((1,), (1,)), ((), ()))) + packed[layer, 864:865, :]

    def back_across(parts, layer):
        def columns(count):
            return wide_b[layer, :, 0:count]

        return joined(parts, columns, (((1,), (0,)), ((), ())))

    def active(value):
        return value * (1.0 / (1.0 + jnp.exp(-value)))

    def slope_of(gradient, value):
        sigma = 1.0 / (1.0 + jnp.exp(-value))
        return gradient * sigma * (1.0 + value * (1.0 - sigma))

    def keep_own(slot, value):
        for y in range(2):
            ext[slot, 2 + y, 16:144, :] = value[y * 128 : (y + 1) * 128, :]

    def forward(pair, carry):
        first = 2 * pair
        await_rims(pair)

        fill_wide(pair, wide_lines.at[pair], wide_rims.at[pair])
        value = across(wide_taps(wide_lines.at[pair], wide_rims.at[pair]), first)
        wide_pre[pair] = value
        keep_inner(active(value))

        @pl.when(pair == 0)
        def _():
            relay(1, range(EARLY, CHUNKS))
            receive(1)

        fill_inner(lines.at[pair])
        value = across(inner_taps(lines.at[pair]), first + 1)
        pre[pair] = value
        result = active(value)

        @pl.when(pair == 0)
        def _():
            keep_own(1, result)
            send_rims(1)
            settle(result, 0, 0, out_act)

        @pl.when(pair == 1)
        def _():
            settle(result, 1, 0, out_act)

        return carry

    lax.fori_loop(0, 2, forward, 0)

    index_one = px + core * (gz - px)
    index_two = gz + core * (px - gz)
    offset_half = core * 256
    offset_one = offset_half + index_one * 64
    offset_two = offset_one + index_two * 16

    def rows_at(ref, layer, start, size):
        return ref.at[layer, pl.ds(pl.multiple_of(start, 8), size), :]

    def push(source, target, send, recv, device):
        pltpu.make_async_remote_copy(
            src_ref=source,
            dst_ref=target,
            send_sem=send,
            recv_sem=recv,
            device_id=device,
            device_id_type=MESH,
        ).start()

    def reduce_start(layer):
        push(
            rows_at(part, layer, (1 - core) * 256, 256),
            half_in.at[layer],
            pair_send.at[0, layer],
            pair_recv.at[0, layer],
            mate,
        )

    def reduce_half(layer):
        landed(half_in.at[layer], pair_recv.at[0, layer])
        half_sum[layer] = (
            part[layer, pl.ds(pl.multiple_of(offset_half, 8), 256), :] + half_in[layer]
        )
        for d in range(1, 4):
            peer = (index_one + d) % 4
            push(
                rows_at(half_sum, layer, peer * 64, 64),
                one_in.at[layer, 3 - d],
                group_send.at[0, layer, 3 - d],
                group_recv.at[0, layer, 3 - d],
                in_plane(True, peer),
            )

    def reduce_one(layer):
        for s in range(3):
            landed(one_in.at[layer, s], group_recv.at[0, layer, s])
        own = half_sum[layer, pl.ds(pl.multiple_of(index_one * 64, 8), 64), :]
        one_sum[layer] = (own + one_in[layer, 0]) + (one_in[layer, 1] + one_in[layer, 2])
        for d in range(1, 4):
            peer = (index_two + d) % 4
            push(
                rows_at(one_sum, layer, peer * 16, 16),
                two_in.at[layer, 3 - d],
                group_send.at[1, layer, 3 - d],
                group_recv.at[1, layer, 3 - d],
                in_plane(False, peer),
            )

    def reduce_two(layer):
        for s in range(3):
            landed(two_in.at[layer, s], group_recv.at[1, layer, s])
        own = one_sum[layer, pl.ds(pl.multiple_of(index_two * 16, 8), 16), :]
        two_sum[layer] = (own + two_in[layer, 0]) + (two_in[layer, 1] + two_in[layer, 2])
        for d in range(1, 8):
            peer = (depth + d) % 8

            @pl.when(peer // 4 == layer // 4)
            def _():
                push(
                    two_sum.at[layer],
                    three_in.at[layer, depth],
                    deep_send.at[layer, d - 1],
                    deep_recv.at[layer, d - 1],
                    at_depth(peer, core),
                )

    def gathered(layer, stage_at, base, index, size):
        for s in range(3):
            sender = (index + 1 + s) % 4
            piece = rows_at(final, layer % 4, base + sender * size, size)
            landed(piece, group_recv.at[stage_at, layer, s])

    def gather_two(layer):
        for d in range(1, 8):
            landed(three_in.at[layer, (depth + 8 - d) % 8], deep_recv.at[layer, d - 1])
        three_in[layer, depth] = two_sum[layer]
        total = three_in[layer, 0]
        for level in range(1, 8):
            total = total + three_in[layer, level]
        final[layer % 4, pl.ds(pl.multiple_of(offset_two, 8), 16), :] = total * scale
        for d in range(1, 4):
            piece = rows_at(final, layer % 4, offset_two, 16)
            push(
                piece,
                piece,
                group_send.at[2, layer, 3 - d],
                group_recv.at[2, layer, 3 - d],
                in_plane(False, (index_two + d) % 4),
            )

    def gather_one(layer):
        gathered(layer, 2, offset_one, index_two, 16)
        for d in range(1, 4):
            piece = rows_at(final, layer % 4, offset_one, 64)
            push(
                piece,
                piece,
                group_send.at[3, layer, 3 - d],
                group_recv.at[3, layer, 3 - d],
                in_plane(True, (index_one + d) % 4),
            )

    def gather_half(layer):
        gathered(layer, 3, offset_half, index_one, 64)
        piece = rows_at(final, layer % 4, offset_half, 256)
        push(piece, piece, pair_send.at[1, layer], pair_recv.at[1, layer], mate)

    def finish(layer):
        piece = rows_at(final, layer % 4, (1 - core) * 256, 256)
        landed(piece, pair_recv.at[1, layer])

    everywhere = [reduce_half, reduce_one, reduce_two]
    at_home = [gather_two, gather_one, gather_half, finish]

    def weigh(layer, slope, high_patch, low_patch):
        turned_slope = jnp.concatenate([slope[0:128, :].T, slope[128:256, :].T], axis=1)
        sides = jnp.concatenate(split_parts(turned_slope), axis=0)
        product = jnp.dot(sides, high_patch, preferred_element_type=F32) + jnp.dot(
            sides, low_patch, preferred_element_type=F32
        )
        sums = jnp.sum(slope, axis=0, keepdims=True)
        part[2 * layer, FRONT * TAP_ROWS : FRONT * TAP_ROWS + 1, :] = sums + turned(sums)
        for tap in range(TAPS):
            cols = slice(tap * 128, tap * 128 + 128)
            block = product[0:128, cols] + product[128:256, cols]
            at = 2 * layer + tap // FRONT
            base = tap % FRONT * TAP_ROWS
            flipped = turned(block[64:128, :])
            part[at, base : base + 64, :] = block[0:64, :] + jnp.where(left, flipped, 0.0)
            part[at, base + 64 : base + 96, :] = jnp.where(
                left, block[64:96, :], flipped[32:64, :]
            )

    def both(stage_of, layer):
        stage_of(2 * layer)
        stage_of(2 * layer + 1)

    def backward(step, carry):
        pair = 1 - step
        first = 2 * pair
        slot = 2 + step
        slope = slope_of(flow[...], pre[pair])
        keep_own(slot, slope)
        send_rims(slot)
        weigh(first + 1, slope, *[taps_of(lines.at[pair], at, 128, 0, 2) for at in range(2)])
        reduce_start(2 * first + 2)
        reduce_start(2 * first + 3)
        await_rims(slot)

        @pl.when(pair == 1)
        def _():
            hand_on(0)
            both(reduce_half, 3)

        @pl.when(pair == 0)
        def _():
            hand_over(0, out_act)
            both(reduce_start, 2)
            both(reduce_one, 3)
            both(reduce_half, 1)

        fill_wide(slot, slope_lines, slope_rims)
        gradient = back_across(wide_taps(slope_lines, slope_rims), first + 1)
        slope = slope_of(gradient, wide_pre[pair])
        keep_inner(slope)
        weigh(
            first,
            slope[128:384, :],
            *[taps_of(wide_lines.at[pair], at, 128, 1, 2) for at in range(2)],
        )

        @pl.when(pair == 0)
        def _():
            both(reduce_start, 0)
            both(reduce_two, 3)
            both(reduce_one, 1)
            both(reduce_half, 2)

        fill_inner(slope_lines)
        gradient = back_across(inner_taps(slope_lines), first)
        flow[...] = gradient

        @pl.when(pair == 1)
        def _():
            settle(gradient, 1, 1, out_grad)

        @pl.when(pair == 0)
        def _():
            settle(gradient, 0, 1, out_grad)

        return carry

    lax.fori_loop(0, 2, backward, 0)

    hand_on(1)
    ahead = {0: 0, 1: 2, 2: 1, 3: 3}
    for round_at in range(7):
        for layer in range(LAYERS):
            tick = round_at + ahead[layer]
            if layer >= 2 and tick >= 3:
                tick = round_at if round_at >= 3 else 7
            if tick < 3:
                both(everywhere[tick], layer)
            elif tick < 7:

                @pl.when(sec == layer // 2)
                def _():
                    both(at_home[tick - 3], layer)

        if round_at == 2:
            hand_over(1, out_grad)

    landed(out_act.at[1 - sec], out_recv.at[0])
    landed(out_grad.at[1 - sec], out_recv.at[1])

    def drain_rims(slot, carry):
        for d, (dy, dz) in enumerate(DIRS):
            rows, cells = source_window(dy, dz)

            @pl.when(exists(dy, dz))
            def _():
                landed(ext.at[slot, rows, cells, :], halo_send.at[slot, d])

        return carry

    lax.fori_loop(0, 4, drain_rims, 0)
    for i in range(2):
        for chunk in range(CHUNKS):

            @pl.when(at_end)
            def _():
                landed(chunk_of(2 * sec + i, core, chunk), source_send.at[i, chunk])

            @pl.when(at_end)
            def _():
                landed(chunk_of(2 * other + i, core, chunk), relay_send.at[i, chunk])

            landed(chunk_of(2 * other + i, core, chunk), mate_send.at[i, chunk])
    for kind in range(2):
        landed(stage.at[kind], out_send.at[kind])
        landed(midway.at[kind], mid_send.at[kind])

    def drain_sums(layer, carry):
        home = sec == layer // 4
        landed(half_in.at[layer], pair_send.at[0, layer])
        for s in range(3):
            landed(one_in.at[layer, s], group_send.at[0, layer, s])
            landed(two_in.at[layer, s], group_send.at[1, layer, s])
        for d in range(1, 8):

            @pl.when(((depth + d) % 8) // 4 == layer // 4)
            def _():
                landed(two_sum.at[layer], deep_send.at[layer, d - 1])

        @pl.when(home)
        def _():
            for s in range(3):
                landed(two_in.at[layer, s], group_send.at[2, layer, s])
                landed(one_in.at[layer, s], group_send.at[3, layer, s])
            landed(half_in.at[layer], pair_send.at[1, layer])

        return carry

    lax.fori_loop(0, 2 * LAYERS, drain_sums, 0)


def unpack(act, grad, total, out_act, out_grad, out_weight, out_bias, spread, sem):
    copies = [
        pltpu.make_async_copy(act, out_act, sem.at[0]),
        pltpu.make_async_copy(grad, out_grad, sem.at[1]),
    ]
    for copy in copies:
        copy.start()
    for i in range(2):
        for tap in range(TAPS):
            at = 2 * i + tap // FRONT
            base = tap % FRONT * TAP_ROWS
            top = total[at, base : base + 64, :]
            near = total[at, base + 64 : base + 96, :]
            spread[i, 9 + tap] = top[:, 0:64]
            spread[i, 18 + tap] = pltpu.roll(top, 64, 1)[:, 0:64]
            spread[i, tap, 0:32, :] = near[:, 0:64]
            spread[i, tap, 32:64, :] = pltpu.roll(near, 64, 1)[:, 0:64]
        copies.append(pltpu.make_async_copy(spread.at[i], out_weight.at[i], sem.at[2 + i]))
        copies[-1].start()
        row = FRONT * TAP_ROWS
        out_bias[i : i + 1, :] = total[2 * i, row : row + 1, 0:64]
    for copy in copies:
        copy.wait()


def per_device(inflow, weights, biases, cotangent):
    micro, channels, nx, ny, nz = inflow.shape
    cells = micro * nx * ny * lax.axis_size("gy") * nz * lax.axis_size("gz")
    scale = 1.0 / math.sqrt(cells)
    rows = channels * nx * ny
    vmem = pltpu.VMEM
    dma = pltpu.SemaphoreType.DMA
    scratch = [
        vmem((rows, nz), F32),
        vmem(weights.shape, F32),
        vmem((rows, nz), F32),
        vmem((4, 6, 160, 128), F32),
        vmem((4, 160, 128), F32),
        vmem((2, 2, 3, 768, 128), BF16),
        vmem((2, 2, 3, 96, 128), BF16),
        vmem((2, 2, 3, 512, 128), BF16),
        vmem((2, 3, 768, 128), BF16),
        vmem((2, 3, 96, 128), BF16),
        vmem((LAYERS, 256, TAPS * 128), BF16),
        vmem((LAYERS, TAPS * 128, 256), BF16),
        vmem((LAYERS, PACK, 128), F32),
        vmem((2, WIDE, 128), F32),
        vmem((2, 256, 128), F32),
        vmem((256, 128), F32),
        vmem((2, 256, 128), F32),
        vmem((2, 256, 128), F32),
        vmem((2 * LAYERS, GRAD, 128), F32),
        vmem((2 * LAYERS, 256, 128), F32),
        vmem((2 * LAYERS, 256, 128), F32),
        vmem((2 * LAYERS, 3, 64, 128), F32),
        vmem((2 * LAYERS, 64, 128), F32),
        vmem((2 * LAYERS, 3, 16, 128), F32),
        vmem((2 * LAYERS, 16, 128), F32),
        vmem((2 * LAYERS, 8, 16, 128), F32),
        dma((3,)),
        dma((4, 8)),
        dma((4, 8)),
        dma((2, CHUNKS)),
        dma((2, CHUNKS)),
        dma((2, CHUNKS)),
        dma((2, CHUNKS)),
        dma((2, CHUNKS)),
        dma((2,)),
        dma((2,)),
        dma((2,)),
        dma((2,)),
        dma((2, 2 * LAYERS)),
        dma((2, 2 * LAYERS)),
        dma((4, 2 * LAYERS, 3)),
        dma((4, 2 * LAYERS, 3)),
        dma((2 * LAYERS, 7)),
        dma((2 * LAYERS, 7)),
    ]
    near = pl.BlockSpec(memory_space=pltpu.VMEM)
    far = pl.BlockSpec(memory_space=pl.ANY)

    def body(*refs):
        kernel(scale, *refs)

    act, grad, total = pl.pallas_call(
        body,
        name="encoder_sections",
        out_shape=(
            vmem((micro, rows, nz), F32),
            vmem((micro, rows, nz), F32),
            vmem((4, GRAD, 128), F32),
        ),
        in_specs=[far, far, near, far],
        out_specs=(near,) * 3,
        scratch_shapes=scratch,
        compiler_params=pltpu.CompilerParams(
            collective_id=0, has_side_effects=True, vmem_limit_bytes=56 << 20
        ),
    )(
        inflow.reshape(micro, rows, nz),
        weights,
        biases,
        cotangent.reshape(micro, rows, nz),
    )
    act, grad, weight, bias = pl.pallas_call(
        unpack,
        name="write_results",
        out_shape=(
            jax.ShapeDtypeStruct(act.shape, F32),
            jax.ShapeDtypeStruct(grad.shape, F32),
            jax.ShapeDtypeStruct(weights.shape, F32),
            jax.ShapeDtypeStruct(biases.shape, F32),
        ),
        in_specs=[near] * 3,
        out_specs=(far, far, far, near),
        scratch_shapes=[vmem(weights.shape, F32), dma((4,))],
        compiler_params=pltpu.CompilerParams(vmem_limit_bytes=8 << 20),
    )(act, grad, total)
    shape = (1, micro, channels, nx, ny, nz)
    return act.reshape(shape), grad.reshape(shape), weight, bias


def solution(mesh):
    return jax.shard_map(
        per_device,
        mesh=mesh,
        in_specs=(
            P(None, None, None, "gy", "gz"),
            P("section", None, None, None),
            P("section", None),
            P(None, None, None, "gy", "gz"),
        ),
        out_specs=(
            P("section", None, None, None, "gy", "gz"),
            P("section", None, None, None, "gy", "gz"),
            P("section", None, None, None),
            P("section", None),
        ),
        check_vma=False,
    )
```

```python
import math

import jax
import jax.numpy as jnp
from jax import lax
from jax.experimental import pallas as pl
from jax.experimental.pallas import tpu as pltpu
from jax.sharding import PartitionSpec as P

MESH = pl.DeviceIdType.MESH
F32 = jnp.float32
BF16 = jnp.bfloat16
LAYERS = 4
TAPS = 9
DIRS = [(dy, dz) for dy in (-1, 0, 1) for dz in (-1, 0, 1) if (dy, dz) != (0, 0)]
TAP_ROWS = 96
PACK = 880
CHUNKS = 11
CHUNK = PACK // 2 // CHUNKS
EARLY = 6
GRAD = 1024
WIDE = 576


def split_parts(value):
    high = value.astype(BF16)
    return high, (value - high.astype(F32)).astype(BF16)


def source_window(dy, dz):
    cells = {1: pl.ds(136, 8), -1: pl.ds(16, 8), 0: pl.ds(16, 128)}[dz]
    return pl.ds(2, 2), cells


def target_window(dy, dz):
    rows = {1: pl.ds(0, 2), -1: pl.ds(4, 2), 0: pl.ds(2, 2)}[dy]
    cells = {1: pl.ds(8, 8), -1: pl.ds(144, 8), 0: pl.ds(16, 128)}[dz]
    return rows, cells


def landed(ref, sem):
    pltpu.make_async_copy(ref, ref, sem).wait()


def kernel(
    scale,
    inflow_hbm,
    weights_hbm,
    biases,
    cotangent_hbm,
    out_act,
    out_grad,
    final,
    inflow,
    weights,
    cotangent,
    ext,
    inner,
    wide_lines,
    wide_rims,
    lines,
    slope_lines,
    slope_rims,
    wide_f,
    wide_b,
    packed,
    wide_pre,
    pre,
    flow,
    stage,
    midway,
    part,
    half_in,
    half_sum,
    one_in,
    one_sum,
    two_in,
    two_sum,
    three_in,
    load_sem,
    halo_send,
    halo_recv,
    source_send,
    relay_send,
    relay_recv,
    mate_send,
    mate_recv,
    out_send,
    out_recv,
    mid_send,
    mid_recv,
    pair_send,
    pair_recv,
    group_send,
    group_recv,
    deep_send,
    deep_recv,
):
    sec = lax.axis_index("section")
    gy = lax.axis_index("gy")
    gz = lax.axis_index("gz")
    core = gy % 2
    px = (gy // 2) % 4
    zlo = gy // 8
    depth = sec * 4 + zlo
    other = 1 - sec

    def at_depth(level, parity):
        return (level // 4, (level % 4) * 8 + px * 2 + parity, gz)

    def in_plane(first, index):
        on_x = (1 - core) if first else core
        new_gy = gy + on_x * 2 * (index - px)
        new_gz = gz + (1 - on_x) * (index - gz)
        return (sec, new_gy, new_gz)

    mate = (sec, gy + 1 - 2 * core, gz)
    first_plane = zlo == 0
    last_plane = zlo == 3
    at_end = jnp.logical_or(first_plane, last_plane)
    outward = at_depth((depth + jnp.where(last_plane, 1, 7)) % 8, core)
    inward = at_depth((depth + jnp.where(last_plane, 7, 1)) % 8, core)

    def exists(dy, dz):
        ok = None
        for index, delta, count in ((gy, dy, 32), (gz, dz, 4)):
            if delta == 0:
                continue
            good = index > 0 if delta < 0 else index < count - 1
            ok = good if ok is None else jnp.logical_and(ok, good)
        return ok

    lane = lax.broadcasted_iota(jnp.int32, (1, 128), 1)
    left = lane < 64

    def turned(value):
        return pltpu.roll(value, 64, 1)

    loads = [
        pltpu.make_async_copy(weights_hbm, weights, load_sem.at[0]),
        pltpu.make_async_copy(inflow_hbm.at[sec], inflow, load_sem.at[1]),
        pltpu.make_async_copy(cotangent_hbm.at[sec], cotangent, load_sem.at[2]),
    ]
    for load in loads:
        load.start()

    barrier = pltpu.get_barrier_semaphore()

    def greet(device):
        pl.semaphore_signal(barrier, inc=1, device_id=device, device_id_type=MESH)

    for d in range(1, 8):
        greet(at_depth((depth + d) % 8, core))
    for d in range(1, 4):
        greet((sec, gy + 2 * ((px + d) % 4 - px), gz))
        greet((sec, gy, (gz + d) % 4))
    for dy, dz in DIRS:
        if dy != 0:

            @pl.when(exists(dy, dz))
            def _():
                greet((sec, gy + dy, gz + dz))

    sides_y = 2 - jnp.where(gy == 0, 1, 0) - jnp.where(gy == 31, 1, 0)
    sides_z = 2 - jnp.where(gz == 0, 1, 0) - jnp.where(gz == 3, 1, 0)
    def clear(rows, cells):
        ext[:, rows, cells, :] = jnp.zeros((4, rows.size, cells.size, 128), F32)

    clear(pl.ds(0, 6), pl.ds(0, 8))
    clear(pl.ds(0, 6), pl.ds(152, 8))

    @pl.when(gy == 0)
    def _():
        clear(pl.ds(0, 2), pl.ds(8, 144))

    @pl.when(gy == 31)
    def _():
        clear(pl.ds(4, 2), pl.ds(8, 144))

    @pl.when(gz == 0)
    def _():
        clear(pl.ds(0, 6), pl.ds(8, 8))

    @pl.when(gz == 3)
    def _():
        clear(pl.ds(0, 6), pl.ds(144, 8))

    def turned_in(ref, y):
        rows = [ref[pl.ds(2 * x + y, 64, stride=4), :] for x in range(2)]
        return jnp.concatenate(rows, axis=0).T

    loads[1].wait()
    for y in range(2):
        ext[0, 2 + y, 16:144, :] = turned_in(inflow, y)
    loads[0].wait()
    for i in range(2):
        for b in range(3):
            for c in range(3):
                tap = b * 3 + c
                base = tap * TAP_ROWS
                middle = weights[i, 9 + tap]
                far = weights[i, 18 + tap]
                near = weights[i, tap]
                packed[2 * sec + i, base : base + 64, :] = jnp.concatenate([middle, far], axis=1)
                packed[2 * sec + i, base + 64 : base + 96, :] = jnp.concatenate(
                    [near[0:32], near[32:64]], axis=1
                )
        row = biases[i : i + 1, :]
        packed[2 * sec + i, 864:880, :] = jnp.broadcast_to(
            jnp.concatenate([row, row], axis=1), (16, 128)
        )

    pl.semaphore_wait(barrier, 13 + sides_y * (1 + sides_z))

    def send_rims(slot):
        for d, (dy, dz) in enumerate(DIRS):
            rows, cells = source_window(dy, dz)
            rows_to, cells_to = target_window(dy, dz)

            @pl.when(exists(dy, dz))
            def _():
                pltpu.make_async_remote_copy(
                    src_ref=ext.at[slot, rows, cells, :],
                    dst_ref=ext.at[slot, rows_to, cells_to, :],
                    send_sem=halo_send.at[slot, d],
                    recv_sem=halo_recv.at[slot, d],
                    device_id=(sec, gy + dy, gz + dz),
                    device_id_type=MESH,
                ).start()

    def await_rims(slot):
        for d, (dy, dz) in enumerate(DIRS):
            rows_to, cells_to = target_window(dy, dz)

            @pl.when(exists(-dy, -dz))
            def _():
                landed(ext.at[slot, rows_to, cells_to, :], halo_recv.at[slot, d])

    send_rims(0)

    def chunk_of(layer, parity, chunk):
        start = parity * (PACK // 2) + chunk * CHUNK
        return packed.at[layer, pl.ds(pl.multiple_of(start, 8), CHUNK), :]

    def pass_on(layer, i, chunk, send, recv, device):
        piece = chunk_of(layer, core, chunk)
        pltpu.make_async_remote_copy(
            src_ref=piece,
            dst_ref=piece,
            send_sem=send.at[i, chunk],
            recv_sem=recv.at[i, chunk],
            device_id=device,
            device_id_type=MESH,
        ).start()

    @pl.when(at_end)
    def _():
        for i in range(2):
            for chunk in range(CHUNKS):
                pass_on(2 * sec + i, i, chunk, source_send, relay_recv, outward)

    def widen(layer):
        for tap in range(TAPS):
            base = tap * TAP_ROWS
            top = packed[layer, base : base + 64, :]
            near = packed[layer, base + 64 : base + 96, :]
            bottom = jnp.where(
                left, jnp.concatenate([near, turned(near)], axis=0), turned(top)
            )
            high, low = split_parts(jnp.concatenate([top, bottom], axis=0))
            cols = slice(tap * 128, tap * 128 + 128)
            wide_f[layer, 0:128, cols] = high
            wide_f[layer, 128:256, cols] = low
            rows = slice((8 - tap) * 128, (8 - tap) * 128 + 128)
            wide_b[layer, rows, 0:128] = high
            wide_b[layer, rows, 128:256] = low

    def widen_own(i, carry):
        widen(2 * sec + i)
        return carry

    lax.fori_loop(0, 2, widen_own, 0)

    loads[2].wait()
    for y in range(2):
        flow[y * 128 : (y + 1) * 128, :] = turned_in(cotangent, y)
    for layer in range(LAYERS):
        part[layer, 864:GRAD, :] = jnp.zeros((GRAD - 864, 128), F32)

    def relay(i, chunks):
        for chunk in chunks:
            landed(chunk_of(2 * other + i, core, chunk), relay_recv.at[i, chunk])

            @pl.when(at_end)
            def _():
                pass_on(2 * other + i, i, chunk, relay_send, relay_recv, inward)

            pass_on(2 * other + i, i, chunk, mate_send, mate_recv, mate)

    def receive(i):
        for chunk in range(CHUNKS):
            landed(chunk_of(2 * other + i, 1 - core, chunk), mate_recv.at[i, chunk])
        widen(2 * other + i)

    relay(0, range(CHUNKS))
    receive(0)
    relay(1, range(EARLY))

    def reach(condition):
        return lane < jnp.where(condition, 128, 0)

    inside_low, inside_high = reach(gz > 0), reach(gz < 3)
    inside_line = [reach(gy > 0), None, None, reach(gy < 31)]

    def fill_wide(slot, line_ref, edge_ref):
        for c in range(3):
            for row in range(6):
                line = ext[slot, row, 15 + c : 143 + c, :]
                edge = jnp.concatenate(
                    [ext[slot, row, 7 + c : 15 + c, :], ext[slot, row, 143 + c : 151 + c, :]],
                    axis=0,
                )
                for at, value in enumerate(split_parts(line)):
                    line_ref[at, c, row * 128 : row * 128 + 128, :] = value
                for at, value in enumerate(split_parts(edge)):
                    edge_ref[at, c, row * 16 : row * 16 + 16, :] = value

    def fill_inner(line_ref):
        for c in range(3):
            for row in range(4):
                line = inner[row, 15 + c : 143 + c, :]
                for at, value in enumerate(split_parts(line)):
                    line_ref[at, c, row * 128 : row * 128 + 128, :] = value

    def taps_of(ref, at, size, first, count):
        return jnp.concatenate(
            [
                ref[at, c, (first + b) * size : (first + b + count) * size, :]
                for b in range(3)
                for c in range(3)
            ],
            axis=1,
        )

    def wide_taps(line_ref, edge_ref):
        return [
            jnp.concatenate(
                [taps_of(line_ref, at, 128, 0, 4), taps_of(edge_ref, at, 16, 0, 4)], axis=0
            )
            for at in range(2)
        ]

    def inner_taps(line_ref):
        return [taps_of(line_ref, at, 128, 0, 2) for at in range(2)]

    def keep_inner(value):
        for y in range(4):
            line = value[y * 128 : (y + 1) * 128, :]
            low = value[512 + y * 16 : 520 + y * 16, :]
            high = value[520 + y * 16 : 528 + y * 16, :]
            low = jnp.where(inside_low, low, 0.0)
            high = jnp.where(inside_high, high, 0.0)
            if inside_line[y] is not None:
                line, low, high = (jnp.where(inside_line[y], v, 0.0) for v in (line, low, high))
            inner[y, 16:144, :] = line
            inner[y, 8:16, :] = low
            inner[y, 144:152, :] = high

    def settle(value, keeper, kind, result):
        def put(ref, lead):
            for y in range(2):
                block = value[y * 128 : (y + 1) * 128, :].T
                for x in range(2):
                    where = pl.ds(2 * x + y, 64, stride=4)
                    ref[lead, where, :] = block[x * 64 : (x + 1) * 64, :]

        @pl.when(sec == keeper)
        def _():
            put(result, sec)

        @pl.when(sec != keeper)
        def _():
            put(stage, kind)

    two_on = at_depth((depth + 2 + 4 * core) % 8, core)
    origin = ((depth + 6 - 4 * core) % 8) // 4

    def hand_on(kind):
        pltpu.make_async_remote_copy(
            src_ref=stage.at[kind],
            dst_ref=midway.at[kind],
            send_sem=out_send.at[kind],
            recv_sem=mid_recv.at[kind],
            device_id=two_on,
            device_id_type=MESH,
        ).start()

    def hand_over(kind, result):
        landed(midway.at[kind], mid_recv.at[kind])
        pltpu.make_async_remote_copy(
            src_ref=midway.at[kind],
            dst_ref=result.at[origin],
            send_sem=mid_send.at[kind],
            recv_sem=out_recv.at[kind],
            device_id=two_on,
            device_id_type=MESH,
        ).start()

    def joined(parts, columns, dims):
        high, low = parts
        both = lax.dot_general(high, columns(256), dims, preferred_element_type=F32)
        rest = lax.dot_general(low, columns(128), dims, preferred_element_type=F32)
        return both[:, 0:128] + (both[:, 128:256] + rest)

    def across(parts, layer):
        def columns(count):
            return wide_f[layer, 0:count, :]

        return joined(parts, columns, (((1,), (1,)), ((), ()))) + packed[layer, 864:865, :]

    def back_across(parts, layer):
        def columns(count):
            return wide_b[layer, :, 0:count]

        return joined(parts, columns, (((1,), (0,)), ((), ())))

    def active(value):
        return value * (1.0 / (1.0 + jnp.exp(-value)))

    def slope_of(gradient, value):
        sigma = 1.0 / (1.0 + jnp.exp(-value))
        return gradient * sigma * (1.0 + value * (1.0 - sigma))

    def keep_own(slot, value):
        for y in range(2):
            ext[slot, 2 + y, 16:144, :] = value[y * 128 : (y + 1) * 128, :]

    def forward(pair, carry):
        first = 2 * pair
        await_rims(pair)

        fill_wide(pair, wide_lines.at[pair], wide_rims.at[pair])
        value = across(wide_taps(wide_lines.at[pair], wide_rims.at[pair]), first)
        wide_pre[pair] = value
        keep_inner(active(value))

        @pl.when(pair == 0)
        def _():
            relay(1, range(EARLY, CHUNKS))
            receive(1)

        fill_inner(lines.at[pair])
        value = across(inner_taps(lines.at[pair]), first + 1)
        pre[pair] = value
        result = active(value)

        @pl.when(pair == 0)
        def _():
            keep_own(1, result)
            send_rims(1)
            settle(result, 0, 0, out_act)

        @pl.when(pair == 1)
        def _():
            settle(result, 1, 0, out_act)

        return carry

    lax.fori_loop(0, 2, forward, 0)

    index_one = px + core * (gz - px)
    index_two = gz + core * (px - gz)
    offset_half = core * 512
    offset_one = offset_half + index_one * 128
    offset_two = offset_one + index_two * 32

    def rows_at(ref, layer, start, size):
        return ref.at[layer, pl.ds(pl.multiple_of(start, 8), size), :]

    def push(source, target, send, recv, device):
        pltpu.make_async_remote_copy(
            src_ref=source,
            dst_ref=target,
            send_sem=send,
            recv_sem=recv,
            device_id=device,
            device_id_type=MESH,
        ).start()

    def reduce_start(layer):
        push(
            rows_at(part, layer, (1 - core) * 512, 512),
            half_in.at[layer],
            pair_send.at[0, layer],
            pair_recv.at[0, layer],
            mate,
        )

    def reduce_half(layer):
        landed(half_in.at[layer], pair_recv.at[0, layer])
        half_sum[layer] = (
            part[layer, pl.ds(pl.multiple_of(offset_half, 8), 512), :] + half_in[layer]
        )
        for d in range(1, 4):
            peer = (index_one + d) % 4
            push(
                rows_at(half_sum, layer, peer * 128, 128),
                one_in.at[layer, 3 - d],
                group_send.at[0, layer, 3 - d],
                group_recv.at[0, layer, 3 - d],
                in_plane(True, peer),
            )

    def reduce_one(layer):
        for s in range(3):
            landed(one_in.at[layer, s], group_recv.at[0, layer, s])
        own = half_sum[layer, pl.ds(pl.multiple_of(index_one * 128, 8), 128), :]
        one_sum[layer] = (own + one_in[layer, 0]) + (one_in[layer, 1] + one_in[layer, 2])
        for d in range(1, 4):
            peer = (index_two + d) % 4
            push(
                rows_at(one_sum, layer, peer * 32, 32),
                two_in.at[layer, 3 - d],
                group_send.at[1, layer, 3 - d],
                group_recv.at[1, layer, 3 - d],
                in_plane(False, peer),
            )

    def reduce_two(layer):
        for s in range(3):
            landed(two_in.at[layer, s], group_recv.at[1, layer, s])
        own = one_sum[layer, pl.ds(pl.multiple_of(index_two * 32, 8), 32), :]
        two_sum[layer] = (own + two_in[layer, 0]) + (two_in[layer, 1] + two_in[layer, 2])
        for d in range(1, 8):
            peer = (depth + d) % 8

            @pl.when(peer // 4 == layer // 2)
            def _():
                push(
                    two_sum.at[layer],
                    three_in.at[layer, depth],
                    deep_send.at[layer, d - 1],
                    deep_recv.at[layer, d - 1],
                    at_depth(peer, core),
                )

    def gathered(layer, stage_at, base, index, size):
        for s in range(3):
            sender = (index + 1 + s) % 4
            piece = rows_at(final, layer % 2, base + sender * size, size)
            landed(piece, group_recv.at[stage_at, layer, s])

    def gather_two(layer):
        for d in range(1, 8):
            landed(three_in.at[layer, (depth + 8 - d) % 8], deep_recv.at[layer, d - 1])
        three_in[layer, depth] = two_sum[layer]
        total = three_in[layer, 0]
        for level in range(1, 8):
            total = total + three_in[layer, level]
        final[layer % 2, pl.ds(pl.multiple_of(offset_two, 8), 32), :] = total * scale
        for d in range(1, 4):
            piece = rows_at(final, layer % 2, offset_two, 32)
            push(
                piece,
                piece,
                group_send.at[2, layer, 3 - d],
                group_recv.at[2, layer, 3 - d],
                in_plane(False, (index_two + d) % 4),
            )

    def gather_one(layer):
        gathered(layer, 2, offset_one, index_two, 32)
        for d in range(1, 4):
            piece = rows_at(final, layer % 2, offset_one, 128)
            push(
                piece,
                piece,
                group_send.at[3, layer, 3 - d],
                group_recv.at[3, layer, 3 - d],
                in_plane(True, (index_one + d) % 4),
            )

    def gather_half(layer):
        gathered(layer, 3, offset_half, index_one, 128)
        piece = rows_at(final, layer % 2, offset_half, 512)
        push(piece, piece, pair_send.at[1, layer], pair_recv.at[1, layer], mate)

    def finish(layer):
        piece = rows_at(final, layer % 2, (1 - core) * 512, 512)
        landed(piece, pair_recv.at[1, layer])

    everywhere = [reduce_half, reduce_one, reduce_two]
    at_home = [gather_two, gather_one, gather_half, finish]

    def weigh(layer, slope, high_patch, low_patch):
        turned_slope = jnp.concatenate([slope[0:128, :].T, slope[128:256, :].T], axis=1)
        sides = jnp.concatenate(split_parts(turned_slope), axis=0)
        product = jnp.dot(sides, high_patch, preferred_element_type=F32) + jnp.dot(
            sides, low_patch, preferred_element_type=F32
        )
        for tap in range(TAPS):
            cols = slice(tap * 128, tap * 128 + 128)
            block = product[0:128, cols] + product[128:256, cols]
            base = tap * TAP_ROWS
            flipped = turned(block[64:128, :])
            part[layer, base : base + 64, :] = block[0:64, :] + jnp.where(left, flipped, 0.0)
            part[layer, base + 64 : base + 96, :] = jnp.where(
                left, block[64:96, :], flipped[32:64, :]
            )
        sums = jnp.sum(slope, axis=0, keepdims=True)
        part[layer, 864:865, :] = sums + turned(sums)
        reduce_start(layer)

    def backward(step, carry):
        pair = 1 - step
        first = 2 * pair
        slot = 2 + step
        slope = slope_of(flow[...], pre[pair])
        keep_own(slot, slope)
        send_rims(slot)
        weigh(first + 1, slope, *[taps_of(lines.at[pair], at, 128, 0, 2) for at in range(2)])

        @pl.when(pair == 0)
        def _():
            reduce_half(2)
            reduce_one(3)

        await_rims(slot)

        @pl.when(pair == 1)
        def _():
            hand_on(0)

        @pl.when(pair == 0)
        def _():
            hand_over(0, out_act)
            reduce_half(1)
            reduce_one(2)
            reduce_two(3)

        fill_wide(slot, slope_lines, slope_rims)
        gradient = back_across(wide_taps(slope_lines, slope_rims), first + 1)
        slope = slope_of(gradient, wide_pre[pair])
        keep_inner(slope)
        weigh(
            first,
            slope[128:384, :],
            *[taps_of(wide_lines.at[pair], at, 128, 1, 2) for at in range(2)],
        )

        @pl.when(pair == 1)
        def _():
            reduce_half(3)

        @pl.when(pair == 0)
        def _():
            reduce_one(1)
            reduce_two(2)

        fill_inner(slope_lines)
        gradient = back_across(inner_taps(slope_lines), first)
        flow[...] = gradient

        @pl.when(pair == 1)
        def _():
            settle(gradient, 1, 1, out_grad)

        @pl.when(pair == 0)
        def _():
            settle(gradient, 0, 1, out_grad)

        return carry

    lax.fori_loop(0, 2, backward, 0)

    hand_on(1)
    for round_at in range(7):
        for layer, tick, ready in ((0, round_at, 0), (1, round_at + 2, 0), (2, round_at, 3), (3, round_at, 3)):
            if round_at < ready:
                continue
            if tick < 3:
                everywhere[tick](layer)
            elif tick < 7:

                @pl.when(sec == layer // 2)
                def _():
                    at_home[tick - 3](layer)

        if round_at == 2:
            hand_over(1, out_grad)

    landed(out_act.at[1 - sec], out_recv.at[0])
    landed(out_grad.at[1 - sec], out_recv.at[1])

    def drain_rims(slot, carry):
        for d, (dy, dz) in enumerate(DIRS):
            rows, cells = source_window(dy, dz)

            @pl.when(exists(dy, dz))
            def _():
                landed(ext.at[slot, rows, cells, :], halo_send.at[slot, d])

        return carry

    lax.fori_loop(0, 4, drain_rims, 0)
    for i in range(2):
        for chunk in range(CHUNKS):

            @pl.when(at_end)
            def _():
                landed(chunk_of(2 * sec + i, core, chunk), source_send.at[i, chunk])

            @pl.when(at_end)
            def _():
                landed(chunk_of(2 * other + i, core, chunk), relay_send.at[i, chunk])

            landed(chunk_of(2 * other + i, core, chunk), mate_send.at[i, chunk])
    for kind in range(2):
        landed(stage.at[kind], out_send.at[kind])
        landed(midway.at[kind], mid_send.at[kind])

    def drain_sums(layer, carry):
        home = sec == layer // 2
        landed(half_in.at[layer], pair_send.at[0, layer])
        for s in range(3):
            landed(one_in.at[layer, s], group_send.at[0, layer, s])
            landed(two_in.at[layer, s], group_send.at[1, layer, s])
        for d in range(1, 8):

            @pl.when(((depth + d) % 8) // 4 == layer // 2)
            def _():
                landed(two_sum.at[layer], deep_send.at[layer, d - 1])

        @pl.when(home)
        def _():
            for s in range(3):
                landed(two_in.at[layer, s], group_send.at[2, layer, s])
                landed(one_in.at[layer, s], group_send.at[3, layer, s])
            landed(half_in.at[layer], pair_send.at[1, layer])

        return carry

    lax.fori_loop(0, LAYERS, drain_sums, 0)


def unpack(act, grad, total, out_act, out_grad, out_weight, out_bias, spread, sem):
    copies = [
        pltpu.make_async_copy(act, out_act, sem.at[0]),
        pltpu.make_async_copy(grad, out_grad, sem.at[1]),
    ]
    for copy in copies:
        copy.start()
    for i in range(2):
        for tap in range(TAPS):
            base = tap * TAP_ROWS
            top = total[i, base : base + 64, :]
            near = total[i, base + 64 : base + 96, :]
            spread[i, 9 + tap] = top[:, 0:64]
            spread[i, 18 + tap] = pltpu.roll(top, 64, 1)[:, 0:64]
            spread[i, tap, 0:32, :] = near[:, 0:64]
            spread[i, tap, 32:64, :] = pltpu.roll(near, 64, 1)[:, 0:64]
        copies.append(pltpu.make_async_copy(spread.at[i], out_weight.at[i], sem.at[2 + i]))
        copies[-1].start()
    out_bias[...] = total[:, 864, 0:64]
    for copy in copies:
        copy.wait()


def per_device(inflow, weights, biases, cotangent):
    micro, channels, nx, ny, nz = inflow.shape
    cells = micro * nx * ny * lax.axis_size("gy") * nz * lax.axis_size("gz")
    scale = 1.0 / math.sqrt(cells)
    rows = channels * nx * ny
    vmem = pltpu.VMEM
    dma = pltpu.SemaphoreType.DMA
    scratch = [
        vmem((rows, nz), F32),
        vmem(weights.shape, F32),
        vmem((rows, nz), F32),
        vmem((4, 6, 160, 128), F32),
        vmem((4, 160, 128), F32),
        vmem((2, 2, 3, 768, 128), BF16),
        vmem((2, 2, 3, 96, 128), BF16),
        vmem((2, 2, 3, 512, 128), BF16),
        vmem((2, 3, 768, 128), BF16),
        vmem((2, 3, 96, 128), BF16),
        vmem((LAYERS, 256, TAPS * 128), BF16),
        vmem((LAYERS, TAPS * 128, 256), BF16),
        vmem((LAYERS, PACK, 128), F32),
        vmem((2, WIDE, 128), F32),
        vmem((2, 256, 128), F32),
        vmem((256, 128), F32),
        vmem((2, 256, 128), F32),
        vmem((2, 256, 128), F32),
        vmem((LAYERS, GRAD, 128), F32),
        vmem((LAYERS, 512, 128), F32),
        vmem((LAYERS, 512, 128), F32),
        vmem((LAYERS, 3, 128, 128), F32),
        vmem((LAYERS, 128, 128), F32),
        vmem((LAYERS, 3, 32, 128), F32),
        vmem((LAYERS, 32, 128), F32),
        vmem((LAYERS, 8, 32, 128), F32),
        dma((3,)),
        dma((4, 8)),
        dma((4, 8)),
        dma((2, CHUNKS)),
        dma((2, CHUNKS)),
        dma((2, CHUNKS)),
        dma((2, CHUNKS)),
        dma((2, CHUNKS)),
        dma((2,)),
        dma((2,)),
        dma((2,)),
        dma((2,)),
        dma((2, LAYERS)),
        dma((2, LAYERS)),
        dma((4, LAYERS, 3)),
        dma((4, LAYERS, 3)),
        dma((LAYERS, 7)),
        dma((LAYERS, 7)),
    ]
    near = pl.BlockSpec(memory_space=pltpu.VMEM)
    far = pl.BlockSpec(memory_space=pl.ANY)

    def body(*refs):
        kernel(scale, *refs)

    act, grad, total = pl.pallas_call(
        body,
        name="encoder_sections",
        out_shape=(
            vmem((micro, rows, nz), F32),
            vmem((micro, rows, nz), F32),
            vmem((2, GRAD, 128), F32),
        ),
        in_specs=[far, far, near, far],
        out_specs=(near,) * 3,
        scratch_shapes=scratch,
        compiler_params=pltpu.CompilerParams(
            collective_id=0, has_side_effects=True, vmem_limit_bytes=56 << 20
        ),
    )(
        inflow.reshape(micro, rows, nz),
        weights,
        biases,
        cotangent.reshape(micro, rows, nz),
    )
    act, grad, weight, bias = pl.pallas_call(
        unpack,
        name="write_results",
        out_shape=(
            jax.ShapeDtypeStruct(act.shape, F32),
            jax.ShapeDtypeStruct(grad.shape, F32),
            jax.ShapeDtypeStruct(weights.shape, F32),
            jax.ShapeDtypeStruct(biases.shape, F32),
        ),
        in_specs=[near] * 3,
        out_specs=(far, far, far, near),
        scratch_shapes=[vmem(weights.shape, F32), dma((4,))],
        compiler_params=pltpu.CompilerParams(vmem_limit_bytes=8 << 20),
    )(act, grad, total)
    shape = (1, micro, channels, nx, ny, nz)
    return act.reshape(shape), grad.reshape(shape), weight, bias


def solution(mesh):
    return jax.shard_map(
        per_device,
        mesh=mesh,
        in_specs=(
            P(None, None, None, "gy", "gz"),
            P("section", None, None, None),
            P("section", None),
            P(None, None, None, "gy", "gz"),
        ),
        out_specs=(
            P("section", None, None, None, "gy", "gz"),
            P("section", None, None, None, "gy", "gz"),
            P("section", None, None, None),
            P("section", None),
        ),
        check_vma=False,
    )
```
